256 devices in a mesh: crop: 2 (over y_hi), rows: 16 (over y_lo, x, core), hid: 8 (over z).
Axes of the slice: x: 4, y: 4 (y_hi: 2, y_lo: 2; y = y_hi * 2 + y_lo), z: 8, core: 2. Of those that a mesh axis runs over, the one named last changes fastest.
Arguments:
- tokens: bfloat16 [2, 32, 64, 4096], P('crop', 'rows', None, 'hid'), may hold values from -6 to 6
- cotangent: bfloat16 [2, 32, 64, 4096], P('crop', 'rows', None, 'hid'), may hold values from -6 to 6
- weight_in: bfloat16 [256, 64, 5, 256], P('rows', 'hid'), may hold values from -0.15625 to 0.15625
- weight_out: bfloat16 [256, 64, 5, 256], P('rows', 'hid'), may hold values from -0.078125 to 0.078125
- mix_kernel: float32 [9, 16384], P(None, 'hid'), may hold values from -4 to 4
- block_rows: int32 [64, 5], P('hid'), may hold values from 0 to 15, as said below
Outputs:
- grad_tokens: bfloat16 [2, 32, 64, 4096], P('crop', 'rows', None, 'hid')
- grad_w_in: float32 [256, 64, 5, 256], P(('crop', 'rows'), 'hid')
- grad_w_out: float32 [256, 64, 5, 256], P(('crop', 'rows'), 'hid')
- grad_kernel: float32 [9, 16384], P(None, 'hid')
The draws below stay inside these ranges and needn't reach their ends.
Inputs may be any that keep to these rules, and one draw needn't show every extreme that they name: In each block column c, block_rows[c, 0] is a label L and block_rows[c, k] for k >= 1 is L with bit k - 1 flipped, so the 5 entries of a column differ; every value is the label of equally many block columns.
All inputs are finite; a program needn't handle non-finite values.
Results may differ from the reference program's by a relative error of at most 0.019.
Values may be sent and summed in bfloat16 or wider, within the bound.
No kernel may reach another device: no remote copies, remote signals or barrier semaphores. Data moves between devices by JAX's collectives and lax.ppermute only.
A program may use at most 128 MiB of HBM per device.

```python
import jax
import jax.numpy as jnp
from jax import lax

D = 4096
F = 16384
BS = 256
NNZ = 5
PW = 64
CROPS = 2
GH = 32
FB = 64
N_ROWS = 16


def draw_block_rows(key, part):
    block_count = D // BS
    perm_key, flip_key = jax.random.split(jax.random.fold_in(key, 7))
    labels = jax.random.permutation(perm_key, jnp.arange(F // BS, dtype=jnp.int32)) % block_count
    flip_bits = jax.random.randint(flip_key, (), 0, block_count).astype(jnp.int32)
    labels = jnp.bitwise_xor(labels, flip_bits)
    shifts = jnp.left_shift(jnp.ones((NNZ - 1,), jnp.int32), jnp.arange(NNZ - 1, dtype=jnp.int32))
    masks = jnp.concatenate([jnp.zeros((1,), jnp.int32), shifts])
    return jnp.bitwise_xor(labels[:, None], masks[None, :]).astype(jnp.int32)


def steps_of(own_key, dims, shards, low, largest):
    gain, own = 1.0, jax.random.fold_in(own_key, 6)
    for axis_at, shards_of in shards:
        steps = jnp.exp(jax.random.uniform(jax.random.fold_in(own, axis_at), (shards_of,), jnp.float32, low / len(shards), largest / len(shards)))
        gain = gain * jnp.repeat(steps, dims[axis_at] // shards_of).reshape([-1 if axis == axis_at else 1 for axis in range(len(dims))])
    return gain


def noise(own_key, shape, width, bound, cuts=(), held_as=jnp.bfloat16):
    entries = width * jax.random.normal(own_key, shape, jnp.float32)
    if cuts:
        entries = entries * steps_of(own_key, shape, cuts, -0.22, 0.18)
    return jnp.clip(entries, -bound, bound).astype(held_as)


def setup_inputs(seed: int = 0) -> dict:
    splits = jax.random.split(jax.random.key(seed), 7)
    tokens = noise(splits[0], (CROPS, GH, PW, D), 1.0, 6.0, ((0, 2), (1, 16), (3, 8)))
    cotangent = noise(splits[1], (CROPS, GH, PW, D), 1.0, 6.0, ((0, 2), (1, 16), (3, 8)))
    weight_in = noise(splits[2], (BS, FB, NNZ, BS), (NNZ * BS) ** -0.5, 0.15625, ((0, 16), (1, 8)))
    weight_out = noise(splits[3], (BS, FB, NNZ, BS), (FB * NNZ * BS * BS // D) ** -0.5, 0.078125, ((0, 16), (1, 8)))
    mix_kernel = noise(splits[4], (9, F), 0.35, 4.0, ((1, 8),), jnp.float32)
    block_rows = draw_block_rows(jax.random.fold_in(splits[6], 71), 0)
    return dict(tokens=tokens, cotangent=cotangent, weight_in=weight_in, weight_out=weight_out, mix_kernel=mix_kernel, block_rows=block_rows)


root_two_pi = 0.7978845608
cubic_coef = 0.044715
loss_scale = 0.03125


def gelu_pair(preact):
    inner = root_two_pi * (preact + cubic_coef * preact * preact * preact)
    tanh_val = jnp.tanh(inner)
    gelu_out = 0.5 * preact * (1.0 + tanh_val)
    slopes = 0.5 * (1.0 + tanh_val) + 0.5 * preact * (1.0 - tanh_val * tanh_val) * root_two_pi * (1.0 + 3.0 * cubic_coef * preact * preact)
    return gelu_out, slopes


def reference(tokens, cotangent, weight_in, weight_out, mix_kernel, block_rows):
    crop_count, height, grid_width, depth_all = tokens.shape
    block_count = depth_all // BS
    tok_count = crop_count * height * grid_width
    groups = crop_count * N_ROWS
    in_blocks = tokens.reshape(tok_count, block_count, BS)
    cot_blocks = cotangent.reshape(tok_count, block_count, BS)
    in_cols = jnp.moveaxis(weight_in, 1, 0)
    out_cols = jnp.moveaxis(weight_out, 1, 0)
    kern_cols = jnp.transpose(mix_kernel.reshape(9, FB, BS), (1, 0, 2))

    def column(dx_carry, slices):
        in_panel, out_panel, kern_local, row_ids = slices
        in_select = jnp.take(in_blocks, row_ids, axis=1).astype(jnp.float32)
        grad_select = jnp.take(cot_blocks, row_ids, axis=1).astype(jnp.float32)
        pre_act = jnp.einsum('nkb,bke->ne', in_select, in_panel.astype(jnp.float32))
        gelu_out, slopes = gelu_pair(pre_act)
        active = gelu_out.astype(jnp.bfloat16).astype(jnp.float32).reshape(crop_count, height, grid_width, BS)
        padded = jnp.pad(active, ((0, 0), (1, 1), (1, 1), (0, 0)))
        mix_sum = jnp.zeros((crop_count, height, grid_width, BS), jnp.float32)
        for row_off in range(3):
            for col_off in range(3):
                mix_sum = mix_sum + kern_local[3 * row_off + col_off] * padded[:, row_off:row_off + height, col_off:col_off + grid_width]
        mix_out = mix_sum.astype(jnp.bfloat16).astype(jnp.float32).reshape(tok_count, BS)
        mix_grad = jnp.einsum('nkd,fkd->nf', grad_select, out_panel.astype(jnp.float32)).astype(jnp.bfloat16).astype(jnp.float32)
        grad_grid = mix_grad.reshape(crop_count, height, grid_width, BS)
        grad_pad = jnp.pad(grad_grid, ((0, 0), (1, 1), (1, 1), (0, 0)))
        act_grad = jnp.zeros((crop_count, height, grid_width, BS), jnp.float32)
        kern_terms = []
        for row_off in range(3):
            for col_off in range(3):
                act_grad = act_grad + kern_local[3 * row_off + col_off] * grad_pad[:, 2 - row_off:2 - row_off + height, 2 - col_off:2 - col_off + grid_width]
                kern_terms.append(jnp.sum(padded[:, row_off:row_off + height, col_off:col_off + grid_width] * grad_grid, axis=(0, 1, 2)))
        kern_sum = jnp.stack(kern_terms, axis=0) * loss_scale
        pre_grad = (act_grad.reshape(tok_count, BS) * slopes).astype(jnp.bfloat16).astype(jnp.float32)
        mix_groups = mix_out.reshape(groups, tok_count // groups, BS)
        cot_groups = grad_select.reshape(groups, tok_count // groups, NNZ, BS)
        out_parts = (jnp.einsum('gtf,gtkd->gfkd', mix_groups, cot_groups) * loss_scale).astype(jnp.bfloat16).astype(jnp.float32)
        in_groups = in_select.reshape(groups, tok_count // groups, NNZ, BS)
        pre_groups = pre_grad.reshape(groups, tok_count // groups, BS)
        in_parts = (jnp.einsum('gtkb,gte->gbke', in_groups, pre_groups) * loss_scale).astype(jnp.bfloat16).astype(jnp.float32)
        back_select = jnp.einsum('ne,bke->nkb', pre_grad, in_panel.astype(jnp.float32))
        dx_carry = dx_carry.at[:, row_ids].add(back_select)
        return dx_carry, (jnp.sum(in_parts, axis=0), jnp.sum(out_parts, axis=0), kern_sum)

    dx_start = jnp.zeros((tok_count, block_count, BS), jnp.float32)
    dx_total, (in_grads, out_grads, kern_grads) = lax.scan(column, dx_start, (in_cols, out_cols, kern_cols, block_rows))
    grad_tokens = dx_total.reshape(crop_count, height, grid_width, depth_all).astype(jnp.bfloat16)
    grad_w_in = jnp.moveaxis(in_grads, 0, 1)
    grad_w_out = jnp.moveaxis(out_grads, 0, 1)
    grad_kernel = jnp.transpose(kern_grads, (1, 0, 2)).reshape(9, FB * BS)
    return grad_tokens, grad_w_in, grad_w_out, grad_kernel
```

```python
import functools

import jax
import jax.numpy as jnp
from jax import lax
from jax.experimental import pallas as pl
from jax.experimental.pallas import tpu as pltpu
from jax.sharding import PartitionSpec as P

root_two_pi = 0.7978845608
cubic_coef = 0.044715
loss_scale = 0.03125

F32, BF16 = jnp.float32, jnp.bfloat16
NX, NY, NC = 4, 4, 2
COLS, NNZ, BS, PW = 4, 5, 256, 64
TOK = 256
CORE, XPOS, YPOS, YLO = 20, 21, 22, 23
ANY = pl.BlockSpec(memory_space=pl.ANY)


def row_perm(move):
    pairs = []
    for y in range(2):
        for x in range(NX):
            for c in range(NC):
                y2, x2, c2 = move(y, x, c)
                pairs.append(((y * NX + x) * NC + c, (y2 * NX + x2 % NX) * NC + c2))
    return pairs


def along_x(value, step):
    return lax.ppermute(value, "rows", row_perm(lambda y, x, c: (y, x + step, c)))


def to_partner(value):
    return lax.ppermute(value, "rows", row_perm(lambda y, x, c: (y, x, 1 - c)))


def along_y(value, step):
    pairs = [(y * 8 + r, (y + step) % NY * 8 + r) for y in range(NY) for r in range(8)]
    return lax.ppermute(value, ("crop", "rows"), pairs)


def to_next_chip(value, step):
    pairs = []
    for q in range(8):
        if 0 <= q + step < 8:
            pairs += [(q * 2 + c, (q + step) * 2 + c) for c in range(NC)]
    return lax.ppermute(value, "rows", pairs)


def dot(a, b, dims):
    return lax.dot_general(a, b, (dims, ((), ())), preferred_element_type=F32)


def params():
    return pltpu.CompilerParams(dimension_semantics=("arbitrary",), vmem_limit_bytes=48 * 2**20)


def start_tokens(meta, own, other, which, buf, sem):
    core = meta[CORE]
    for src, at in ((own, core), (other, 1 - core)):
        rows = pl.ds(pl.multiple_of(at * 128, 128), 128)
        for half in range(2):
            pltpu.make_async_copy(
                src.at[:, which, :, pl.ds(half * BS, BS)], buf.at[:, half, rows], sem
            ).start()


def wait_all(buf, sem):
    pltpu.make_async_copy(buf, buf, sem).wait()


def start_weights(meta, pieces, which, buf, sems):
    x, ylo = meta[XPOS], meta[YLO]
    own, xm, xp, x2, yo, ym, yp, y2a, y2b = pieces
    here, there = ylo * NX, (1 - ylo) * NX
    at = lambda base, d: base + (x + d) % NX
    plan = []
    for s in range(2):
        plan += [
            (own, s, at(here, 0), s),
            (xm, s, at(here, 3), s),
            (xp, s, at(here, 1), s),
            (x2, s, at(here, 2), s),
            (yo, s, at(there, 0), s),
            (ym, s, at(there, 3), s),
            (yp, s, at(there, 1), s),
        ]
    plan += [(y2a, 0, at(there, 2), 0), (y2b, 0, at(there, 2), 1)]
    for c in range(COLS):
        for src, row, j, s in plan:
            pltpu.make_async_copy(src.at[row, which, c], buf.at[c, :, 2 * j + s], sems.at[c]).start()


def token_block(buf, row):
    return buf[row // 2, row % 2]


def forward_kernel(which, meta, own, other, *refs):
    pieces, refs = refs[:9], refs[9:]
    if which == 0:
        pre_ref, act_ref, top_ref, bot_ref, tok, wts, tok_sem, w_sems = refs
    else:
        act_ref, top_ref, bot_ref, tok, wts, tok_sem, w_sems = refs
    c = pl.program_id(0)

    @pl.when(c == 0)
    def _():
        start_tokens(meta, own, other, which, tok, tok_sem)
        start_weights(meta, pieces, which, wts, w_sems)
        wait_all(tok, tok_sem)

    wait_all(wts.at[c], w_sems.at[c])
    dims = ((1,), (0,)) if which == 0 else ((1,), (1,))
    total = jnp.zeros((TOK, BS), F32)
    for k in range(NNZ):
        total += dot(token_block(tok, meta[c * NNZ + k]), wts[c, k].reshape(BS, BS), dims)
    if which == 0:
        pre_ref[...] = total
        inner = root_two_pi * (total + cubic_coef * total * total * total)
        total = 0.5 * total * (1.0 + jnp.tanh(inner))
    out = total.astype(BF16)
    act_ref[...] = out
    top_ref[...] = out[:PW]
    bot_ref[...] = out[TOK - PW :]


def column(rows):
    return pl.BlockSpec((rows, BS), lambda c, m: (0, c))


def forward(which, meta, own, other, pieces):
    outs = [(TOK, BF16), (PW, BF16), (PW, BF16)]
    if which == 0:
        outs = [(TOK, F32)] + outs
    return pl.pallas_call(
        functools.partial(forward_kernel, which),
        out_shape=[jax.ShapeDtypeStruct((r, COLS * BS), t) for r, t in outs],
        grid_spec=pltpu.PrefetchScalarGridSpec(
            num_scalar_prefetch=1,
            grid=(COLS,),
            in_specs=[ANY] * 11,
            out_specs=[column(r) for r, _ in outs],
            scratch_shapes=[
                pltpu.VMEM((8, 2, TOK, BS), BF16),
                pltpu.VMEM((COLS, NNZ, 16, 16, BS), BF16),
                pltpu.SemaphoreType.DMA,
                pltpu.SemaphoreType.DMA((COLS,)),
            ],
        ),
        compiler_params=params(),
        cost_estimate=pl.CostEstimate(
            flops=2 * TOK * BS * BS * NNZ * COLS, transcendentals=TOK * BS * COLS, bytes_accessed=7 * 2**20
        ),
        name=("preact", "mixgrad")[which],
    )(meta, own, other, *pieces)


def shifted_rows(mid, up, down):
    cells = lax.broadcasted_iota(jnp.int32, (PW, BS), 0)
    out = []
    for row in [up[...]] + [mid[i * PW : (i + 1) * PW] for i in range(4)] + [down[...]]:
        row = row.astype(F32)
        left = jnp.where(cells == 0, 0.0, pltpu.roll(row, 1, 0))
        right = jnp.where(cells == PW - 1, 0.0, pltpu.roll(row, PW - 1, 0))
        out.append((left, row, right))
    return out


def grad_out_kernel(meta, own, other, act, up, down, mgrad, taps, *refs):
    outs, (cot, mixed, res, sem) = refs[:NX], refs[NX:]
    c = pl.program_id(0)
    x = meta[XPOS]

    @pl.when(c == 0)
    def _():
        start_tokens(meta, own, other, 1, cot, sem)

    rows = shifted_rows(act, up, down)
    for i in range(4):
        total = jnp.zeros((PW, BS), F32)
        for a in range(3):
            for b in range(3):
                total += taps[3 * a + b : 3 * a + b + 1] * rows[i + a][b]
        mixed[i * PW : (i + 1) * PW] = total.astype(BF16)
    sums = []
    for a in range(3):
        for b in range(3):
            total = jnp.zeros((PW, BS), F32)
            for i in range(4):
                total += rows[i + a][b] * mgrad[i * PW : (i + 1) * PW].astype(F32)
            sums.append(jnp.sum(total, axis=0, keepdims=True))
    slab = jnp.concatenate(sums + [jnp.zeros((7, BS), F32)], axis=0) * loss_scale
    for d in range(NX):
        outs[d][0, 20] = slab.astype(BF16)

    @pl.when(c == 0)
    def _():
        wait_all(cot, sem)

    mix = mixed[...]
    for k in range(NNZ):
        part = dot(mix, token_block(cot, meta[c * NNZ + k]), ((0,), (0,))) * loss_scale
        res[k] = part.astype(BF16).reshape(16, 16, BS)
        for d in range(NX):
            for y in range(NY):
                outs[d][0, k * NY + y] = res[k, y * NX + (x + d) % NX]


def slabs(count):
    return pl.BlockSpec((1, count, 16, BS), lambda c, m: (c, 0, 0, 0))


def taps_spec():
    return pl.BlockSpec((9, BS), lambda c, m: (0, m[CORE] * COLS + c))


def grad_out(meta, own, other, act, up, down, mgrad, taps):
    return pl.pallas_call(
        grad_out_kernel,
        out_shape=[jax.ShapeDtypeStruct((COLS, 21, 16, BS), BF16)] * NX,
        grid_spec=pltpu.PrefetchScalarGridSpec(
            num_scalar_prefetch=1,
            grid=(COLS,),
            in_specs=[ANY, ANY, column(TOK), column(PW), column(PW), column(TOK), taps_spec()],
            out_specs=[slabs(21)] * NX,
            scratch_shapes=[
                pltpu.VMEM((8, 2, TOK, BS), BF16),
                pltpu.VMEM((TOK, BS), BF16),
                pltpu.VMEM((NNZ, 16, 16, BS), BF16),
                pltpu.SemaphoreType.DMA,
            ],
        ),
        compiler_params=params(),
        cost_estimate=pl.CostEstimate(
            flops=2 * TOK * BS * BS * NNZ * COLS, transcendentals=0, bytes_accessed=7 * 2**20
        ),
        name="gradout",
    )(meta, own, other, act, up, down, mgrad, taps)


def grad_in_kernel(meta, own, other, *refs):
    pieces, refs = refs[:9], refs[9:]
    pre, mgrad, up, down, taps = refs[:5]
    outs, (keep, send, tok, wts, pgrad, res, acc, sem, w_sems) = refs[5 : 5 + NY], refs[5 + NY :]
    c = pl.program_id(0)
    core, y_here = meta[CORE], meta[YPOS]

    @pl.when(c == 0)
    def _():
        start_tokens(meta, own, other, 0, tok, sem)
        start_weights(meta, pieces, 0, wts, w_sems)
        acc[...] = jnp.zeros_like(acc)

    rows = shifted_rows(mgrad, up, down)
    for i in range(4):
        part = pl.ds(i * PW, PW)
        total = jnp.zeros((PW, BS), F32)
        for a in range(3):
            for b in range(3):
                total += taps[3 * a + b : 3 * a + b + 1] * rows[i + 2 - a][2 - b]
        p = pre[part]
        t = jnp.tanh(root_two_pi * (p + cubic_coef * p * p * p))
        slope = 0.5 * (1.0 + t) + 0.5 * p * (1.0 - t * t) * root_two_pi * (1.0 + 3.0 * cubic_coef * p * p)
        pgrad[part] = (total * slope).astype(BF16)

    @pl.when(c == 0)
    def _():
        wait_all(tok, sem)

    wait_all(wts.at[c], w_sems.at[c])
    grads = pgrad[...]
    for k in range(NNZ):
        row = meta[c * NNZ + k]
        acc[row] += dot(grads, wts[c, k].reshape(BS, BS), ((1,), (1,)))
        part = dot(token_block(tok, row), grads, ((0,), (0,))) * loss_scale
        res[k] = part.astype(BF16).reshape(16, 16, BS)
        for d in range(NY):
            for x in range(NX):
                outs[d][0, k * NX + x] = res[k, (y_here + d) % NY * NX + x]

    @pl.when(c == COLS - 1)
    def _():
        keep[...] = acc[:, pl.ds(pl.multiple_of(core * 128, 128), 128)].astype(BF16)
        send[...] = acc[:, pl.ds(pl.multiple_of((1 - core) * 128, 128), 128)].astype(BF16)


def grad_in(meta, own, other, pieces, pre, mgrad, up, down, taps):
    half = pl.BlockSpec((16, 128, BS), lambda c, m: (0, 0, 0))
    return pl.pallas_call(
        grad_in_kernel,
        out_shape=[jax.ShapeDtypeStruct((COLS, 20, 16, BS), BF16)] * NY
        + [jax.ShapeDtypeStruct((16, 128, BS), BF16)] * 2,
        grid_spec=pltpu.PrefetchScalarGridSpec(
            num_scalar_prefetch=1,
            grid=(COLS,),
            in_specs=[ANY] * 11 + [column(TOK), column(TOK), column(PW), column(PW), taps_spec()],
            out_specs=[slabs(20)] * NY + [half, half],
            scratch_shapes=[
                pltpu.VMEM((8, 2, TOK, BS), BF16),
                pltpu.VMEM((COLS, NNZ, 16, 16, BS), BF16),
                pltpu.VMEM((TOK, BS), BF16),
                pltpu.VMEM((NNZ, 16, 16, BS), BF16),
                pltpu.VMEM((16, TOK, BS), F32),
                pltpu.SemaphoreType.DMA,
                pltpu.SemaphoreType.DMA((COLS,)),
            ],
        ),
        compiler_params=params(),
        cost_estimate=pl.CostEstimate(
            flops=4 * TOK * BS * BS * NNZ * COLS, transcendentals=TOK * BS * COLS, bytes_accessed=12 * 2**20
        ),
        name="gradin",
    )(meta, own, other, *pieces, pre, mgrad, up, down, taps)


def first_sum_kernel(pos, extra, meta, a, b, e, f, *outs):
    here = meta[pos]
    for d in range(4):
        for k in range(NNZ):
            at = k * 4 + (here + d) % 4
            total = a[0, at].astype(F32) + b[0, at].astype(F32) + e[0, at].astype(F32) + f[0, at].astype(F32)
            outs[d][0, k] = total.astype(BF16)
        if extra:
            total = a[0, 20].astype(F32) + b[0, 20].astype(F32) + e[0, 20].astype(F32) + f[0, 20].astype(F32)
            outs[d][0, NNZ] = total.astype(BF16)


def first_sum(pos, extra, meta, parts):
    count = NNZ + extra
    return pl.pallas_call(
        functools.partial(first_sum_kernel, pos, extra),
        out_shape=[jax.ShapeDtypeStruct((COLS, count, 16, BS), BF16)] * 4,
        grid_spec=pltpu.PrefetchScalarGridSpec(
            num_scalar_prefetch=1,
            grid=(COLS,),
            in_specs=[slabs(20 + extra)] * 4,
            out_specs=[slabs(count)] * 4,
        ),
        compiler_params=params(),
        cost_estimate=pl.CostEstimate(flops=2**21, transcendentals=0, bytes_accessed=7 * 2**19),
        name="firstsum",
    )(meta, *parts)


def second_sum_kernel(meta, *refs):
    a_parts, b_parts, (keep, send) = refs[:4], refs[4:8], refs[8:]
    core = meta[CORE]

    def total(parts, c, k):
        return sum(p[c, k].astype(F32) for p in parts)

    for c in range(COLS):
        for w, parts in ((0, b_parts), (1, a_parts)):
            for k in range(NNZ):
                val = total(parts, c, k)
                low, high = val[:8], val[8:]
                keep[w, c, k] = jnp.where(core == 0, low, high)
                send[w, c, k] = jnp.where(core == 0, high, low).astype(BF16)
        slab = total(a_parts, c, NNZ)
        for part in range(2):
            half = slab[part * 8 : part * 8 + 8]
            keep[part, c, NNZ] = half.astype(BF16).astype(F32)
            send[part, c, NNZ] = half.astype(BF16)


def second_sum(meta, a_parts, b_parts):
    shape = (2, COLS, NNZ + 1, 8, BS)
    vmem = pl.BlockSpec(memory_space=pltpu.VMEM)
    return pl.pallas_call(
        second_sum_kernel,
        out_shape=[jax.ShapeDtypeStruct(shape, F32), jax.ShapeDtypeStruct(shape, BF16)],
        in_specs=[pl.BlockSpec(memory_space=pltpu.SMEM)] + [vmem] * 8,
        out_specs=[vmem] * 2,
        compiler_params=pltpu.CompilerParams(vmem_limit_bytes=48 * 2**20),
        name="secondsum",
    )(meta, *a_parts, *b_parts)


def place_kernel(meta, keep, got, win, wout, kern):
    first = meta[CORE] == 0
    for w, out in ((0, win), (1, wout)):
        for k in range(NNZ):
            mine = [keep[w, c, k] for c in range(COLS)]
            its = [got[w, c, k].astype(F32) for c in range(COLS)]
            low = [jnp.where(first, m, i) for m, i in zip(mine, its)]
            high = [jnp.where(first, i, m) for m, i in zip(mine, its)]
            block = jnp.stack(low + high, axis=0)
            out[:, k] = jnp.swapaxes(block, 0, 1)
    for c in range(COLS):
        mine = jnp.concatenate([keep[0, c, NNZ], keep[1, c, NNZ]], axis=0)[:9]
        its = jnp.concatenate([got[0, c, NNZ].astype(F32), got[1, c, NNZ].astype(F32)], axis=0)[:9]
        kern[:, c * BS : (c + 1) * BS] = jnp.where(first, mine, its)
        kern[:, (COLS + c) * BS : (COLS + c + 1) * BS] = jnp.where(first, its, mine)


def place(meta, keep, got):
    vmem = pl.BlockSpec(memory_space=pltpu.VMEM)
    return pl.pallas_call(
        place_kernel,
        out_shape=[
            jax.ShapeDtypeStruct((8, NNZ, 8, BS), F32),
            jax.ShapeDtypeStruct((8, NNZ, 8, BS), F32),
            jax.ShapeDtypeStruct((9, 8 * BS), F32),
        ],
        in_specs=[pl.BlockSpec(memory_space=pltpu.SMEM), vmem, vmem],
        out_specs=[vmem] * 3,
        compiler_params=pltpu.CompilerParams(vmem_limit_bytes=48 * 2**20),
        name="place",
    )(meta, keep, got)


def on_device(tokens, cotangent, weight_in, weight_out, mix_kernel, block_rows):
    row, crop = lax.axis_index("rows"), lax.axis_index("crop")
    core, x, ylo = row % 2, row // 2 % NX, row // 8
    my_rows = lax.dynamic_slice_in_dim(block_rows, core * COLS, COLS, axis=0).reshape(-1)
    meta = jnp.concatenate([my_rows, jnp.stack([core, x, crop * 2 + ylo, ylo]).astype(jnp.int32)])

    both = jnp.stack([tokens.reshape(128, 512), cotangent.reshape(128, 512)])
    own = lax.all_gather(both, "hid", axis=0)

    panels = jnp.stack([weight_in, weight_out]).reshape(2, 16, 2, COLS, NNZ, BS)
    panels = panels.transpose(2, 0, 3, 4, 1, 5)
    mine = lax.dynamic_index_in_dim(panels, core, 0, keepdims=False)
    theirs = lax.dynamic_index_in_dim(panels, 1 - core, 0, keepdims=False)
    got = to_partner(theirs)
    piece = jnp.stack([jnp.where(core == 0, mine, got), jnp.where(core == 0, got, mine)])
    xm, xp = along_x(piece, 1), along_x(piece, -1)
    yo = along_y(piece, 1)
    x2 = along_x(piece, 2)
    ym, yp = along_y(xm, 1), along_y(xp, -1)
    y2a, y2b = along_y(x2[:1], 1), along_y(x2[1:], -1)
    pieces = (piece, xm, xp, x2, yo, ym, yp, y2a, y2b)

    other = to_partner(own)
    pre, act, act_top, act_bot = forward(0, meta, own, other, pieces)
    act_up, act_down = to_next_chip(act_bot, 1), to_next_chip(act_top, -1)
    mgrad, mg_top, mg_bot = forward(1, meta, own, other, pieces)
    mg_up, mg_down = to_next_chip(mg_bot, 1), to_next_chip(mg_top, -1)

    outs = grad_out(meta, own, other, act, act_up, act_down, mgrad, mix_kernel)
    a_parts = (outs[0], along_x(outs[1], 1), along_x(outs[3], -1), along_x(outs[2], 2))
    *ins, keep, send = grad_in(meta, own, other, pieces, pre, mgrad, mg_up, mg_down, mix_kernel)
    b_parts = (ins[0], along_y(ins[1], 1), along_y(ins[3], -1), along_y(ins[2], 2))

    terms = (keep.astype(F32) + to_partner(send).astype(F32)).astype(BF16)
    shares = lax.psum_scatter(terms.reshape(8, 2, 128, BS), "hid", scatter_dimension=0, tiled=True)
    grad_tokens = shares.reshape(2, 128, BS).transpose(1, 0, 2).reshape(1, 2, PW, 512)

    a_next = first_sum(YPOS, 1, meta, a_parts)
    a_last = (a_next[0], along_y(a_next[1], 1), along_y(a_next[3], -1), along_y(a_next[2], 2))
    b_next = first_sum(XPOS, 0, meta, b_parts)
    b_last = (b_next[0], along_x(b_next[1], 1), along_x(b_next[3], -1), along_x(b_next[2], 2))
    kept, sent = second_sum(meta, a_last, b_last)
    win, wout, kern = place(meta, kept, to_partner(sent))
    return grad_tokens, win.transpose(0, 2, 1, 3), wout.transpose(0, 2, 1, 3), kern


def solution(mesh):
    placed = (
        P("crop", "rows", None, "hid"),
        P("crop", "rows", None, "hid"),
        P("rows", "hid", None, None),
        P("rows", "hid", None, None),
        P(None, "hid"),
        P("hid", None),
    )
    return jax.shard_map(
        on_device,
        mesh=mesh,
        in_specs=placed,
        out_specs=(
            P("crop", "rows", None, "hid"),
            P(("crop", "rows"), "hid", None, None),
            P(("crop", "rows"), "hid", None, None),
            P(None, "hid"),
        ),
        check_vma=False,
    )
```

```python
import functools

import jax
import jax.numpy as jnp
from jax import lax
from jax.experimental import pallas as pl
from jax.experimental.pallas import tpu as pltpu
from jax.sharding import PartitionSpec as P

root_two_pi = 0.7978845608
cubic_coef = 0.044715
loss_scale = 0.03125

F32, BF16 = jnp.float32, jnp.bfloat16
NX, NY, NC = 4, 4, 2
COLS, NNZ, BS, PW = 4, 5, 256, 64
TOK = 256
CORE, XPOS, YPOS, YLO = 20, 21, 22, 23
ANY = pl.BlockSpec(memory_space=pl.ANY)


def row_perm(move):
    pairs = []
    for y in range(2):
        for x in range(NX):
            for c in range(NC):
                y2, x2, c2 = move(y, x, c)
                pairs.append(((y * NX + x) * NC + c, (y2 * NX + x2 % NX) * NC + c2))
    return pairs


def along_x(value, step):
    return lax.ppermute(value, "rows", row_perm(lambda y, x, c: (y, x + step, c)))


def to_partner(value):
    return lax.ppermute(value, "rows", row_perm(lambda y, x, c: (y, x, 1 - c)))


def along_y(value, step):
    pairs = [(y * 8 + r, (y + step) % NY * 8 + r) for y in range(NY) for r in range(8)]
    return lax.ppermute(value, ("crop", "rows"), pairs)


def to_next_chip(value, step):
    pairs = []
    for q in range(8):
        if 0 <= q + step < 8:
            pairs += [(q * 2 + c, (q + step) * 2 + c) for c in range(NC)]
    return lax.ppermute(value, "rows", pairs)


def dot(a, b, dims):
    return lax.dot_general(a, b, (dims, ((), ())), preferred_element_type=F32)


def params():
    return pltpu.CompilerParams(dimension_semantics=("arbitrary",), vmem_limit_bytes=48 * 2**20)


def after(value, *others):
    return pl.pallas_call(
        lambda *refs: None,
        out_shape=jax.ShapeDtypeStruct(value.shape, value.dtype),
        in_specs=[ANY] * (1 + len(others)),
        out_specs=ANY,
        input_output_aliases={0: 0},
        name="after",
    )(value, *others)


def start_tokens(meta, own, other, which, buf, sem):
    core = meta[CORE]
    for src, at in ((own, core), (other, 1 - core)):
        rows = pl.ds(pl.multiple_of(at * 128, 128), 128)
        for half in range(2):
            pltpu.make_async_copy(
                src.at[:, which, :, pl.ds(half * BS, BS)], buf.at[:, half, rows], sem
            ).start()


def wait_all(buf, sem):
    pltpu.make_async_copy(buf, buf, sem).wait()


def start_weights(meta, pieces, which, buf, sems):
    x, ylo = meta[XPOS], meta[YLO]
    own, xm, xp, x2a, x2b, yo, ym, yp, y2a, y2b = pieces
    here, there = ylo * NX, (1 - ylo) * NX
    at = lambda base, d: base + (x + d) % NX
    plan = []
    for s in range(2):
        plan += [
            (own, s, at(here, 0), s),
            (xm, s, at(here, 3), s),
            (xp, s, at(here, 1), s),
            (yo, s, at(there, 0), s),
            (ym, s, at(there, 3), s),
            (yp, s, at(there, 1), s),
        ]
    for base, a, b in ((here, x2a, x2b), (there, y2a, y2b)):
        plan += [(a, 0, at(base, 2), 0), (b, 0, at(base, 2), 1)]
    for c in range(COLS):
        for src, row, j, s in plan:
            pltpu.make_async_copy(src.at[row, which, c], buf.at[c, :, 2 * j + s], sems.at[c]).start()


def token_block(buf, row):
    return buf[row // 2, row % 2]


def forward_kernel(which, meta, own, other, *refs):
    pieces, refs = refs[:10], refs[10:]
    if which == 0:
        pre_ref, act_ref, top_ref, bot_ref, tok, wts, tok_sem, w_sems = refs
    else:
        act_ref, top_ref, bot_ref, tok, wts, tok_sem, w_sems = refs
    c = pl.program_id(0)

    @pl.when(c == 0)
    def _():
        start_tokens(meta, own, other, which, tok, tok_sem)
        start_weights(meta, pieces, which, wts, w_sems)
        wait_all(tok, tok_sem)

    wait_all(wts.at[c], w_sems.at[c])
    dims = ((1,), (0,)) if which == 0 else ((1,), (1,))
    total = jnp.zeros((TOK, BS), F32)
    for k in range(NNZ):
        total += dot(token_block(tok, meta[c * NNZ + k]), wts[c, k].reshape(BS, BS), dims)
    if which == 0:
        pre_ref[...] = total
        inner = root_two_pi * (total + cubic_coef * total * total * total)
        total = 0.5 * total * (1.0 + jnp.tanh(inner))
    out = total.astype(BF16)
    act_ref[...] = out
    top_ref[...] = out[:PW]
    bot_ref[...] = out[TOK - PW :]


def column(rows):
    return pl.BlockSpec((rows, BS), lambda c, m: (0, c))


def forward(which, meta, own, other, pieces):
    outs = [(TOK, BF16), (PW, BF16), (PW, BF16)]
    if which == 0:
        outs = [(TOK, F32)] + outs
    return pl.pallas_call(
        functools.partial(forward_kernel, which),
        out_shape=[jax.ShapeDtypeStruct((r, COLS * BS), t) for r, t in outs],
        grid_spec=pltpu.PrefetchScalarGridSpec(
            num_scalar_prefetch=1,
            grid=(COLS,),
            in_specs=[ANY] * 12,
            out_specs=[column(r) for r, _ in outs],
            scratch_shapes=[
                pltpu.VMEM((8, 2, TOK, BS), BF16),
                pltpu.VMEM((COLS, NNZ, 16, 16, BS), BF16),
                pltpu.SemaphoreType.DMA,
                pltpu.SemaphoreType.DMA((COLS,)),
            ],
        ),
        compiler_params=params(),
        cost_estimate=pl.CostEstimate(
            flops=2 * TOK * BS * BS * NNZ * COLS, transcendentals=TOK * BS * COLS, bytes_accessed=7 * 2**20
        ),
        name=("preact", "mixgrad")[which],
    )(meta, own, other, *pieces)


def shifted_rows(mid, up, down):
    cells = lax.broadcasted_iota(jnp.int32, (PW, BS), 0)
    out = []
    for row in [up[...]] + [mid[i * PW : (i + 1) * PW] for i in range(4)] + [down[...]]:
        row = row.astype(F32)
        left = jnp.where(cells == 0, 0.0, pltpu.roll(row, 1, 0))
        right = jnp.where(cells == PW - 1, 0.0, pltpu.roll(row, PW - 1, 0))
        out.append((left, row, right))
    return out


def grad_out_kernel(meta, own, other, act, up, down, mgrad, taps, *refs):
    outs, (cot, mixed, res, sem) = refs[:NX], refs[NX:]
    c = pl.program_id(0)
    x = meta[XPOS]

    @pl.when(c == 0)
    def _():
        start_tokens(meta, own, other, 1, cot, sem)

    rows = shifted_rows(act, up, down)
    for i in range(4):
        total = jnp.zeros((PW, BS), F32)
        for a in range(3):
            for b in range(3):
                total += taps[3 * a + b : 3 * a + b + 1] * rows[i + a][b]
        mixed[i * PW : (i + 1) * PW] = total.astype(BF16)
    sums = []
    for a in range(3):
        for b in range(3):
            total = jnp.zeros((PW, BS), F32)
            for i in range(4):
                total += rows[i + a][b] * mgrad[i * PW : (i + 1) * PW].astype(F32)
            sums.append(jnp.sum(total, axis=0, keepdims=True))
    slab = jnp.concatenate(sums + [jnp.zeros((7, BS), F32)], axis=0) * loss_scale
    for d in range(NX):
        outs[d][0, 20] = slab.astype(BF16)

    @pl.when(c == 0)
    def _():
        wait_all(cot, sem)

    mix = mixed[...]
    for k in range(NNZ):
        part = dot(mix, token_block(cot, meta[c * NNZ + k]), ((0,), (0,))) * loss_scale
        res[k] = part.astype(BF16).reshape(16, 16, BS)
        for d in range(NX):
            for y in range(NY):
                outs[d][0, k * NY + y] = res[k, y * NX + (x + d) % NX]


def slabs(count):
    return pl.BlockSpec((1, count, 16, BS), lambda c, m: (c, 0, 0, 0))


def taps_spec():
    return pl.BlockSpec((9, BS), lambda c, m: (0, m[CORE] * COLS + c))


def grad_out(meta, own, other, act, up, down, mgrad, taps):
    return pl.pallas_call(
        grad_out_kernel,
        out_shape=[jax.ShapeDtypeStruct((COLS, 21, 16, BS), BF16)] * NX,
        grid_spec=pltpu.PrefetchScalarGridSpec(
            num_scalar_prefetch=1,
            grid=(COLS,),
            in_specs=[ANY, ANY, column(TOK), column(PW), column(PW), column(TOK), taps_spec()],
            out_specs=[slabs(21)] * NX,
            scratch_shapes=[
                pltpu.VMEM((8, 2, TOK, BS), BF16),
                pltpu.VMEM((TOK, BS), BF16),
                pltpu.VMEM((NNZ, 16, 16, BS), BF16),
                pltpu.SemaphoreType.DMA,
            ],
        ),
        compiler_params=params(),
        cost_estimate=pl.CostEstimate(
            flops=2 * TOK * BS * BS * NNZ * COLS, transcendentals=0, bytes_accessed=7 * 2**20
        ),
        name="gradout",
    )(meta, own, other, act, up, down, mgrad, taps)


def grad_in_kernel(meta, own, other, *refs):
    pieces, refs = refs[:10], refs[10:]
    _, pre, mgrad, up, down, taps = refs[:6]
    outs, (keep, send, tok, wts, pgrad, res, acc, sem, w_sems) = refs[6 : 6 + NY], refs[6 + NY :]
    c = pl.program_id(0)
    core, y_here = meta[CORE], meta[YPOS]

    @pl.when(c == 0)
    def _():
        start_tokens(meta, own, other, 0, tok, sem)
        start_weights(meta, pieces, 0, wts, w_sems)
        acc[...] = jnp.zeros_like(acc)

    rows = shifted_rows(mgrad, up, down)
    for i in range(4):
        part = pl.ds(i * PW, PW)
        total = jnp.zeros((PW, BS), F32)
        for a in range(3):
            for b in range(3):
                total += taps[3 * a + b : 3 * a + b + 1] * rows[i + 2 - a][2 - b]
        p = pre[part]
        t = jnp.tanh(root_two_pi * (p + cubic_coef * p * p * p))
        slope = 0.5 * (1.0 + t) + 0.5 * p * (1.0 - t * t) * root_two_pi * (1.0 + 3.0 * cubic_coef * p * p)
        pgrad[part] = (total * slope).astype(BF16)

    @pl.when(c == 0)
    def _():
        wait_all(tok, sem)

    wait_all(wts.at[c], w_sems.at[c])
    grads = pgrad[...]
    for k in range(NNZ):
        row = meta[c * NNZ + k]
        acc[row] += dot(grads, wts[c, k].reshape(BS, BS), ((1,), (1,)))
        part = dot(token_block(tok, row), grads, ((0,), (0,))) * loss_scale
        res[k] = part.astype(BF16).reshape(16, 16, BS)
        for d in range(NY):
            for x in range(NX):
                outs[d][0, k * NX + x] = res[k, (y_here + d) % NY * NX + x]

    @pl.when(c == COLS - 1)
    def _():
        keep[...] = acc[:, pl.ds(pl.multiple_of(core * 128, 128), 128)].astype(BF16)
        send[...] = acc[:, pl.ds(pl.multiple_of((1 - core) * 128, 128), 128)].astype(BF16)


def grad_in(meta, own, other, pieces, after, pre, mgrad, up, down, taps):
    half = pl.BlockSpec((16, 128, BS), lambda c, m: (0, 0, 0))
    return pl.pallas_call(
        grad_in_kernel,
        out_shape=[jax.ShapeDtypeStruct((COLS, 20, 16, BS), BF16)] * NY
        + [jax.ShapeDtypeStruct((16, 128, BS), BF16)] * 2,
        grid_spec=pltpu.PrefetchScalarGridSpec(
            num_scalar_prefetch=1,
            grid=(COLS,),
            in_specs=[ANY] * 13 + [column(TOK), column(TOK), column(PW), column(PW), taps_spec()],
            out_specs=[slabs(20)] * NY + [half, half],
            scratch_shapes=[
                pltpu.VMEM((8, 2, TOK, BS), BF16),
                pltpu.VMEM((COLS, NNZ, 16, 16, BS), BF16),
                pltpu.VMEM((TOK, BS), BF16),
                pltpu.VMEM((NNZ, 16, 16, BS), BF16),
                pltpu.VMEM((16, TOK, BS), F32),
                pltpu.SemaphoreType.DMA,
                pltpu.SemaphoreType.DMA((COLS,)),
            ],
        ),
        compiler_params=params(),
        cost_estimate=pl.CostEstimate(
            flops=4 * TOK * BS * BS * NNZ * COLS, transcendentals=TOK * BS * COLS, bytes_accessed=12 * 2**20
        ),
        name="gradin",
    )(meta, own, other, *pieces, after, pre, mgrad, up, down, taps)


def first_sum_kernel(pos, extra, meta, a, b, e, f, *outs):
    here = meta[pos]
    for d in range(4):
        for k in range(NNZ):
            at = k * 4 + (here + d) % 4
            total = a[0, at].astype(F32) + b[0, at].astype(F32) + e[0, at].astype(F32) + f[0, at].astype(F32)
            outs[d][0, k] = total.astype(BF16)
        if extra:
            total = a[0, 20].astype(F32) + b[0, 20].astype(F32) + e[0, 20].astype(F32) + f[0, 20].astype(F32)
            outs[d][0, NNZ] = total.astype(BF16)


def first_sum(pos, extra, meta, parts):
    count = NNZ + extra
    return pl.pallas_call(
        functools.partial(first_sum_kernel, pos, extra),
        out_shape=[jax.ShapeDtypeStruct((COLS, count, 16, BS), BF16)] * 4,
        grid_spec=pltpu.PrefetchScalarGridSpec(
            num_scalar_prefetch=1,
            grid=(COLS,),
            in_specs=[slabs(20 + extra)] * 4,
            out_specs=[slabs(count)] * 4,
        ),
        compiler_params=params(),
        cost_estimate=pl.CostEstimate(flops=2**21, transcendentals=0, bytes_accessed=7 * 2**19),
        name="firstsum",
    )(meta, *parts)


def second_sum_kernel(meta, *refs):
    a_parts, b_parts, (keep, send) = refs[:4], refs[4:8], refs[8:]
    core = meta[CORE]

    def total(parts, c, k):
        return sum(p[c, k].astype(F32) for p in parts)

    for c in range(COLS):
        for w, parts in ((0, b_parts), (1, a_parts)):
            for k in range(NNZ):
                val = total(parts, c, k)
                low, high = val[:8], val[8:]
                keep[w, c, k] = jnp.where(core == 0, low, high)
                send[w, c, k] = jnp.where(core == 0, high, low).astype(BF16)
        slab = total(a_parts, c, NNZ)
        for part in range(2):
            half = slab[part * 8 : part * 8 + 8]
            keep[part, c, NNZ] = half.astype(BF16).astype(F32)
            send[part, c, NNZ] = half.astype(BF16)


def second_sum(meta, a_parts, b_parts):
    shape = (2, COLS, NNZ + 1, 8, BS)
    vmem = pl.BlockSpec(memory_space=pltpu.VMEM)
    return pl.pallas_call(
        second_sum_kernel,
        out_shape=[jax.ShapeDtypeStruct(shape, F32), jax.ShapeDtypeStruct(shape, BF16)],
        in_specs=[pl.BlockSpec(memory_space=pltpu.SMEM)] + [vmem] * 8,
        out_specs=[vmem] * 2,
        compiler_params=pltpu.CompilerParams(vmem_limit_bytes=48 * 2**20),
        name="secondsum",
    )(meta, *a_parts, *b_parts)


def place_kernel(meta, keep, got, win, wout, kern):
    first = meta[CORE] == 0
    for w, out in ((0, win), (1, wout)):
        for k in range(NNZ):
            mine = [keep[w, c, k] for c in range(COLS)]
            its = [got[w, c, k].astype(F32) for c in range(COLS)]
            low = [jnp.where(first, m, i) for m, i in zip(mine, its)]
            high = [jnp.where(first, i, m) for m, i in zip(mine, its)]
            block = jnp.stack(low + high, axis=0)
            out[:, k] = jnp.swapaxes(block, 0, 1)
    for c in range(COLS):
        mine = jnp.concatenate([keep[0, c, NNZ], keep[1, c, NNZ]], axis=0)[:9]
        its = jnp.concatenate([got[0, c, NNZ].astype(F32), got[1, c, NNZ].astype(F32)], axis=0)[:9]
        kern[:, c * BS : (c + 1) * BS] = jnp.where(first, mine, its)
        kern[:, (COLS + c) * BS : (COLS + c + 1) * BS] = jnp.where(first, its, mine)


def place(meta, keep, got):
    vmem = pl.BlockSpec(memory_space=pltpu.VMEM)
    return pl.pallas_call(
        place_kernel,
        out_shape=[
            jax.ShapeDtypeStruct((8, NNZ, 8, BS), F32),
            jax.ShapeDtypeStruct((8, NNZ, 8, BS), F32),
            jax.ShapeDtypeStruct((9, 8 * BS), F32),
        ],
        in_specs=[pl.BlockSpec(memory_space=pltpu.SMEM), vmem, vmem],
        out_specs=[vmem] * 3,
        compiler_params=pltpu.CompilerParams(vmem_limit_bytes=48 * 2**20),
        name="place",
    )(meta, keep, got)


def on_device(tokens, cotangent, weight_in, weight_out, mix_kernel, block_rows):
    row, crop = lax.axis_index("rows"), lax.axis_index("crop")
    core, x, ylo = row % 2, row // 2 % NX, row // 8
    my_rows = lax.dynamic_slice_in_dim(block_rows, core * COLS, COLS, axis=0).reshape(-1)
    meta = jnp.concatenate([my_rows, jnp.stack([core, x, crop * 2 + ylo, ylo]).astype(jnp.int32)])

    both = jnp.stack([tokens.reshape(128, 512), cotangent.reshape(128, 512)])
    own = lax.all_gather(both, "hid", axis=0)

    panels = jnp.stack([weight_in, weight_out]).reshape(2, 16, 2, COLS, NNZ, BS)
    panels = panels.transpose(2, 0, 3, 4, 1, 5)
    mine = lax.dynamic_index_in_dim(panels, core, 0, keepdims=False)
    theirs = lax.dynamic_index_in_dim(panels, 1 - core, 0, keepdims=False)
    got = to_partner(theirs)
    piece = jnp.stack([jnp.where(core == 0, mine, got), jnp.where(core == 0, got, mine)])
    xm, xp = along_x(piece, 1), along_x(piece, -1)
    yo = along_y(piece, 1)
    ym, yp = along_y(xm, 1), along_y(xp, -1)
    x2a, x2b = along_x(xm[:1], 1), along_x(xp[1:], -1)
    y2a, y2b = along_y(x2a, 1), along_y(x2b, -1)
    pieces = (piece, xm, xp, x2a, x2b, yo, ym, yp, y2a, y2b)

    own = after(own, y2a, y2b)
    other = to_partner(own)
    pre, act, act_top, act_bot = forward(0, meta, own, other, pieces)
    act_up, act_down = to_next_chip(act_bot, 1), to_next_chip(act_top, -1)
    mgrad, mg_top, mg_bot = forward(1, meta, own, other, pieces)
    mg_up, mg_down = to_next_chip(mg_bot, 1), to_next_chip(mg_top, -1)

    outs = grad_out(meta, own, other, act, act_up, act_down, mgrad, mix_kernel)
    a_parts = (outs[0], along_x(outs[1], 1), along_x(outs[3], -1), along_x(outs[2], 2))
    *ins, keep, send = grad_in(meta, own, other, pieces, outs[0], pre, mgrad, mg_up, mg_down, mix_kernel)
    b_parts = (ins[0], along_y(ins[1], 1), along_y(ins[3], -1), along_y(ins[2], 2))

    terms = (keep.astype(F32) + to_partner(send).astype(F32)).astype(BF16)
    shares = lax.psum_scatter(terms.reshape(8, 2, 128, BS), "hid", scatter_dimension=0, tiled=True)
    grad_tokens = shares.reshape(2, 128, BS).transpose(1, 0, 2).reshape(1, 2, PW, 512)

    a_next = first_sum(YPOS, 1, meta, a_parts)
    a_last = (a_next[0], along_y(a_next[1], 1), along_y(a_next[3], -1), along_y(a_next[2], 2))
    b_next = first_sum(XPOS, 0, meta, b_parts)
    b_last = (b_next[0], along_x(b_next[1], 1), along_x(b_next[3], -1), along_x(b_next[2], 2))
    kept, sent = second_sum(meta, a_last, b_last)
    win, wout, kern = place(meta, kept, to_partner(sent))
    return grad_tokens, win.transpose(0, 2, 1, 3), wout.transpose(0, 2, 1, 3), kern


def solution(mesh):
    placed = (
        P("crop", "rows", None, "hid"),
        P("crop", "rows", None, "hid"),
        P("rows", "hid", None, None),
        P("rows", "hid", None, None),
        P(None, "hid"),
        P("hid", None),
    )
    return jax.shard_map(
        on_device,
        mesh=mesh,
        in_specs=placed,
        out_specs=(
            P("crop", "rows", None, "hid"),
            P(("crop", "rows"), "hid", None, None),
            P(("crop", "rows"), "hid", None, None),
            P(None, "hid"),
        ),
        check_vma=False,
    )
```

```python
import functools

import jax
import jax.numpy as jnp
from jax import lax
from jax.experimental import pallas as pl
from jax.experimental.pallas import tpu as pltpu
from jax.sharding import PartitionSpec as P

root_two_pi = 0.7978845608
cubic_coef = 0.044715
loss_scale = 0.03125

F32, BF16 = jnp.float32, jnp.bfloat16
NX, NY, NZ = 4, 4, 8
HALF, NNZ, BS, PW = 4, 5, 256, 64
TOK = 256
CORE, XPOS, YPOS, YLO, ZPOS = 40, 41, 42, 43, 44
VMEM = pl.BlockSpec(memory_space=pltpu.VMEM)
SMEM = pl.BlockSpec(memory_space=pltpu.SMEM)


def by_core(value, step0, step1):
    pairs = []
    for y in range(NY):
        for x in range(NX):
            for c, (dy, dx) in enumerate((step0, step1)):
                target = (y + dy) % NY * 8 + (x + dx) % NX * 2 + c
                pairs.append((y * 8 + x * 2 + c, target))
    return lax.ppermute(value, ("crop", "rows"), pairs)


def first(value, step):
    return by_core(value, (step, 0), (0, step))


def second(value, step):
    return by_core(value, (0, step), (step, 0))


def to_partner(value):
    return lax.ppermute(value, "rows", [(r, r ^ 1) for r in range(16)])


def to_next_chip(value, step):
    pairs = []
    for q in range(8):
        if 0 <= q + step < 8:
            pairs += [(q * 2 + c, (q + step) * 2 + 1 - c) for c in range(2)]
    return lax.ppermute(value, "rows", pairs)


def along_z(value, step):
    return lax.ppermute(value, "hid", [(z, (z + step) % NZ) for z in range(NZ)])


def dot(a, b, dims):
    return lax.dot_general(a, b, (dims, ((), ())), preferred_element_type=F32)


def local(kernel, name, outs, args, scratch=(), flops=2**20):
    shapes = [jax.ShapeDtypeStruct(s, t) for s, t in outs]
    size = sum(a.size * a.dtype.itemsize for a in args[1:])
    return pl.pallas_call(
        kernel,
        out_shape=shapes,
        in_specs=[SMEM] + [VMEM] * (len(args) - 1),
        out_specs=[VMEM] * len(outs),
        scratch_shapes=list(scratch),
        compiler_params=pltpu.CompilerParams(vmem_limit_bytes=28 * 2**20),
        cost_estimate=pl.CostEstimate(flops=flops, transcendentals=0, bytes_accessed=size),
        name=name,
    )(*args)


def place_tokens(meta, pieces, buf):
    z = meta[ZPOS]
    own, r1, r2, r3, l1, l2, l3, r4, l4 = pieces
    plan = [(own, 0, 0), (r1, 7, 0), (r2, 6, 0), (r3, 5, 0), (l1, 1, 0), (l2, 2, 0), (l3, 3, 0)]
    for src, d, at in plan + [(r4, 4, 0), (l4, 4, 128)]:
        h = (z + d) % NZ
        for part in range(2):
            buf[2 * h + part, at : at + src.shape[0]] = src[:, part * BS : (part + 1) * BS]


def weight_plan(meta, pieces):
    core, x, ylo = meta[CORE], meta[XPOS], meta[YLO]
    own, r1, r2, r3, r4, r5, r6, r7, r8, r9 = pieces
    here, there = ylo * NX, (1 - ylo) * NX
    at = lambda base, d: base + (x + d) % NX
    pick = lambda a, b: jnp.where(core == 0, a, b)
    slots = [
        (own, at(here, 0)),
        (r1, pick(at(here, 3), at(there, 0))),
        (r2, pick(at(here, 1), at(here, 3))),
        (r3, pick(at(there, 0), at(here, 1))),
        (r4, pick(at(there, 3), at(there, 1))),
        (r5, pick(at(there, 1), at(there, 3))),
    ]
    plan = [(src, s, 2 * j + s) for src, j in slots for s in range(2)]
    for j, a, b in ((at(here, 2), r6, r7), (at(there, 2), r8, r9)):
        plan += [(a, 0, 2 * j), (b, 0, 2 * j + 1)]
    return plan


def forward_kernel(half, meta, *refs):
    if half == 0:
        tokens, pieces, outs = refs[:9], refs[9:19], refs[19:]
        pre, out, top, bot, wts, tok = outs
        place_tokens(meta, tokens, tok)
    else:
        tok, pieces, outs = refs[0], refs[1:11], refs[11:]
        pre, out, top, bot, wts = outs
    plan = weight_plan(meta, pieces)
    core = meta[CORE]
    for c in range(HALF):
        col = half * HALF + c
        for k in range(NNZ):
            for src, row, slot in plan:
                wts[c, k, slot] = src[row, col, k]

    def total(c, dims):
        acc = None
        for k in range(NNZ):
            part = dot(tok[meta[(half * HALF + c) * NNZ + k]], wts[c, k].reshape(BS, BS), dims)
            acc = part if acc is None else acc + part
        return acc

    @pl.when(core == 0)
    def _():
        for c in range(HALF):
            cols = slice(c * BS, (c + 1) * BS)
            p = total(c, ((1,), (0,)))
            pre[:, cols] = p
            t = jnp.tanh(root_two_pi * (p + cubic_coef * p * p * p))
            out[:, cols] = (0.5 * p * (1.0 + t)).astype(BF16)

    @pl.when(core != 0)
    def _():
        for c in range(HALF):
            cols = slice(c * BS, (c + 1) * BS)
            out[:, cols] = total(c, ((1,), (1,))).astype(BF16)

    top[...] = out[:PW]
    bot[...] = out[TOK - PW :]


def forward(half, meta, tokens, pieces):
    wide = HALF * BS
    outs = [((TOK, wide), F32), ((TOK, wide), BF16), ((PW, wide), BF16), ((PW, wide), BF16)]
    outs.append(((HALF, NNZ, 16, 16, BS), BF16))
    if half == 0:
        outs.append(((16, TOK, BS), BF16))
    kernel = functools.partial(forward_kernel, half)
    return local(kernel, "forward", outs, (meta, *tokens, *pieces), flops=2 * TOK * BS * BS * NNZ * HALF)


def shifted_rows(mid, up, down, cols):
    cells = lax.broadcasted_iota(jnp.int32, (PW, BS), 0)
    out = []
    for row in [up[:, cols]] + [mid[i * PW : (i + 1) * PW, cols] for i in range(4)] + [down[:, cols]]:
        row = row.astype(F32)
        left = jnp.where(cells == 0, 0.0, pltpu.roll(row, 1, 0))
        right = jnp.where(cells == PW - 1, 0.0, pltpu.roll(row, PW - 1, 0))
        out.append((left, row, right))
    return out


def backward_kernel(half, meta, tok, got, mine, up, down, pre, taps, *refs):
    if half == 1:
        kern_first, refs = refs[0], refs[1:]
    g0, g1, g3, g2a, g2b, pgrad, kern, conv, lhs, res = refs
    core, x, y = meta[CORE], meta[XPOS], meta[YPOS]
    is_in = core == 0
    kern[...] = jnp.zeros_like(kern)
    base = 0
    if half == 1:
        kern[:, : HALF * BS] = kern_first[...]
        base = HALF * BS
    for c in range(HALF):
        col = half * HALF + c
        cols = slice(c * BS, (c + 1) * BS)
        wide = slice(col * BS, (col + 1) * BS)
        tap = [jnp.where(is_in, taps[8 - j : 9 - j, wide], taps[j : j + 1, wide]) for j in range(9)]
        rows = shifted_rows(got, up, down, cols)
        for i in range(4):
            acc = jnp.zeros((PW, BS), F32)
            for a in range(3):
                for b in range(3):
                    acc += tap[3 * a + b] * rows[i + a][b]
            conv[i * PW : (i + 1) * PW] = acc

        @pl.when(is_in)
        def _():
            p = pre[:, cols]
            t = jnp.tanh(root_two_pi * (p + cubic_coef * p * p * p))
            slope = 0.5 * (1.0 + t) + 0.5 * p * (1.0 - t * t) * root_two_pi * (
                1.0 + 3.0 * cubic_coef * p * p
            )
            lhs[...] = (conv[...] * slope).astype(BF16)
            pgrad[:, cols] = lhs[...]
            for k in range(NNZ):
                part = dot(tok[meta[col * NNZ + k]], lhs[...], ((0,), (0,))) * loss_scale
                res[k] = part.astype(BF16).reshape(16, 16, BS)

        @pl.when(core != 0)
        def _():
            lhs[...] = conv[...].astype(BF16)
            for k in range(NNZ):
                part = dot(lhs[...], tok[meta[col * NNZ + k]], ((0,), (0,))) * loss_scale
                res[k] = part.astype(BF16).reshape(16, 16, BS)
            sums = []
            near = shifted_rows(got, up, down, cols)
            for a in range(3):
                for b in range(3):
                    acc = jnp.zeros((PW, BS), F32)
                    for i in range(4):
                        acc += near[i + a][b] * mine[i * PW : (i + 1) * PW, cols].astype(F32)
                    sums.append(jnp.sum(acc, axis=0, keepdims=True))
            slab = jnp.concatenate(sums + [jnp.zeros((7, BS), F32)], axis=0) * loss_scale
            kern[:, base + c * BS : base + (c + 1) * BS] = slab.astype(BF16)

        here = jnp.where(is_in, y, x)
        far = jnp.where(is_in, NX, 1)
        near_step = jnp.where(is_in, 1, NY)
        for d, out in ((0, g0), (1, g1), (3, g3), (2, g2a if c < 2 else g2b)):
            start = (here + d) % 4 * far
            for k in range(NNZ):
                for s in range(4):
                    out[c % 2 if d == 2 else c, k * 4 + s] = res[k, start + s * near_step]


def backward(half, meta, tok, got, mine, up, down, pre, taps, kern_first=()):
    full, part = (HALF, 20, 16, BS), (2, 20, 16, BS)
    outs = [(full, BF16)] * 3 + [(part, BF16)] * 2
    outs += [((TOK, HALF * BS), BF16), ((16, (1 + half) * HALF * BS), BF16)]
    scratch = [
        pltpu.VMEM((TOK, BS), F32),
        pltpu.VMEM((TOK, BS), BF16),
        pltpu.VMEM((NNZ, 16, 16, BS), BF16),
    ]
    kernel = functools.partial(backward_kernel, half)
    args = (meta, tok, got, mine, up, down, pre, taps, *kern_first)
    return local(kernel, "backward", outs, args, scratch, flops=2 * TOK * BS * BS * NNZ * HALF)


def token_grad_kernel(meta, pg0, pg1, w0, w1, keep, send, acc):
    @pl.when(meta[CORE] == 0)
    def _():
        acc[...] = jnp.zeros_like(acc)
        for half, (pg, wts) in enumerate(((pg0, w0), (pg1, w1))):
            for c in range(HALF):
                for k in range(NNZ):
                    row = meta[(half * HALF + c) * NNZ + k]
                    wt = wts[c, k].reshape(BS, BS)
                    acc[row] += dot(pg[:, c * BS : (c + 1) * BS], wt, ((1,), (1,)))
        for r in range(16):
            keep[r // 2, r % 2] = acc[r, :128].astype(BF16)
            send[r // 2, r % 2] = acc[r, 128:].astype(BF16)


def token_grad(meta, *args):
    shape = ((NZ, 2, 128, BS), BF16)
    return local(
        token_grad_kernel,
        "tokengrad",
        [shape] * 2,
        (meta, *args),
        [pltpu.VMEM((16, TOK, BS), F32)],
        flops=4 * TOK * BS * BS * NNZ * HALF,
    )


def spread_kernel(meta, keep, got, *outs):
    for d, out in enumerate(outs):
        z = (meta[ZPOS] + d) % NZ
        out[...] = jnp.where(meta[CORE] == 0, keep[z], got[z])


def gather_sum_kernel(meta, *refs):
    parts, out = refs[:NZ], refs[NZ]
    for b in range(2):
        out[:, b * BS : (b + 1) * BS] = sum(p[b].astype(F32) for p in parts).astype(BF16)


def relay_kernel(meta, g1, g3, ra, rb, o1, o3):
    for c in range(HALF):
        if c < 2:
            o1[c] = (g1[c].astype(F32) + ra[c].astype(F32)).astype(BF16)
            o3[c] = g3[c]
        else:
            o1[c] = g1[c]
            o3[c] = (g3[c].astype(F32) + rb[c - 2].astype(F32)).astype(BF16)


def first_sum_kernel(meta, *refs):
    halves, kerns, outs = (refs[:3], refs[3:6]), refs[6:10], refs[10:]
    own, prev, nxt, far = (k[...].astype(F32) for k in kerns)
    slab = ((own + far) + (prev + nxt)).astype(BF16)
    here = jnp.where(meta[CORE] == 0, meta[XPOS], meta[YPOS])
    for d in range(4):
        s = (here + d) % 4
        for c in range(2 * HALF):
            for k in range(NNZ):
                at = k * 4 + s
                a, b, e = (g[c % HALF, at].astype(F32) for g in halves[c // HALF])
                outs[d][c, k] = (a + b + e).astype(BF16)
            outs[d][c, NNZ] = slab[:, c * BS : (c + 1) * BS]


def second_sum_kernel(meta, own, prev, nxt, far, keep, send):
    first_core = meta[CORE] == 0
    for c in range(2 * HALF):
        for k in range(NNZ + 1):
            a, b, e, f = (r[c, k].astype(F32) for r in (own, prev, nxt, far))
            total = ((a + f) + (b + e)).astype(BF16)
            low, high = total[:8], total[8:]
            if k < NNZ:
                keep[c, k] = jnp.where(first_core, low, high)
                send[c, k] = jnp.where(first_core, high, low)
            else:
                for out in (keep, send):
                    out[c, NNZ] = low
                    out[c, NNZ + 1] = high


def place_kernel(meta, keep, got, win, wout, kern):
    is_in = meta[CORE] == 0
    for k in range(NNZ):
        mine = jnp.stack([keep[c, k].astype(F32) for c in range(2 * HALF)], axis=0)
        its = jnp.stack([got[c, k].astype(F32) for c in range(2 * HALF)], axis=0)
        mine, its = jnp.swapaxes(mine, 0, 1), jnp.swapaxes(its, 0, 1)
        win[:, k] = jnp.where(is_in, mine, its)
        wout[:, k] = jnp.where(is_in, its, mine)
    for c in range(2 * HALF):
        rows = [jnp.where(is_in, got[c, NNZ + i], keep[c, NNZ + i]).astype(F32) for i in range(2)]
        kern[:, c * BS : (c + 1) * BS] = jnp.concatenate(rows, axis=0)[:9]


def on_device(tokens, cotangent, weight_in, weight_out, mix_kernel, block_rows):
    row, crop, z = lax.axis_index("rows"), lax.axis_index("crop"), lax.axis_index("hid")
    core, x, ylo = row % 2, row // 2 % NX, row // 8
    place = jnp.stack([core, x, crop * 2 + ylo, ylo, z]).astype(jnp.int32)
    meta = jnp.concatenate([block_rows.reshape(-1), place])
    is_in = core == 0

    def side(a, b):
        mine, theirs = jnp.where(is_in, a, b), jnp.where(is_in, b, a)
        got = to_partner(theirs)
        return jnp.where(is_in, mine, got), jnp.where(is_in, got, mine)

    own = jnp.stack(side(*(w.transpose(1, 2, 0, 3) for w in (weight_in, weight_out))))
    t0 = jnp.concatenate(side(tokens.reshape(128, 512), cotangent.reshape(128, 512)))

    r1 = by_core(own, (0, 1), (1, 0))
    r2 = by_core(own, (0, -1), (0, 1))
    r3 = by_core(own, (-1, 0), (0, -1))
    zr1, zl1 = along_z(t0, 1), along_z(t0, -1)
    r4 = by_core(r1, (1, 0), (0, -1))
    r5 = by_core(r2, (-1, 0), (-1, 0))
    zr2, zl2 = along_z(zr1, 1), along_z(zl1, -1)
    r6 = by_core(jnp.where(is_in, r1[:1], r2[:1]), (0, 1), (0, 1))
    r7 = by_core(jnp.where(is_in, r2[1:], r3[1:]), (0, -1), (0, -1))
    zr3, zl3 = along_z(zr2, 1), along_z(zl2, -1)
    r8 = by_core(r6, (1, 0), (1, 0))
    r9 = by_core(r7, (-1, 0), (-1, 0))
    zr4, zl4 = along_z(zr3[:128], 1), along_z(zl3[128:], -1)
    pieces = (own, r1, r2, r3, r4, r5, r6, r7, r8, r9)
    token_pieces = (t0, zr1, zr2, zr3, zl1, zl2, zl3, zr4, zl4)

    *fwd0, tok = forward(0, meta, token_pieces, pieces)
    fwd1 = forward(1, meta, (tok,), pieces)
    grads, kern, pgrads = [], (), []
    for half, (pre, out, top, bot, _) in enumerate((fwd0, fwd1)):
        got = to_partner(out)
        up, down = to_next_chip(bot, 1), to_next_chip(top, -1)
        g0, g1, g3, g2a, g2b, pgrad, kern_now = backward(
            half, meta, tok, got, out, up, down, pre, mix_kernel, kern
        )
        kern = (kern_now,)
        pgrads.append(pgrad)
        ra, rb = first(g2a, 1), first(g2b, -1)
        g1, g3 = local(
            relay_kernel, "relay", [((HALF, 20, 16, BS), BF16)] * 2, (meta, g1, g3, ra, rb)
        )
        grads += [g0, first(g1, 1), first(g3, -1)]

    keep, send = token_grad(meta, *pgrads, fwd0[4], fwd1[4])
    parts = local(
        spread_kernel, "spread", [((2, 128, BS), BF16)] * NZ, (meta, keep, to_partner(send))
    )
    parts = [parts[0]] + [along_z(parts[d], d) for d in range(1, NZ)]
    (grad_tokens,) = local(gather_sum_kernel, "gathersum", [((128, 512), BF16)], (meta, *parts))

    kern = kern[0]
    kerns = (kern, first(kern, 1), first(kern, -1), first(kern, 2))
    h = local(
        first_sum_kernel,
        "firstsum",
        [((2 * HALF, NNZ + 1, 16, BS), BF16)] * 4,
        (meta, *grads, *kerns),
    )
    last = (h[0], second(h[1], 1), second(h[3], -1), second(h[2], 2))
    shape = ((2 * HALF, NNZ + 2, 8, BS), BF16)
    kept, sent = local(second_sum_kernel, "secondsum", [shape] * 2, (meta, *last))
    out_shape = ((8, NNZ, 8, BS), F32)
    win, wout, kern = local(
        place_kernel,
        "place",
        [out_shape, out_shape, ((9, 8 * BS), F32)],
        (meta, kept, to_partner(sent)),
    )
    grad_tokens = grad_tokens.reshape(1, 2, PW, 512)
    return grad_tokens, win.transpose(0, 2, 1, 3), wout.transpose(0, 2, 1, 3), kern


def solution(mesh):
    placed = (
        P("crop", "rows", None, "hid"),
        P("crop", "rows", None, "hid"),
        P("rows", "hid", None, None),
        P("rows", "hid", None, None),
        P(None, "hid"),
        P("hid", None),
    )
    return jax.shard_map(
        on_device,
        mesh=mesh,
        in_specs=placed,
        out_specs=(
            P("crop", "rows", None, "hid"),
            P(("crop", "rows"), "hid", None, None),
            P(("crop", "rows"), "hid", None, None),
            P(None, "hid"),
        ),
        check_vma=False,
    )
```

```python
import jax
import jax.numpy as jnp
from jax import lax
from jax.experimental import pallas as pl
from jax.experimental.pallas import tpu as pltpu
from jax.sharding import PartitionSpec as P

root_two_pi = 0.7978845608
cubic_coef = 0.044715
loss_scale = 0.03125

F32, BF16 = jnp.float32, jnp.bfloat16
NX, NY, NZ = 4, 4, 8
COLS, NNZ, BS, PW = 8, 5, 256, 64
TOK, KERN = 256, 20
CORE, XPOS, YPOS, YLO, ZPOS = 40, 41, 42, 43, 44
ANY = pl.BlockSpec(memory_space=pl.ANY)
VMEM = pl.BlockSpec(memory_space=pltpu.VMEM)
SMEM = pl.BlockSpec(memory_space=pltpu.SMEM)


def by_core(value, step0, step1):
    pairs = []
    for y in range(NY):
        for x in range(NX):
            for c, (dy, dx) in enumerate((step0, step1)):
                target = (y + dy) % NY * 8 + (x + dx) % NX * 2 + c
                pairs.append((y * 8 + x * 2 + c, target))
    return lax.ppermute(value, ("crop", "rows"), pairs)


def first(value, step):
    return by_core(value, (step, 0), (0, step))


def second(value, step):
    return by_core(value, (0, step), (step, 0))


def to_partner(value):
    return lax.ppermute(value, "rows", [(r, r ^ 1) for r in range(16)])


def to_next_chip(value, step):
    pairs = []
    for q in range(8):
        if 0 <= q + step < 8:
            pairs += [(q * 2 + c, (q + step) * 2 + 1 - c) for c in range(2)]
    return lax.ppermute(value, "rows", pairs)


def along_z(value, step):
    return lax.ppermute(value, "hid", [(z, (z + step) % NZ) for z in range(NZ)])


def dot(a, b, dims):
    return lax.dot_general(a, b, (dims, ((), ())), preferred_element_type=F32)


def local(kernel, name, outs, args, scratch=(), flops=2**20, hbm=()):
    shapes = [jax.ShapeDtypeStruct(s, t) for s, t in outs]
    size = sum(a.size * a.dtype.itemsize for a in args[1:])
    return pl.pallas_call(
        kernel,
        out_shape=shapes,
        in_specs=[SMEM] + [ANY if i in hbm else VMEM for i in range(1, len(args))],
        out_specs=[VMEM] * len(outs),
        scratch_shapes=list(scratch),
        compiler_params=pltpu.CompilerParams(vmem_limit_bytes=28 * 2**20),
        cost_estimate=pl.CostEstimate(flops=flops, transcendentals=0, bytes_accessed=size),
        name=name,
    )(*args)


def lanes(c):
    return pl.ds(pl.multiple_of(c * BS, BS), BS)


def start_tokens(meta, pieces, buf, sem):
    z = meta[ZPOS]
    own, r1, r2, r3, l1, l2, l3, r4, l4 = pieces
    plan = [(own, 0, 0), (r1, 7, 0), (r2, 6, 0), (r3, 5, 0), (l1, 1, 0), (l2, 2, 0), (l3, 3, 0)]
    for src, d, at in plan + [(r4, 4, 0), (l4, 4, 128)]:
        h = (z + d) % NZ
        for part in range(2):
            rows = pl.ds(at, src.shape[0])
            target = buf.at[2 * h + part, rows]
            pltpu.make_async_copy(src.at[:, pl.ds(part * BS, BS)], target, sem).start()


def weight_plan(meta, pieces):
    core, x, ylo = meta[CORE], meta[XPOS], meta[YLO]
    own, r1, r2, r3, r4, r5, r6, r7, r8, r9 = pieces
    here, there = ylo * NX, (1 - ylo) * NX
    at = lambda base, d: base + (x + d) % NX
    pick = lambda a, b: jnp.where(core == 0, a, b)
    slots = [
        (own, at(here, 0)),
        (r1, pick(at(here, 3), at(there, 0))),
        (r2, pick(at(here, 1), at(here, 3))),
        (r3, pick(at(there, 0), at(here, 1))),
        (r4, pick(at(there, 3), at(there, 1))),
        (r5, pick(at(there, 1), at(there, 3))),
    ]
    plan = [(src, s, 2 * j + s) for src, j in slots for s in range(2)]
    for j, a, b in ((at(here, 2), r6, r7), (at(there, 2), r8, r9)):
        plan += [(a, 0, 2 * j), (b, 0, 2 * j + 1)]
    return plan


def forward_kernel(meta, *refs):
    tokens, pieces, outs = refs[:9], refs[9:19], refs[19:]
    pre, out, top, bot, wts, tok, sem = outs
    start_tokens(meta, tokens, tok, sem)
    plan = weight_plan(meta, pieces)
    core = meta[CORE]

    @pl.loop(0, COLS)
    def _(c):
        for k in range(NNZ):
            for src, row, slot in plan:
                wts[c, k, slot] = src[row, c, k]

    pltpu.make_async_copy(tok, tok, sem).wait()

    def total(c, dims):
        acc = None
        for k in range(NNZ):
            part = dot(tok[meta[c * NNZ + k]], wts[c, k].reshape(BS, BS), dims)
            acc = part if acc is None else acc + part
        return acc

    @pl.when(core == 0)
    def _():
        @pl.loop(0, COLS)
        def _(c):
            p = total(c, ((1,), (0,)))
            pre[:, lanes(c)] = p
            t = jnp.tanh(root_two_pi * (p + cubic_coef * p * p * p))
            out[:, lanes(c)] = (0.5 * p * (1.0 + t)).astype(BF16)

    @pl.when(core != 0)
    def _():
        @pl.loop(0, COLS)
        def _(c):
            out[:, lanes(c)] = total(c, ((1,), (1,))).astype(BF16)

    top[...] = out[:PW]
    bot[...] = out[TOK - PW :]


def forward(meta, tokens, pieces):
    wide = COLS * BS
    outs = [((TOK, wide), F32), ((TOK, wide), BF16), ((PW, wide), BF16), ((PW, wide), BF16)]
    outs += [((COLS, NNZ, 16, 16, BS), BF16), ((16, TOK, BS), BF16)]
    return local(
        forward_kernel,
        "forward",
        outs,
        (meta, *tokens, *pieces),
        [pltpu.SemaphoreType.DMA],
        flops=2 * TOK * BS * BS * NNZ * COLS,
        hbm=range(1, 10),
    )


def shifted_rows(mid, up, down, cols):
    cells = lax.broadcasted_iota(jnp.int32, (PW, BS), 0)
    out = []
    for row in [up[:, cols]] + [mid[i * PW : (i + 1) * PW, cols] for i in range(4)] + [down[:, cols]]:
        row = row.astype(F32)
        left = jnp.where(cells == 0, 0.0, pltpu.roll(row, 1, 0))
        right = jnp.where(cells == PW - 1, 0.0, pltpu.roll(row, PW - 1, 0))
        out.append((left, row, right))
    return out


def backward_kernel(meta, tok, got, mine, up, down, pre, taps, *refs):
    g0, g1, g3, g2a, g2b, pgrad, conv, lhs, res, slab, moved = refs
    core, x, y = meta[CORE], meta[XPOS], meta[YPOS]
    is_in = core == 0
    slab[...] = jnp.zeros_like(slab)
    here = jnp.where(is_in, y, x)
    far = jnp.where(is_in, NX, 1)
    near = jnp.where(is_in, 1, NY)

    @pl.loop(0, COLS)
    def _(c):
        cols = lanes(c)
        for i, rows in enumerate(shifted_rows(got, up, down, cols)):
            for b in range(3):
                moved[3 * i + b] = rows[b]
        tap = [jnp.where(is_in, taps[8 - j : 9 - j, cols], taps[j : j + 1, cols]) for j in range(9)]
        for i in range(4):
            acc = jnp.zeros((PW, BS), F32)
            for a in range(3):
                for b in range(3):
                    acc += tap[3 * a + b] * moved[3 * (i + a) + b]
            conv[i * PW : (i + 1) * PW] = acc

        @pl.when(is_in)
        def _():
            p = pre[:, cols]
            t = jnp.tanh(root_two_pi * (p + cubic_coef * p * p * p))
            slope = 0.5 * (1.0 + t) + 0.5 * p * (1.0 - t * t) * root_two_pi * (
                1.0 + 3.0 * cubic_coef * p * p
            )
            lhs[...] = (conv[...] * slope).astype(BF16)
            pgrad[:, cols] = lhs[...]
            for k in range(NNZ):
                part = dot(tok[meta[c * NNZ + k]], lhs[...], ((0,), (0,))) * loss_scale
                res[k] = part.astype(BF16).reshape(16, 16, BS)

        @pl.when(core != 0)
        def _():
            lhs[...] = conv[...].astype(BF16)
            for k in range(NNZ):
                part = dot(lhs[...], tok[meta[c * NNZ + k]], ((0,), (0,))) * loss_scale
                res[k] = part.astype(BF16).reshape(16, 16, BS)
            sums = []
            for a in range(3):
                for b in range(3):
                    acc = jnp.zeros((PW, BS), F32)
                    for i in range(4):
                        acc += moved[3 * (i + a) + b] * mine[i * PW : (i + 1) * PW, cols].astype(F32)
                    sums.append(jnp.sum(acc, axis=0, keepdims=True))
            rows = jnp.concatenate(sums + [jnp.zeros((7, BS), F32)], axis=0) * loss_scale
            slab[...] = rows.astype(BF16)

        def emit(out, d, at):
            start = (here + d) % 4 * far
            for k in range(NNZ):
                for s in range(4):
                    out[at, k * 4 + s] = res[k, start + s * near]
            out[at, KERN] = slab[...]

        emit(g0, 0, c)
        emit(g1, 1, c)
        emit(g3, 3, c)

        @pl.when(c < COLS // 2)
        def _():
            emit(g2a, 2, c)

        @pl.when(c >= COLS // 2)
        def _():
            emit(g2b, 2, c - COLS // 2)


def backward(meta, tok, got, mine, up, down, pre, taps):
    full, part = (COLS, KERN + 1, 16, BS), (COLS // 2, KERN + 1, 16, BS)
    outs = [(full, BF16)] * 3 + [(part, BF16)] * 2 + [((TOK, COLS * BS), BF16)]
    scratch = [
        pltpu.VMEM((TOK, BS), F32),
        pltpu.VMEM((TOK, BS), BF16),
        pltpu.VMEM((NNZ, 16, 16, BS), BF16),
        pltpu.VMEM((16, BS), BF16),
        pltpu.VMEM((18, PW, BS), F32),
    ]
    args = (meta, tok, got, mine, up, down, pre, taps)
    return local(
        backward_kernel, "backward", outs, args, scratch, flops=2 * TOK * BS * BS * NNZ * COLS
    )


def token_grad_kernel(meta, pgrad, wts, keep, send, acc):
    @pl.when(meta[CORE] == 0)
    def _():
        acc[...] = jnp.zeros_like(acc)

        @pl.loop(0, COLS)
        def _(c):
            for k in range(NNZ):
                wt = wts[c, k].reshape(BS, BS)
                acc[meta[c * NNZ + k]] += dot(pgrad[:, lanes(c)], wt, ((1,), (1,)))

        @pl.loop(0, 16)
        def _(r):
            keep[r] = acc[r, :128].astype(BF16)
            send[r] = acc[r, 128:].astype(BF16)


def token_grad(meta, pgrad, wts):
    return local(
        token_grad_kernel,
        "tokengrad",
        [((16, 128, BS), BF16)] * 2,
        (meta, pgrad, wts),
        [pltpu.VMEM((16, TOK, BS), F32)],
        flops=2 * TOK * BS * BS * NNZ * COLS,
    )


def gather_sum_kernel(meta, parts, out):
    for b in range(2):
        total = parts[b].astype(F32)
        for z in range(1, NZ):
            total += parts[2 * z + b].astype(F32)
        out[:, b * BS : (b + 1) * BS] = total.astype(BF16)


def relay_kernel(meta, g1, g3, ra, rb, o1, o3):
    for out, own, got, first_half in ((o1, g1, ra, 0), (o3, g3, rb, COLS // 2)):

        @pl.loop(0, COLS // 2)
        def _(c):
            at, other = c + first_half, c + COLS // 2 - first_half
            for k in range(KERN):
                out[at, k] = (own[at, k].astype(F32) + got[c, k].astype(F32)).astype(BF16)
                out[other, k] = own[other, k]
            out[at, KERN] = own[at, KERN]
            out[other, KERN] = own[other, KERN]
            out[at, KERN + 1] = got[c, KERN]
            out[other, KERN + 1] = own[other, KERN]


def relay(meta, g1, g3, ra, rb):
    shape = ((COLS, KERN + 2, 16, BS), BF16)
    return local(relay_kernel, "relay", [shape] * 2, (meta, g1, g3, ra, rb))


def first_sum_kernel(meta, own, prev, nxt, *outs):
    here = jnp.where(meta[CORE] == 0, meta[XPOS], meta[YPOS])

    @pl.loop(0, COLS)
    def _(c):
        far = jnp.where(c < COLS // 2, prev[c, KERN + 1], nxt[c, KERN + 1]).astype(F32)
        near = prev[c, KERN].astype(F32) + nxt[c, KERN].astype(F32)
        slab = ((own[c, KERN].astype(F32) + far) + near).astype(BF16)
        for d in range(4):
            s = (here + d) % 4
            for k in range(NNZ):
                at = k * 4 + s
                total = own[c, at].astype(F32) + prev[c, at].astype(F32) + nxt[c, at].astype(F32)
                outs[d][c, k] = total.astype(BF16)
            outs[d][c, NNZ] = slab


def second_sum_kernel(meta, own, prev, nxt, far, keep, send):
    first_core = meta[CORE] == 0

    @pl.loop(0, COLS)
    def _(c):
        for k in range(NNZ + 1):
            a, b, e, f = (r[c, k].astype(F32) for r in (own, prev, nxt, far))
            total = ((a + f) + (b + e)).astype(BF16)
            low, high = total[:8], total[8:]
            if k < NNZ:
                keep[c, k] = jnp.where(first_core, low, high)
                send[c, k] = jnp.where(first_core, high, low)
            else:
                for out in (keep, send):
                    out[c, NNZ] = low
                    out[c, NNZ + 1] = high


def place_kernel(meta, keep, got, win, wout, kern):
    is_in = meta[CORE] == 0

    @pl.loop(0, NNZ)
    def _(k):
        mine = jnp.stack([keep[c, k].astype(F32) for c in range(COLS)], axis=0)
        its = jnp.stack([got[c, k].astype(F32) for c in range(COLS)], axis=0)
        mine, its = jnp.swapaxes(mine, 0, 1), jnp.swapaxes(its, 0, 1)
        win[:, k] = jnp.where(is_in, mine, its)
        wout[:, k] = jnp.where(is_in, its, mine)

    for c in range(COLS):
        rows = [jnp.where(is_in, got[c, NNZ + i], keep[c, NNZ + i]).astype(F32) for i in range(2)]
        kern[:, c * BS : (c + 1) * BS] = jnp.concatenate(rows, axis=0)[:9]


def on_device(tokens, cotangent, weight_in, weight_out, mix_kernel, block_rows):
    row, crop, z = lax.axis_index("rows"), lax.axis_index("crop"), lax.axis_index("hid")
    core, x, ylo = row % 2, row // 2 % NX, row // 8
    place = jnp.stack([core, x, crop * 2 + ylo, ylo, z]).astype(jnp.int32)
    meta = jnp.concatenate([block_rows.reshape(-1), place])
    is_in = core == 0

    def side(a, b):
        mine, theirs = jnp.where(is_in, a, b), jnp.where(is_in, b, a)
        got = to_partner(theirs)
        return jnp.where(is_in, mine, got), jnp.where(is_in, got, mine)

    own = jnp.stack(side(*(w.transpose(1, 2, 0, 3) for w in (weight_in, weight_out))))
    t0 = jnp.concatenate(side(tokens.reshape(128, 512), cotangent.reshape(128, 512)))

    r1 = by_core(own, (0, 1), (1, 0))
    r2 = by_core(own, (0, -1), (0, 1))
    r3 = by_core(own, (-1, 0), (0, -1))
    zr1, zl1 = along_z(t0, 1), along_z(t0, -1)
    r4 = by_core(r1, (1, 0), (0, -1))
    r5 = by_core(r2, (-1, 0), (-1, 0))
    zr2, zl2 = along_z(zr1, 1), along_z(zl1, -1)
    r6 = by_core(jnp.where(is_in, r1[:1], r2[:1]), (0, 1), (0, 1))
    r7 = by_core(jnp.where(is_in, r2[1:], r3[1:]), (0, -1), (0, -1))
    zr3, zl3 = along_z(zr2, 1), along_z(zl2, -1)
    r8 = by_core(r6, (1, 0), (1, 0))
    r9 = by_core(r7, (-1, 0), (-1, 0))
    zr4, zl4 = along_z(zr3[:128], 1), along_z(zl3[128:], -1)
    pieces = (own, r1, r2, r3, r4, r5, r6, r7, r8, r9)
    token_pieces = (t0, zr1, zr2, zr3, zl1, zl2, zl3, zr4, zl4)

    pre, out, top, bot, wts, tok = forward(meta, token_pieces, pieces)
    got = to_partner(out)
    up, down = to_next_chip(bot, 1), to_next_chip(top, -1)
    g0, g1, g3, g2a, g2b, pgrad = backward(meta, tok, got, out, up, down, pre, mix_kernel)
    ra, rb = first(g2a, 1), first(g2b, -1)

    keep, send = token_grad(meta, pgrad, wts)
    terms = jnp.where(is_in, keep, to_partner(send))
    terms = lax.all_to_all(terms, "hid", 0, 0, tiled=True)
    (grad_tokens,) = local(gather_sum_kernel, "gathersum", [((128, 512), BF16)], (meta, terms))

    g1, g3 = relay(meta, g1, g3, ra, rb)
    h = local(
        first_sum_kernel,
        "firstsum",
        [((COLS, NNZ + 1, 16, BS), BF16)] * 4,
        (meta, g0, first(g1, 1), first(g3, -1)),
    )
    last = (h[0], second(h[1], 1), second(h[3], -1), second(h[2], 2))
    shape = ((COLS, NNZ + 2, 8, BS), BF16)
    kept, sent = local(second_sum_kernel, "secondsum", [shape] * 2, (meta, *last))
    out_shape = ((8, NNZ, 8, BS), F32)
    win, wout, kern = local(
        place_kernel,
        "place",
        [out_shape, out_shape, ((9, 8 * BS), F32)],
        (meta, kept, to_partner(sent)),
    )
    grad_tokens = grad_tokens.reshape(1, 2, PW, 512)
    return grad_tokens, win.transpose(0, 2, 1, 3), wout.transpose(0, 2, 1, 3), kern


def solution(mesh):
    placed = (
        P("crop", "rows", None, "hid"),
        P("crop", "rows", None, "hid"),
        P("rows", "hid", None, None),
        P("rows", "hid", None, None),
        P(None, "hid"),
        P("hid", None),
    )
    return jax.shard_map(
        on_device,
        mesh=mesh,
        in_specs=placed,
        out_specs=(
            P("crop", "rows", None, "hid"),
            P(("crop", "rows"), "hid", None, None),
            P(("crop", "rows"), "hid", None, None),
            P(None, "hid"),
        ),
        check_vma=False,
    )
```

```python
import jax
import jax.numpy as jnp
from jax import lax
from jax.experimental import pallas as pl
from jax.experimental.pallas import tpu as pltpu
from jax.sharding import PartitionSpec as P

root_two_pi = 0.7978845608
cubic_coef = 0.044715
loss_scale = 0.03125

F32, BF16 = jnp.float32, jnp.bfloat16
NX, NY, NZ = 4, 4, 8
COLS, NNZ, BS, PW = 8, 5, 256, 64
TOK, KERN, SPLIT = 256, 20, 4
CORE, XPOS, YPOS, YLO, ZPOS = 40, 41, 42, 43, 44
HBM = pl.BlockSpec(memory_space=pltpu.MemorySpace.HBM)
VMEM = pl.BlockSpec(memory_space=pltpu.VMEM)
SMEM = pl.BlockSpec(memory_space=pltpu.SMEM)


def by_core(value, step0, step1):
    pairs = []
    for y in range(NY):
        for x in range(NX):
            for c, (dy, dx) in enumerate((step0, step1)):
                target = (y + dy) % NY * 8 + (x + dx) % NX * 2 + c
                pairs.append((y * 8 + x * 2 + c, target))
    return lax.ppermute(value, ("crop", "rows"), pairs)


def first(value, step):
    return by_core(value, (step, 0), (0, step))


def second(value, step):
    return by_core(value, (0, step), (step, 0))


def to_partner(value):
    return lax.ppermute(value, "rows", [(r, r ^ 1) for r in range(16)])


def to_next_chip(value, step):
    pairs = []
    for q in range(8):
        if 0 <= q + step < 8:
            pairs += [(q * 2 + c, (q + step) * 2 + 1 - c) for c in range(2)]
    return lax.ppermute(value, "rows", pairs)


def along_z(value, step):
    return lax.ppermute(value, "hid", [(z, (z + step) % NZ) for z in range(NZ)])


def dot(a, b, dims):
    return lax.dot_general(a, b, (dims, ((), ())), preferred_element_type=F32)


def local(kernel, name, outs, args, scratch=(), flops=2**20, hbm=()):
    shapes = [jax.ShapeDtypeStruct(s, t) for s, t in outs]
    size = sum(a.size * a.dtype.itemsize for a in args[1:])
    return pl.pallas_call(
        kernel,
        out_shape=shapes,
        in_specs=[SMEM] + [HBM if i in hbm else VMEM for i in range(1, len(args))],
        out_specs=[VMEM] * len(outs),
        scratch_shapes=list(scratch),
        compiler_params=pltpu.CompilerParams(vmem_limit_bytes=14 * 2**20),
        cost_estimate=pl.CostEstimate(flops=flops, transcendentals=0, bytes_accessed=size),
        name=name,
    )(*args)


def lanes(c):
    return pl.ds(pl.multiple_of(c * BS, BS), BS)


def start_tokens(meta, pieces, buf, sem):
    z = meta[ZPOS]
    own, r1, r2, r3, l1, l2, l3, r4, l4 = pieces
    plan = [(own, 0, 0), (r1, 7, 0), (r2, 6, 0), (r3, 5, 0), (l1, 1, 0), (l2, 2, 0), (l3, 3, 0)]
    for src, d, at in plan + [(r4, 4, 0), (l4, 4, 128)]:
        h = (z + d) % NZ
        for part in range(2):
            rows = pl.ds(at, src.shape[0])
            target = buf.at[2 * h + part, rows]
            pltpu.make_async_copy(src.at[:, pl.ds(part * BS, BS)], target, sem).start()


def weight_plan(meta, pieces):
    core, x, ylo = meta[CORE], meta[XPOS], meta[YLO]
    own, a, b, c, d, e, f, g, h, i = pieces
    here, there = ylo * NX, (1 - ylo) * NX
    side = jnp.where(core == 0, NX - 1, 1)
    at = lambda base, step: base + (x + step) % NX
    slots = [
        (own, at(here, 0)),
        (a, at(here, side)),
        (b, at(there, 0)),
        (c, at(here, NX - side)),
        (d, at(there, side)),
        (e, at(there, NX - side)),
    ]
    plan = [(src, s, 2 * j + s) for src, j in slots for s in range(2)]
    for j, low, high in ((at(here, 2), f, g), (at(there, 2), h, i)):
        plan += [(low, 0, 2 * j), (high, 0, 2 * j + 1)]
    return plan


def hold(meta, value, *others):
    def kernel(meta, src, *refs):
        refs[-1][...] = src[...]

    outs = [(value.shape, value.dtype)]
    return local(kernel, "hold", outs, (meta, value, *others))[0]


def cut_kernel(meta, a, c, *refs):
    low, high = refs[-2:]
    low[...] = a[:1]
    high[...] = c[1:]


def forward_kernel(meta, *refs):
    tokens, pieces, outs = refs[:9], refs[9:19], refs[19:]
    pre, out, top, bot, wts, tok, sem = outs
    start_tokens(meta, tokens, tok, sem)
    plan = weight_plan(meta, pieces)
    core = meta[CORE]

    @pl.loop(0, COLS)
    def _(c):
        for k in range(NNZ):
            for src, row, slot in plan:
                wts[c, k, slot] = src[row, c, k]

    pltpu.make_async_copy(tok, tok, sem).wait()

    def total(c, dims):
        acc = None
        for k in range(NNZ):
            part = dot(tok[meta[c * NNZ + k]], wts[c, k].reshape(BS, BS), dims)
            acc = part if acc is None else acc + part
        return acc

    @pl.when(core == 0)
    def _():
        @pl.loop(0, COLS)
        def _(c):
            p = total(c, ((1,), (0,)))
            pre[:, lanes(c)] = p
            t = jnp.tanh(root_two_pi * (p + cubic_coef * p * p * p))
            out[:, lanes(c)] = (0.5 * p * (1.0 + t)).astype(BF16)

    @pl.when(core != 0)
    def _():
        @pl.loop(0, COLS)
        def _(c):
            out[:, lanes(c)] = total(c, ((1,), (1,))).astype(BF16)

    top[...] = out[:PW]
    bot[...] = out[TOK - PW :]


def forward(meta, tokens, pieces):
    wide = COLS * BS
    outs = [((TOK, wide), F32), ((TOK, wide), BF16), ((PW, wide), BF16), ((PW, wide), BF16)]
    outs += [((COLS, NNZ, 16, 16, BS), BF16), ((16, TOK, BS), BF16)]
    return local(
        forward_kernel,
        "forward",
        outs,
        (meta, *tokens, *pieces),
        [pltpu.SemaphoreType.DMA],
        flops=2 * TOK * BS * BS * NNZ * COLS,
        hbm=range(1, 10),
    )


def shifted_rows(mid, up, down, cols):
    cells = lax.broadcasted_iota(jnp.int32, (PW, BS), 0)
    out = []
    for row in [up[:, cols]] + [mid[i * PW : (i + 1) * PW, cols] for i in range(4)] + [down[:, cols]]:
        row = row.astype(F32)
        left = jnp.where(cells == 0, 0.0, pltpu.roll(row, 1, 0))
        right = jnp.where(cells == PW - 1, 0.0, pltpu.roll(row, PW - 1, 0))
        out.append((left, row, right))
    return out


def backward_kernel(meta, tok, got, mine, up, down, pre, taps, *refs):
    g0, m1, m3, g1, g3, pgrad, conv, lhs, res, slab, moved = refs
    core, x, y = meta[CORE], meta[XPOS], meta[YPOS]
    is_in = core == 0
    slab[...] = jnp.zeros_like(slab)
    here = jnp.where(is_in, y, x)
    far = jnp.where(is_in, NX, 1)
    near = jnp.where(is_in, 1, NY)

    @pl.loop(0, COLS)
    def _(c):
        cols = lanes(c)
        for i, rows in enumerate(shifted_rows(got, up, down, cols)):
            for b in range(3):
                moved[3 * i + b] = rows[b]
        tap = [jnp.where(is_in, taps[8 - j : 9 - j, cols], taps[j : j + 1, cols]) for j in range(9)]
        for i in range(4):
            acc = jnp.zeros((PW, BS), F32)
            for a in range(3):
                for b in range(3):
                    acc += tap[3 * a + b] * moved[3 * (i + a) + b]
            conv[i * PW : (i + 1) * PW] = acc

        @pl.when(is_in)
        def _():
            p = pre[:, cols]
            t = jnp.tanh(root_two_pi * (p + cubic_coef * p * p * p))
            slope = 0.5 * (1.0 + t) + 0.5 * p * (1.0 - t * t) * root_two_pi * (
                1.0 + 3.0 * cubic_coef * p * p
            )
            lhs[...] = (conv[...] * slope).astype(BF16)
            pgrad[:, cols] = lhs[...]
            for k in range(NNZ):
                part = dot(tok[meta[c * NNZ + k]], lhs[...], ((0,), (0,))) * loss_scale
                res[k] = part.astype(BF16).reshape(16, 16, BS)

        @pl.when(core != 0)
        def _():
            lhs[...] = conv[...].astype(BF16)
            for k in range(NNZ):
                part = dot(lhs[...], tok[meta[c * NNZ + k]], ((0,), (0,))) * loss_scale
                res[k] = part.astype(BF16).reshape(16, 16, BS)
            sums = []
            for a in range(3):
                for b in range(3):
                    acc = jnp.zeros((PW, BS), F32)
                    for i in range(4):
                        acc += moved[3 * (i + a) + b] * mine[i * PW : (i + 1) * PW, cols].astype(F32)
                    sums.append(jnp.sum(acc, axis=0, keepdims=True))
            rows = jnp.concatenate(sums + [jnp.zeros((7, BS), F32)], axis=0) * loss_scale
            slab[...] = rows.astype(BF16)

        def emit(out, d, at):
            start = (here + d) % 4 * far
            for k in range(NNZ):
                for s in range(4):
                    out[at, k * 4 + s] = res[k, start + s * near]
            out[at, KERN] = slab[...]

        emit(g0, 0, c)

        @pl.when(c < SPLIT)
        def _():
            emit(m1, 2, c)
            emit(g1, 1, c)
            emit(m3, 3, c + SPLIT)

        @pl.when(c >= SPLIT)
        def _():
            emit(m3, 2, c - SPLIT)
            emit(m1, 1, c)
            emit(g3, 3, c - SPLIT)


def backward(meta, tok, got, mine, up, down, pre, taps):
    full, part = (COLS, KERN + 1, 16, BS), (SPLIT, KERN + 1, 16, BS)
    outs = [(full, BF16)] * 3 + [(part, BF16)] * 2 + [((TOK, COLS * BS), BF16)]
    scratch = [
        pltpu.VMEM((TOK, BS), F32),
        pltpu.VMEM((TOK, BS), BF16),
        pltpu.VMEM((NNZ, 16, 16, BS), BF16),
        pltpu.VMEM((16, BS), BF16),
        pltpu.VMEM((18, PW, BS), F32),
    ]
    args = (meta, tok, got, mine, up, down, pre, taps)
    return local(
        backward_kernel, "backward", outs, args, scratch, flops=2 * TOK * BS * BS * NNZ * COLS
    )


def token_grad_kernel(meta, pgrad, wts, keep, send, acc):
    @pl.when(meta[CORE] == 0)
    def _():
        acc[...] = jnp.zeros_like(acc)

        @pl.loop(0, COLS)
        def _(c):
            for k in range(NNZ):
                wt = wts[c, k].reshape(BS, BS)
                acc[meta[c * NNZ + k]] += dot(pgrad[:, lanes(c)], wt, ((1,), (1,)))

        @pl.loop(0, 16)
        def _(r):
            keep[r] = acc[r, :128].astype(BF16)
            send[r] = acc[r, 128:].astype(BF16)


def token_grad(meta, pgrad, wts):
    return local(
        token_grad_kernel,
        "tokengrad",
        [((16, 128, BS), BF16)] * 2,
        (meta, pgrad, wts),
        [pltpu.VMEM((16, TOK, BS), F32)],
        flops=2 * TOK * BS * BS * NNZ * COLS,
    )


def gather_sum_kernel(meta, parts, out):
    for b in range(2):
        total = parts[b].astype(F32)
        for z in range(1, NZ):
            total += parts[2 * z + b].astype(F32)
        out[:, b * BS : (b + 1) * BS] = total.astype(BF16)


def relay_kernel(meta, g1, g3, m1, m3, _, o1, o3):
    for out, own, got in ((o1, g1, m1), (o3, g3, m3)):

        @pl.loop(0, SPLIT)
        def _(c):
            for k in range(KERN):
                out[c, k] = (own[c, k].astype(F32) + got[c, k].astype(F32)).astype(BF16)
            out[c, KERN] = own[c, KERN]
            out[c, KERN + 1] = got[c, KERN]


def first_sum_kernel(meta, own, m1, m3, p1, p3, *outs):
    here = jnp.where(meta[CORE] == 0, meta[XPOS], meta[YPOS])

    for shift, relayed, direct in ((0, p1, m3), (SPLIT, p3, m1)):

        @pl.loop(0, SPLIT)
        def _(c):
            at, got = c + shift, c + SPLIT
            near = relayed[c, KERN].astype(F32) + direct[got, KERN].astype(F32)
            far = own[at, KERN].astype(F32) + relayed[c, KERN + 1].astype(F32)
            for d in range(4):
                s = (here + d) % 4
                for k in range(NNZ):
                    total = own[at, k * 4 + s].astype(F32) + relayed[c, k * 4 + s].astype(F32)
                    outs[d][at, k] = (total + direct[got, k * 4 + s].astype(F32)).astype(BF16)
                outs[d][at, NNZ] = (far + near).astype(BF16)


def second_sum_kernel(meta, own, prev, nxt, far, keep, send):
    first_core = meta[CORE] == 0

    @pl.loop(0, COLS)
    def _(c):
        for k in range(NNZ + 1):
            a, b, e, f = (r[c, k].astype(F32) for r in (own, prev, nxt, far))
            total = ((a + f) + (b + e)).astype(BF16)
            low, high = total[:8], total[8:]
            if k < NNZ:
                keep[c, k] = jnp.where(first_core, low, high)
                send[c, k] = jnp.where(first_core, high, low)
            else:
                for out in (keep, send):
                    out[c, NNZ] = low
                    out[c, NNZ + 1] = high


def place_kernel(meta, keep, got, _, win, wout, kern):
    is_in = meta[CORE] == 0

    @pl.loop(0, NNZ)
    def _(k):
        mine = jnp.stack([keep[c, k].astype(F32) for c in range(COLS)], axis=0)
        its = jnp.stack([got[c, k].astype(F32) for c in range(COLS)], axis=0)
        mine, its = jnp.swapaxes(mine, 0, 1), jnp.swapaxes(its, 0, 1)
        win[:, k] = jnp.where(is_in, mine, its)
        wout[:, k] = jnp.where(is_in, its, mine)

    for c in range(COLS):
        rows = [jnp.where(is_in, got[c, NNZ + i], keep[c, NNZ + i]).astype(F32) for i in range(2)]
        kern[:, c * BS : (c + 1) * BS] = jnp.concatenate(rows, axis=0)[:9]


def on_device(tokens, cotangent, weight_in, weight_out, mix_kernel, block_rows):
    row, crop, z = lax.axis_index("rows"), lax.axis_index("crop"), lax.axis_index("hid")
    core, x, ylo = row % 2, row // 2 % NX, row // 8
    place = jnp.stack([core, x, crop * 2 + ylo, ylo, z]).astype(jnp.int32)
    meta = jnp.concatenate([block_rows.reshape(-1), place])
    is_in = core == 0

    def side(a, b):
        mine, theirs = jnp.where(is_in, a, b), jnp.where(is_in, b, a)
        got = to_partner(theirs)
        return jnp.where(is_in, mine, got), jnp.where(is_in, got, mine)

    own = jnp.stack(side(*(w.transpose(1, 2, 0, 3) for w in (weight_in, weight_out))))
    t0 = jnp.concatenate(side(tokens.reshape(128, 512), cotangent.reshape(128, 512)))

    wa = by_core(own, (0, 1), (0, -1))
    wb = by_core(own, (-1, 0), (1, 0))
    zr1, zl1 = along_z(t0, 1), along_z(t0, -1)
    wc = by_core(hold(meta, own, wa, wb, zr1, zl1), (0, -1), (0, 1))
    wd = by_core(wa, (1, 0), (-1, 0))
    zr2, zl2 = along_z(zr1, 1), along_z(zl1, -1)
    cuts = [((1, *own.shape[1:]), BF16)] * 2
    low, high = local(cut_kernel, "cut", cuts, (meta, wa, wc, wd, zr2, zl2))
    wf = by_core(low, (0, 1), (0, -1))
    wg = by_core(high, (0, -1), (0, 1))
    we = by_core(wc, (-1, 0), (1, 0))
    zr3, zl3 = along_z(zr2, 1), along_z(zl2, -1)
    wh = by_core(wf, (1, 0), (-1, 0))
    wi = by_core(wg, (-1, 0), (1, 0))
    zr4, zl4 = along_z(zr3[:128], 1), along_z(zl3[128:], -1)
    pieces = (own, wa, wb, wc, wd, we, wf, wg, wh, wi)
    token_pieces = (t0, zr1, zr2, zr3, zl1, zl2, zl3, zr4, zl4)

    pre, out, top, bot, wts, tok = forward(meta, token_pieces, pieces)
    got = to_partner(out)
    up, down = to_next_chip(bot, 1), to_next_chip(top, -1)
    g0, m1, m3, g1, g3, pgrad = backward(meta, tok, got, out, up, down, pre, mix_kernel)
    m1, m3 = first(m1, 1), first(m3, -1)

    keep, send = token_grad(meta, pgrad, wts)
    terms = jnp.where(is_in, keep, to_partner(send))
    relayed = [((SPLIT, KERN + 2, 16, BS), BF16)] * 2
    r1, r3 = local(relay_kernel, "relay", relayed, (meta, g1, g3, m1, m3, terms), hbm=(5,))
    terms = lax.all_to_all(terms, "hid", 0, 0, tiled=True)
    (grad_tokens,) = local(gather_sum_kernel, "gathersum", [((128, 512), BF16)], (meta, terms))

    h = local(
        first_sum_kernel,
        "firstsum",
        [((COLS, NNZ + 1, 16, BS), BF16)] * 4,
        (meta, g0, m1, m3, first(r1, 1), first(r3, -1)),
    )
    last = (h[0], second(h[1], 1), second(h[3], -1), second(h[2], 2))
    shape = ((COLS, NNZ + 2, 8, BS), BF16)
    kept, sent = local(second_sum_kernel, "secondsum", [shape] * 2, (meta, *last))
    out_shape = ((8, NNZ, 8, BS), F32)
    win, wout, kern = local(
        place_kernel,
        "place",
        [out_shape, out_shape, ((9, 8 * BS), F32)],
        (meta, kept, to_partner(sent), grad_tokens),
    )
    grad_tokens = grad_tokens.reshape(1, 2, PW, 512)
    return grad_tokens, win.transpose(0, 2, 1, 3), wout.transpose(0, 2, 1, 3), kern


def solution(mesh):
    placed = (
        P("crop", "rows", None, "hid"),
        P("crop", "rows", None, "hid"),
        P("rows", "hid", None, None),
        P("rows", "hid", None, None),
        P(None, "hid"),
        P("hid", None),
    )
    return jax.shard_map(
        on_device,
        mesh=mesh,
        in_specs=placed,
        out_specs=(
            P("crop", "rows", None, "hid"),
            P(("crop", "rows"), "hid", None, None),
            P(("crop", "rows"), "hid", None, None),
            P(None, "hid"),
        ),
        check_vma=False,
    )
```

```python
import functools

import jax
import jax.numpy as jnp
from jax import lax
from jax.experimental import pallas as pl
from jax.experimental.pallas import tpu as pltpu
from jax.sharding import PartitionSpec as P

root_two_pi = 0.7978845608
cubic_coef = 0.044715
loss_scale = 0.03125

F32, BF16 = jnp.float32, jnp.bfloat16
NX, NY, NZ = 4, 4, 8
COLS, NNZ, BS, PW = 8, 5, 256, 64
TOK, KERN, SPLIT = 256, 20, 4
CORE, XPOS, YPOS, YLO, ZPOS = 40, 41, 42, 43, 44
HBM = pl.BlockSpec(memory_space=pltpu.MemorySpace.HBM)
VMEM = pl.BlockSpec(memory_space=pltpu.VMEM)
SMEM = pl.BlockSpec(memory_space=pltpu.SMEM)


def by_core(value, step0, step1):
    pairs = []
    for y in range(NY):
        for x in range(NX):
            for c, (dy, dx) in enumerate((step0, step1)):
                target = (y + dy) % NY * 8 + (x + dx) % NX * 2 + c
                pairs.append((y * 8 + x * 2 + c, target))
    return lax.ppermute(value, ("crop", "rows"), pairs)


def first(value, step):
    return by_core(value, (step, 0), (0, step))


def second(value, step):
    return by_core(value, (0, step), (step, 0))


def to_partner(value):
    return lax.ppermute(value, "rows", [(r, r ^ 1) for r in range(16)])


def to_next_chip(value, step):
    pairs = []
    for q in range(8):
        if 0 <= q + step < 8:
            pairs += [(q * 2 + c, (q + step) * 2 + 1 - c) for c in range(2)]
    return lax.ppermute(value, "rows", pairs)


def along_z(value, step):
    return lax.ppermute(value, "hid", [(z, (z + step) % NZ) for z in range(NZ)])


def dot(a, b, dims):
    return lax.dot_general(a, b, (dims, ((), ())), preferred_element_type=F32)


def local(kernel, name, outs, args, scratch=(), flops=2**20, hbm=()):
    shapes = [jax.ShapeDtypeStruct(s, t) for s, t in outs]
    size = sum(a.size * a.dtype.itemsize for a in args[1:])
    return pl.pallas_call(
        kernel,
        out_shape=shapes,
        in_specs=[SMEM] + [HBM if i in hbm else VMEM for i in range(1, len(args))],
        out_specs=[VMEM] * len(outs),
        scratch_shapes=list(scratch),
        compiler_params=pltpu.CompilerParams(vmem_limit_bytes=14 * 2**20),
        cost_estimate=pl.CostEstimate(flops=flops, transcendentals=0, bytes_accessed=size),
        name=name,
    )(*args)


def lanes(c):
    return pl.ds(pl.multiple_of(c * BS, BS), BS)


def start_tokens(meta, pieces, buf, sem):
    z = meta[ZPOS]
    own, r1, r2, r3, l1, l2, l3, r4, l4 = pieces
    plan = [(own, 0, 0), (r1, 7, 0), (r2, 6, 0), (r3, 5, 0), (l1, 1, 0), (l2, 2, 0), (l3, 3, 0)]
    for src, d, at in plan + [(r4, 4, 0), (l4, 4, 128)]:
        h = (z + d) % NZ
        for part in range(2):
            rows = pl.ds(at, src.shape[0])
            target = buf.at[2 * h + part, rows]
            pltpu.make_async_copy(src.at[:, pl.ds(part * BS, BS)], target, sem).start()


def weight_plan(meta, pieces):
    core, x, ylo = meta[CORE], meta[XPOS], meta[YLO]
    own, a, b, c, d, e, f, g, h, i = pieces
    here, there = ylo * NX, (1 - ylo) * NX
    side = jnp.where(core == 0, NX - 1, 1)
    at = lambda base, step: base + (x + step) % NX
    slots = [
        (own, at(here, 0)),
        (a, at(here, side)),
        (b, at(there, 0)),
        (c, at(here, NX - side)),
        (d, at(there, side)),
        (e, at(there, NX - side)),
    ]
    plan = [(src, s, 2 * j + s) for src, j in slots for s in range(2)]
    for j, low, high in ((at(here, 2), f, g), (at(there, 2), h, i)):
        plan += [(low, 0, 2 * j), (high, 0, 2 * j + 1)]
    return plan


def hold(meta, value, *others):
    def kernel(meta, src, *refs):
        refs[-1][...] = src[...]

    outs = [(value.shape, value.dtype)]
    return local(kernel, "hold", outs, (meta, value, *others))[0]


def cut_kernel(meta, a, c, *refs):
    low, high = refs[-2:]
    low[...] = a[:1]
    high[...] = c[1:]


def forward_kernel(meta, *refs):
    tokens, pieces, outs = refs[:9], refs[9:19], refs[19:]
    pre, *halves, wts, tok, sem = outs
    rows, tops, bots = halves[:2], halves[2:4], halves[4:]
    start_tokens(meta, tokens, tok, sem)
    plan = weight_plan(meta, pieces)
    core = meta[CORE]

    @pl.loop(0, COLS)
    def _(c):
        for k in range(NNZ):
            for src, row, slot in plan:
                wts[c, k, slot] = src[row, c, k]

    pltpu.make_async_copy(tok, tok, sem).wait()

    def total(c, dims):
        acc = None
        for k in range(NNZ):
            part = dot(tok[meta[c * NNZ + k]], wts[c, k].reshape(BS, BS), dims)
            acc = part if acc is None else acc + part
        return acc

    for half, out in enumerate(rows):
        first_col = half * SPLIT

        @pl.when(core == 0)
        def _():
            @pl.loop(0, SPLIT)
            def _(c):
                p = total(c + first_col, ((1,), (0,)))
                pre[:, lanes(c + first_col)] = p
                t = jnp.tanh(root_two_pi * (p + cubic_coef * p * p * p))
                out[:, lanes(c)] = (0.5 * p * (1.0 + t)).astype(BF16)

        @pl.when(core != 0)
        def _():
            @pl.loop(0, SPLIT)
            def _(c):
                out[:, lanes(c)] = total(c + first_col, ((1,), (1,))).astype(BF16)

        tops[half][...] = out[:PW]
        bots[half][...] = out[TOK - PW :]


def forward(meta, tokens, pieces):
    wide = SPLIT * BS
    outs = [((TOK, COLS * BS), F32)] + [((TOK, wide), BF16)] * 2 + [((PW, wide), BF16)] * 4
    outs += [((COLS, NNZ, 16, 16, BS), BF16), ((16, TOK, BS), BF16)]
    return local(
        forward_kernel,
        "forward",
        outs,
        (meta, *tokens, *pieces),
        [pltpu.SemaphoreType.DMA],
        flops=2 * TOK * BS * BS * NNZ * COLS,
        hbm=range(1, 10),
    )


def shifted_rows(mid, up, down, cols):
    cells = lax.broadcasted_iota(jnp.int32, (PW, BS), 0)
    out = []
    for row in [up[:, cols]] + [mid[i * PW : (i + 1) * PW, cols] for i in range(4)] + [down[:, cols]]:
        row = row.astype(F32)
        left = jnp.where(cells == 0, 0.0, pltpu.roll(row, 1, 0))
        right = jnp.where(cells == PW - 1, 0.0, pltpu.roll(row, PW - 1, 0))
        out.append((left, row, right))
    return out


def backward_kernel(half, meta, tok, got, mine, up, down, pre, taps, *refs):
    refs = refs[-10:]
    g0, far_out, direct, through, pgrad, conv, lhs, res, slab, moved = refs
    core, x, y = meta[CORE], meta[XPOS], meta[YPOS]
    is_in = core == 0
    slab[...] = jnp.zeros_like(slab)
    here = jnp.where(is_in, y, x)
    far = jnp.where(is_in, NX, 1)
    near = jnp.where(is_in, 1, NY)

    @pl.loop(0, SPLIT)
    def _(c):
        cols = lanes(c)
        wide = lanes(c + half * SPLIT)
        first_row = (c + half * SPLIT) * NNZ
        for i, rows in enumerate(shifted_rows(got, up, down, cols)):
            for b in range(3):
                moved[3 * i + b] = rows[b]
        tap = [jnp.where(is_in, taps[8 - j : 9 - j, wide], taps[j : j + 1, wide]) for j in range(9)]
        for i in range(4):
            acc = jnp.zeros((PW, BS), F32)
            for a in range(3):
                for b in range(3):
                    acc += tap[3 * a + b] * moved[3 * (i + a) + b]
            conv[i * PW : (i + 1) * PW] = acc

        @pl.when(is_in)
        def _():
            p = pre[:, wide]
            t = jnp.tanh(root_two_pi * (p + cubic_coef * p * p * p))
            slope = 0.5 * (1.0 + t) + 0.5 * p * (1.0 - t * t) * root_two_pi * (
                1.0 + 3.0 * cubic_coef * p * p
            )
            lhs[...] = (conv[...] * slope).astype(BF16)
            pgrad[:, cols] = lhs[...]
            for k in range(NNZ):
                part = dot(tok[meta[first_row + k]], lhs[...], ((0,), (0,))) * loss_scale
                res[k] = part.astype(BF16).reshape(16, 16, BS)

        @pl.when(core != 0)
        def _():
            lhs[...] = conv[...].astype(BF16)
            for k in range(NNZ):
                part = dot(lhs[...], tok[meta[first_row + k]], ((0,), (0,))) * loss_scale
                res[k] = part.astype(BF16).reshape(16, 16, BS)
            sums = []
            for a in range(3):
                for b in range(3):
                    acc = jnp.zeros((PW, BS), F32)
                    for i in range(4):
                        acc += moved[3 * (i + a) + b] * mine[i * PW : (i + 1) * PW, cols].astype(F32)
                    sums.append(jnp.sum(acc, axis=0, keepdims=True))
            rows = jnp.concatenate(sums + [jnp.zeros((7, BS), F32)], axis=0) * loss_scale
            slab[...] = rows.astype(BF16)

        for out, d in ((g0, 0), (far_out, 2), (direct, 1 if half else 3), (through, 3 if half else 1)):
            start = (here + d) % 4 * far
            for k in range(NNZ):
                for s in range(4):
                    out[c, k * 4 + s] = res[k, start + s * near]
            out[c, KERN] = slab[...]


def backward(half, meta, tok, got, mine, up, down, pre, taps, before):
    outs = [((SPLIT, KERN + 1, 16, BS), BF16)] * 4 + [((TOK, SPLIT * BS), BF16)]
    scratch = [
        pltpu.VMEM((TOK, BS), F32),
        pltpu.VMEM((TOK, BS), BF16),
        pltpu.VMEM((NNZ, 16, 16, BS), BF16),
        pltpu.VMEM((16, BS), BF16),
        pltpu.VMEM((18, PW, BS), F32),
    ]
    kernel = functools.partial(backward_kernel, half)
    args = (meta, tok, got, mine, up, down, pre, taps, *before)
    return local(kernel, "backward", outs, args, scratch, flops=2 * TOK * BS * BS * NNZ * SPLIT)


def token_grad_kernel(meta, pg0, pg1, wts, _, keep, send, acc):
    @pl.when(meta[CORE] == 0)
    def _():
        acc[...] = jnp.zeros_like(acc)

        for half, pgrad in enumerate((pg0, pg1)):

            @pl.loop(0, SPLIT)
            def _(c):
                for k in range(NNZ):
                    wt = wts[c + half * SPLIT, k].reshape(BS, BS)
                    row = meta[(c + half * SPLIT) * NNZ + k]
                    acc[row] += dot(pgrad[:, lanes(c)], wt, ((1,), (1,)))

        @pl.loop(0, 16)
        def _(r):
            keep[r] = acc[r, :128].astype(BF16)
            send[r] = acc[r, 128:].astype(BF16)


def token_grad(meta, pg0, pg1, wts, before):
    return local(
        token_grad_kernel,
        "tokengrad",
        [((16, 128, BS), BF16)] * 2,
        (meta, pg0, pg1, wts, before),
        [pltpu.VMEM((16, TOK, BS), F32)],
        flops=2 * TOK * BS * BS * NNZ * COLS,
    )


def gather_sum_kernel(meta, parts, out):
    for b in range(2):
        total = parts[b].astype(F32)
        for z in range(1, NZ):
            total += parts[2 * z + b].astype(F32)
        out[:, b * BS : (b + 1) * BS] = total.astype(BF16)


def relay_kernel(meta, own, got, *refs):
    out = refs[-1]

    @pl.loop(0, SPLIT)
    def _(c):
        for k in range(KERN):
            out[c, k] = (own[c, k].astype(F32) + got[c, k].astype(F32)).astype(BF16)
        out[c, KERN] = own[c, KERN]
        out[c, KERN + 1] = got[c, KERN]


def relay(meta, own, got, *others):
    outs = [((SPLIT, KERN + 2, 16, BS), BF16)]
    return local(relay_kernel, "relay", outs, (meta, own, got, *others), hbm=(4,))[0]


def first_sum_kernel(meta, *refs):
    outs = refs[6:]
    here = jnp.where(meta[CORE] == 0, meta[XPOS], meta[YPOS])

    for half in range(2):
        own, direct, relayed = refs[3 * half : 3 * half + 3]

        @pl.loop(0, SPLIT)
        def _(c):
            at = c + half * SPLIT
            near = relayed[c, KERN].astype(F32) + direct[c, KERN].astype(F32)
            far = own[c, KERN].astype(F32) + relayed[c, KERN + 1].astype(F32)
            for d in range(4):
                s = (here + d) % 4
                for k in range(NNZ):
                    total = own[c, k * 4 + s].astype(F32) + relayed[c, k * 4 + s].astype(F32)
                    outs[d][at, k] = (total + direct[c, k * 4 + s].astype(F32)).astype(BF16)
                outs[d][at, NNZ] = (far + near).astype(BF16)


def second_sum_kernel(meta, own, prev, nxt, far, keep, send):
    first_core = meta[CORE] == 0

    @pl.loop(0, COLS)
    def _(c):
        for k in range(NNZ + 1):
            a, b, e, f = (r[c, k].astype(F32) for r in (own, prev, nxt, far))
            total = ((a + f) + (b + e)).astype(BF16)
            low, high = total[:8], total[8:]
            if k < NNZ:
                keep[c, k] = jnp.where(first_core, low, high)
                send[c, k] = jnp.where(first_core, high, low)
            else:
                for out in (keep, send):
                    out[c, NNZ] = low
                    out[c, NNZ + 1] = high


def place_kernel(meta, keep, got, _, win, wout, kern):
    is_in = meta[CORE] == 0

    @pl.loop(0, NNZ)
    def _(k):
        mine = jnp.stack([keep[c, k].astype(F32) for c in range(COLS)], axis=0)
        its = jnp.stack([got[c, k].astype(F32) for c in range(COLS)], axis=0)
        mine, its = jnp.swapaxes(mine, 0, 1), jnp.swapaxes(its, 0, 1)
        win[:, k] = jnp.where(is_in, mine, its)
        wout[:, k] = jnp.where(is_in, its, mine)

    for c in range(COLS):
        rows = [jnp.where(is_in, got[c, NNZ + i], keep[c, NNZ + i]).astype(F32) for i in range(2)]
        kern[:, c * BS : (c + 1) * BS] = jnp.concatenate(rows, axis=0)[:9]


def on_device(tokens, cotangent, weight_in, weight_out, mix_kernel, block_rows):
    row, crop, z = lax.axis_index("rows"), lax.axis_index("crop"), lax.axis_index("hid")
    core, x, ylo = row % 2, row // 2 % NX, row // 8
    place = jnp.stack([core, x, crop * 2 + ylo, ylo, z]).astype(jnp.int32)
    meta = jnp.concatenate([block_rows.reshape(-1), place])
    is_in = core == 0

    def side(a, b):
        mine, theirs = jnp.where(is_in, a, b), jnp.where(is_in, b, a)
        got = to_partner(theirs)
        return jnp.where(is_in, mine, got), jnp.where(is_in, got, mine)

    own = jnp.stack(side(*(w.transpose(1, 2, 0, 3) for w in (weight_in, weight_out))))
    t0 = jnp.concatenate(side(tokens.reshape(128, 512), cotangent.reshape(128, 512)))

    wa = by_core(own, (0, 1), (0, -1))
    wb = by_core(own, (-1, 0), (1, 0))
    zr1, zl1 = along_z(t0, 1), along_z(t0, -1)
    wc = by_core(hold(meta, own, wa, wb, zr1, zl1), (0, -1), (0, 1))
    wd = by_core(wa, (1, 0), (-1, 0))
    zr2, zl2 = along_z(zr1, 1), along_z(zl1, -1)
    cuts = [((1, *own.shape[1:]), BF16)] * 2
    low, high = local(cut_kernel, "cut", cuts, (meta, wa, wc, wd, zr2, zl2))
    wf = by_core(low, (0, 1), (0, -1))
    wg = by_core(high, (0, -1), (0, 1))
    we = by_core(wc, (-1, 0), (1, 0))
    zr3, zl3 = along_z(zr2, 1), along_z(zl2, -1)
    wh = by_core(wf, (1, 0), (-1, 0))
    wi = by_core(wg, (-1, 0), (1, 0))
    zr4, zl4 = along_z(zr3[:128], 1), along_z(zl3[128:], -1)
    pieces = (own, wa, wb, wc, wd, we, wf, wg, wh, wi)
    token_pieces = (t0, zr1, zr2, zr3, zl1, zl2, zl3, zr4, zl4)

    pre, *halves, wts, tok = forward(meta, token_pieces, pieces)
    out, top, bot = halves[:2], halves[2:4], halves[4:]
    got = [to_partner(o) for o in out]
    edges = [(to_next_chip(b, 1), to_next_chip(t, -1)) for t, b in zip(top, bot)]
    signs = (1, -1)
    half0 = backward(0, meta, tok, got[0], out[0], *edges[0], pre, mix_kernel, ())
    half1 = backward(1, meta, tok, got[1], out[1], *edges[1], pre, mix_kernel, ())
    g0, far, direct, through, pgrad = zip(half0, half1)
    far = [first(f, s) for f, s in zip(far, signs)]
    direct = [first(d, -s) for d, s in zip(direct, signs)]

    relayed = [relay(meta, through[0], far[0], direct[0])]
    keep, send = token_grad(meta, *pgrad, wts, relayed[0])
    terms = jnp.where(is_in, keep, to_partner(send))
    relayed.append(relay(meta, through[1], far[1], direct[1], terms))
    relayed = [first(r, s) for r, s in zip(relayed, signs)]
    terms = lax.all_to_all(terms, "hid", 0, 0, tiled=True)
    (grad_tokens,) = local(gather_sum_kernel, "gathersum", [((128, 512), BF16)], (meta, terms))

    h = local(
        first_sum_kernel,
        "firstsum",
        [((COLS, NNZ + 1, 16, BS), BF16)] * 4,
        (meta, g0[0], direct[0], relayed[0], g0[1], direct[1], relayed[1]),
    )
    last = (h[0], second(h[1], 1), second(h[3], -1), second(h[2], 2))
    shape = ((COLS, NNZ + 2, 8, BS), BF16)
    kept, sent = local(second_sum_kernel, "secondsum", [shape] * 2, (meta, *last))
    out_shape = ((8, NNZ, 8, BS), F32)
    win, wout, kern = local(
        place_kernel,
        "place",
        [out_shape, out_shape, ((9, 8 * BS), F32)],
        (meta, kept, to_partner(sent), grad_tokens),
    )
    grad_tokens = grad_tokens.reshape(1, 2, PW, 512)
    return grad_tokens, win.transpose(0, 2, 1, 3), wout.transpose(0, 2, 1, 3), kern


def solution(mesh):
    placed = (
        P("crop", "rows", None, "hid"),
        P("crop", "rows", None, "hid"),
        P("rows", "hid", None, None),
        P("rows", "hid", None, None),
        P(None, "hid"),
        P("hid", None),
    )
    return jax.shard_map(
        on_device,
        mesh=mesh,
        in_specs=placed,
        out_specs=(
            P("crop", "rows", None, "hid"),
            P(("crop", "rows"), "hid", None, None),
            P(("crop", "rows"), "hid", None, None),
            P(None, "hid"),
        ),
        check_vma=False,
    )
```

```python
import jax
import jax.numpy as jnp
from jax import lax
from jax.experimental import pallas as pl
from jax.experimental.pallas import tpu as pltpu
from jax.sharding import PartitionSpec as P

root_two_pi = 0.7978845608
cubic_coef = 0.044715
loss_scale = 0.03125

F32, BF16 = jnp.float32, jnp.bfloat16
NX, NY, NZ = 4, 4, 8
COLS, NNZ, BS, PW = 8, 5, 256, 64
TOK, KERN = 256, 20
CORE, XPOS, YPOS, YLO, ZPOS = 40, 41, 42, 43, 44
HBM = pl.BlockSpec(memory_space=pltpu.MemorySpace.HBM)
VMEM = pl.BlockSpec(memory_space=pltpu.VMEM)
SMEM = pl.BlockSpec(memory_space=pltpu.SMEM)


def by_core(value, step0, step1):
    pairs = []
    for y in range(NY):
        for x in range(NX):
            for c, (dy, dx) in enumerate((step0, step1)):
                target = (y + dy) % NY * 8 + (x + dx) % NX * 2 + c
                pairs.append((y * 8 + x * 2 + c, target))
    return lax.ppermute(value, ("crop", "rows"), pairs)


def first(value, step):
    return by_core(value, (step, 0), (0, step))


def second(value, step):
    return by_core(value, (0, step), (step, 0))


def to_partner(value):
    return lax.ppermute(value, "rows", [(r, r ^ 1) for r in range(16)])


def to_next_chip(value, step):
    pairs = []
    for q in range(8):
        if 0 <= q + step < 8:
            pairs += [(q * 2 + c, (q + step) * 2 + 1 - c) for c in range(2)]
    return lax.ppermute(value, "rows", pairs)


def along_z(value, step):
    return lax.ppermute(value, "hid", [(z, (z + step) % NZ) for z in range(NZ)])


def dot(a, b, dims):
    return lax.dot_general(a, b, (dims, ((), ())), preferred_element_type=F32)


def local(kernel, name, outs, args, scratch=(), flops=2**20, hbm=()):
    shapes = [jax.ShapeDtypeStruct(s, t) for s, t in outs]
    size = sum(a.size * a.dtype.itemsize for a in args[1:])
    return pl.pallas_call(
        kernel,
        out_shape=shapes,
        in_specs=[SMEM] + [HBM if i in hbm else VMEM for i in range(1, len(args))],
        out_specs=[VMEM] * len(outs),
        scratch_shapes=list(scratch),
        compiler_params=pltpu.CompilerParams(vmem_limit_bytes=14 * 2**20),
        cost_estimate=pl.CostEstimate(flops=flops, transcendentals=0, bytes_accessed=size),
        name=name,
    )(*args)


def lanes(c):
    return pl.ds(pl.multiple_of(c * BS, BS), BS)


def start_tokens(meta, pieces, buf, sem):
    z = meta[ZPOS]
    own, r1, r2, r3, l1, l2, l3, r4, l4 = pieces
    plan = [(own, 0, 0), (r1, 7, 0), (r2, 6, 0), (r3, 5, 0), (l1, 1, 0), (l2, 2, 0), (l3, 3, 0)]
    for src, d, at in plan + [(r4, 4, 0), (l4, 4, 128)]:
        h = (z + d) % NZ
        for part in range(2):
            rows = pl.ds(at, src.shape[0])
            target = buf.at[2 * h + part, rows]
            pltpu.make_async_copy(src.at[:, pl.ds(part * BS, BS)], target, sem).start()


def weight_plan(meta, pieces):
    core, x, ylo = meta[CORE], meta[XPOS], meta[YLO]
    own, a, b, c, d, e, f, g, h, i = pieces
    here, there = ylo * NX, (1 - ylo) * NX
    side = jnp.where(core == 0, NX - 1, 1)
    at = lambda base, step: base + (x + step) % NX
    slots = [
        (own, at(here, 0)),
        (a, at(here, side)),
        (b, at(there, 0)),
        (c, at(here, NX - side)),
        (d, at(there, side)),
        (e, at(there, NX - side)),
    ]
    plan = [(src, s, 2 * j + s) for src, j in slots for s in range(2)]
    for j, low, high in ((at(here, 2), f, g), (at(there, 2), h, i)):
        plan += [(low, 0, 2 * j), (high, 0, 2 * j + 1)]
    return plan


def hold(meta, value, *others):
    def kernel(meta, src, *refs):
        refs[-1][...] = src[...]

    outs = [(value.shape, value.dtype)]
    return local(kernel, "hold", outs, (meta, value, *others))[0]


def cut_kernel(meta, a, c, *refs):
    low, high = refs[-2:]
    low[...] = a[:1]
    high[...] = c[1:]


def forward_kernel(meta, *refs):
    tokens, pieces, outs = refs[:9], refs[9:19], refs[19:]
    pre, out, top, bot, wts, tok, sem = outs
    start_tokens(meta, tokens, tok, sem)
    plan = weight_plan(meta, pieces)
    core = meta[CORE]

    @pl.loop(0, COLS)
    def _(c):
        for k in range(NNZ):
            for src, row, slot in plan:
                wts[c, k, slot] = src[row, c, k]

    pltpu.make_async_copy(tok, tok, sem).wait()

    def total(c, dims):
        acc = None
        for k in range(NNZ):
            part = dot(tok[meta[c * NNZ + k]], wts[c, k].reshape(BS, BS), dims)
            acc = part if acc is None else acc + part
        return acc

    @pl.when(core == 0)
    def _():
        @pl.loop(0, COLS)
        def _(c):
            p = total(c, ((1,), (0,)))
            pre[:, lanes(c)] = p
            t = jnp.tanh(root_two_pi * (p + cubic_coef * p * p * p))
            out[:, lanes(c)] = (0.5 * p * (1.0 + t)).astype(BF16)

    @pl.when(core != 0)
    def _():
        @pl.loop(0, COLS)
        def _(c):
            out[:, lanes(c)] = total(c, ((1,), (1,))).astype(BF16)

    top[...] = out[:PW]
    bot[...] = out[TOK - PW :]


def forward(meta, tokens, pieces):
    wide = COLS * BS
    outs = [((TOK, wide), F32), ((TOK, wide), BF16), ((PW, wide), BF16), ((PW, wide), BF16)]
    outs += [((COLS, NNZ, 16, 16, BS), BF16), ((16, TOK, BS), BF16)]
    return local(
        forward_kernel,
        "forward",
        outs,
        (meta, *tokens, *pieces),
        [pltpu.SemaphoreType.DMA],
        flops=2 * TOK * BS * BS * NNZ * COLS,
        hbm=range(1, 10),
    )


def shifted_rows(mid, up, down, cols):
    cells = lax.broadcasted_iota(jnp.int32, (PW, BS), 0)
    out = []
    for row in [up[:, cols]] + [mid[i * PW : (i + 1) * PW, cols] for i in range(4)] + [down[:, cols]]:
        row = row.astype(F32)
        left = jnp.where(cells == 0, 0.0, pltpu.roll(row, 1, 0))
        right = jnp.where(cells == PW - 1, 0.0, pltpu.roll(row, PW - 1, 0))
        out.append((left, row, right))
    return out


def backward_kernel(meta, tok, got, mine, up, down, pre, taps, *refs):
    *outs, pgrad, conv, lhs, res, slab, moved = refs
    core, x, y = meta[CORE], meta[XPOS], meta[YPOS]
    is_in = core == 0
    slab[...] = jnp.zeros_like(slab)
    here = jnp.where(is_in, y, x)
    far = jnp.where(is_in, NX, 1)
    near = jnp.where(is_in, 1, NY)

    @pl.loop(0, COLS)
    def _(c):
        cols = lanes(c)
        for i, rows in enumerate(shifted_rows(got, up, down, cols)):
            for b in range(3):
                moved[3 * i + b] = rows[b]
        tap = [jnp.where(is_in, taps[8 - j : 9 - j, cols], taps[j : j + 1, cols]) for j in range(9)]
        for i in range(4):
            acc = jnp.zeros((PW, BS), F32)
            for a in range(3):
                for b in range(3):
                    acc += tap[3 * a + b] * moved[3 * (i + a) + b]
            conv[i * PW : (i + 1) * PW] = acc

        @pl.when(is_in)
        def _():
            p = pre[:, cols]
            t = jnp.tanh(root_two_pi * (p + cubic_coef * p * p * p))
            slope = 0.5 * (1.0 + t) + 0.5 * p * (1.0 - t * t) * root_two_pi * (
                1.0 + 3.0 * cubic_coef * p * p
            )
            lhs[...] = (conv[...] * slope).astype(BF16)
            pgrad[:, cols] = lhs[...]
            for k in range(NNZ):
                part = dot(tok[meta[c * NNZ + k]], lhs[...], ((0,), (0,))) * loss_scale
                res[k] = part.astype(BF16).reshape(16, 16, BS)

        @pl.when(core != 0)
        def _():
            lhs[...] = conv[...].astype(BF16)
            for k in range(NNZ):
                part = dot(lhs[...], tok[meta[c * NNZ + k]], ((0,), (0,))) * loss_scale
                res[k] = part.astype(BF16).reshape(16, 16, BS)
            sums = []
            for a in range(3):
                for b in range(3):
                    acc = jnp.zeros((PW, BS), F32)
                    for i in range(4):
                        acc += moved[3 * (i + a) + b] * mine[i * PW : (i + 1) * PW, cols].astype(F32)
                    sums.append(jnp.sum(acc, axis=0, keepdims=True))
            rows = jnp.concatenate(sums + [jnp.zeros((7, BS), F32)], axis=0) * loss_scale
            slab[...] = rows.astype(BF16)

        for d, out in enumerate(outs):
            start = (here + d) % 4 * far
            for k in range(NNZ):
                for s in range(4):
                    out[c, k * 4 + s] = res[k, start + s * near]
            out[c, KERN] = slab[...]


def backward(meta, tok, got, mine, up, down, pre, taps):
    outs = [((COLS, KERN + 1, 16, BS), BF16)] * 4 + [((TOK, COLS * BS), BF16)]
    scratch = [
        pltpu.VMEM((TOK, BS), F32),
        pltpu.VMEM((TOK, BS), BF16),
        pltpu.VMEM((NNZ, 16, 16, BS), BF16),
        pltpu.VMEM((16, BS), BF16),
        pltpu.VMEM((18, PW, BS), F32),
    ]
    args = (meta, tok, got, mine, up, down, pre, taps)
    return local(
        backward_kernel, "backward", outs, args, scratch, flops=2 * TOK * BS * BS * NNZ * COLS
    )


def token_grad_kernel(meta, pgrad, wts, keep, send, acc):
    @pl.when(meta[CORE] == 0)
    def _():
        acc[...] = jnp.zeros_like(acc)

        @pl.loop(0, COLS)
        def _(c):
            for k in range(NNZ):
                wt = wts[c, k].reshape(BS, BS)
                acc[meta[c * NNZ + k]] += dot(pgrad[:, lanes(c)], wt, ((1,), (1,)))

        @pl.loop(0, 16)
        def _(r):
            keep[r] = acc[r, :128].astype(BF16)
            send[r] = acc[r, 128:].astype(BF16)


def token_grad(meta, pgrad, wts):
    return local(
        token_grad_kernel,
        "tokengrad",
        [((16, 128, BS), BF16)] * 2,
        (meta, pgrad, wts),
        [pltpu.VMEM((16, TOK, BS), F32)],
        flops=2 * TOK * BS * BS * NNZ * COLS,
    )


def gather_sum_kernel(meta, parts, out, flag):
    flag[...] = jnp.zeros_like(flag)
    for b in range(2):
        total = parts[b].astype(F32)
        for z in range(1, NZ):
            total += parts[2 * z + b].astype(F32)
        out[:, b * BS : (b + 1) * BS] = total.astype(BF16)


def first_sum_kernel(meta, own, prev, nxt, far, *refs):
    outs = refs[-4:]
    here = jnp.where(meta[CORE] == 0, meta[XPOS], meta[YPOS])

    def total(c, at):
        a, b, e, f = (r[c, at].astype(F32) for r in (own, prev, nxt, far))
        return ((a + f) + (b + e)).astype(BF16)

    @pl.loop(0, COLS)
    def _(c):
        for d in range(4):
            for k in range(NNZ):
                outs[d][c, k] = total(c, k * 4 + (here + d) % 4)
        slab = total(c, KERN)
        for out in outs:
            out[c, NNZ] = slab


def second_sum_kernel(meta, own, prev, nxt, far, keep, send):
    first_core = meta[CORE] == 0

    @pl.loop(0, COLS)
    def _(c):
        for k in range(NNZ + 1):
            a, b, e, f = (r[c, k].astype(F32) for r in (own, prev, nxt, far))
            total = ((a + f) + (b + e)).astype(BF16)
            low, high = total[:8], total[8:]
            if k < NNZ:
                keep[c, k] = jnp.where(first_core, low, high)
                send[c, k] = jnp.where(first_core, high, low)
            else:
                for out in (keep, send):
                    out[c, NNZ] = low
                    out[c, NNZ + 1] = high


def place_kernel(meta, keep, got, _, win, wout, kern):
    is_in = meta[CORE] == 0

    @pl.loop(0, NNZ)
    def _(k):
        mine = jnp.stack([keep[c, k].astype(F32) for c in range(COLS)], axis=0)
        its = jnp.stack([got[c, k].astype(F32) for c in range(COLS)], axis=0)
        mine, its = jnp.swapaxes(mine, 0, 1), jnp.swapaxes(its, 0, 1)
        win[:, k] = jnp.where(is_in, mine, its)
        wout[:, k] = jnp.where(is_in, its, mine)

    for c in range(COLS):
        rows = [jnp.where(is_in, got[c, NNZ + i], keep[c, NNZ + i]).astype(F32) for i in range(2)]
        kern[:, c * BS : (c + 1) * BS] = jnp.concatenate(rows, axis=0)[:9]


def on_device(tokens, cotangent, weight_in, weight_out, mix_kernel, block_rows):
    row, crop, z = lax.axis_index("rows"), lax.axis_index("crop"), lax.axis_index("hid")
    core, x, ylo = row % 2, row // 2 % NX, row // 8
    place = jnp.stack([core, x, crop * 2 + ylo, ylo, z]).astype(jnp.int32)
    meta = jnp.concatenate([block_rows.reshape(-1), place])
    is_in = core == 0

    def side(a, b):
        mine, theirs = jnp.where(is_in, a, b), jnp.where(is_in, b, a)
        got = to_partner(theirs)
        return jnp.where(is_in, mine, got), jnp.where(is_in, got, mine)

    own = jnp.stack(side(*(w.transpose(1, 2, 0, 3) for w in (weight_in, weight_out))))
    t0 = jnp.concatenate(side(tokens.reshape(128, 512), cotangent.reshape(128, 512)))

    wa = by_core(own, (0, 1), (0, -1))
    wb = by_core(own, (-1, 0), (1, 0))
    zr1, zl1 = along_z(t0, 1), along_z(t0, -1)
    wc = by_core(hold(meta, own, wa, wb, zr1, zl1), (0, -1), (0, 1))
    wd = by_core(wa, (1, 0), (-1, 0))
    zr2, zl2 = along_z(zr1, 1), along_z(zl1, -1)
    cuts = [((1, *own.shape[1:]), BF16)] * 2
    low, high = local(cut_kernel, "cut", cuts, (meta, wa, wc, wd, zr2, zl2))
    wf = by_core(low, (0, 1), (0, -1))
    wg = by_core(high, (0, -1), (0, 1))
    we = by_core(wc, (-1, 0), (1, 0))
    zr3, zl3 = along_z(zr2, 1), along_z(zl2, -1)
    wh = by_core(wf, (1, 0), (-1, 0))
    wi = by_core(wg, (-1, 0), (1, 0))
    zr4, zl4 = along_z(zr3[:128], 1), along_z(zl3[128:], -1)
    pieces = (own, wa, wb, wc, wd, we, wf, wg, wh, wi)
    token_pieces = (t0, zr1, zr2, zr3, zl1, zl2, zl3, zr4, zl4)

    pre, out, top, bot, wts, tok = forward(meta, token_pieces, pieces)
    got = to_partner(out)
    up, down = to_next_chip(bot, 1), to_next_chip(top, -1)
    *g, pgrad = backward(meta, tok, got, out, up, down, pre, mix_kernel)
    parts = (g[0], first(g[1], 1), first(g[3], -1), first(g[2], 2))

    keep, send = token_grad(meta, pgrad, wts)
    terms = jnp.where(is_in, keep, to_partner(send))
    shares = lax.all_to_all(terms, "hid", 0, 0, tiled=True)
    outs = [((128, 512), BF16), ((8, 128), F32)]
    grad_tokens, flag = local(gather_sum_kernel, "gathersum", outs, (meta, shares))

    h = local(
        first_sum_kernel,
        "firstsum",
        [((COLS, NNZ + 1, 16, BS), BF16)] * 4,
        (meta, *parts, terms),
        hbm=(5,),
    )
    last = (h[0], second(h[1], 1), second(h[3], -1), second(h[2], 2))
    shape = ((COLS, NNZ + 2, 8, BS), BF16)
    kept, sent = local(second_sum_kernel, "secondsum", [shape] * 2, (meta, *last))
    out_shape = ((8, NNZ, 8, BS), F32)
    win, wout, kern = local(
        place_kernel,
        "place",
        [out_shape, out_shape, ((9, 8 * BS), F32)],
        (meta, kept, to_partner(sent), flag),
    )
    grad_tokens = grad_tokens.reshape(1, 2, PW, 512)
    return grad_tokens, win.transpose(0, 2, 1, 3), wout.transpose(0, 2, 1, 3), kern


def solution(mesh):
    placed = (
        P("crop", "rows", None, "hid"),
        P("crop", "rows", None, "hid"),
        P("rows", "hid", None, None),
        P("rows", "hid", None, None),
        P(None, "hid"),
        P("hid", None),
    )
    return jax.shard_map(
        on_device,
        mesh=mesh,
        in_specs=placed,
        out_specs=(
            P("crop", "rows", None, "hid"),
            P(("crop", "rows"), "hid", None, None),
            P(("crop", "rows"), "hid", None, None),
            P(None, "hid"),
        ),
        check_vma=False,
    )
```

```python
import jax
import jax.numpy as jnp
from jax import lax
from jax.experimental import pallas as pl
from jax.experimental.pallas import tpu as pltpu
from jax.sharding import PartitionSpec as P

root_two_pi = 0.7978845608
cubic_coef = 0.044715
loss_scale = 0.03125

F32, BF16 = jnp.float32, jnp.bfloat16
NX, NY, NZ = 4, 4, 8
COLS, NNZ, BS, PW = 8, 5, 256, 64
TOK, KERN, SLABS = 256, 20, 56
CORE, XPOS, YPOS, YLO, ZPOS = 40, 41, 42, 43, 44
HBM = pl.BlockSpec(memory_space=pltpu.MemorySpace.HBM)
VMEM = pl.BlockSpec(memory_space=pltpu.VMEM)
SMEM = pl.BlockSpec(memory_space=pltpu.SMEM)


def by_core(value, step0, step1):
    pairs = []
    for y in range(NY):
        for x in range(NX):
            for c, (dy, dx) in enumerate((step0, step1)):
                target = (y + dy) % NY * 8 + (x + dx) % NX * 2 + c
                pairs.append((y * 8 + x * 2 + c, target))
    return lax.ppermute(value, ("crop", "rows"), pairs)


def first(value, step):
    return by_core(value, (step, 0), (0, step))


def second(value, step):
    return by_core(value, (0, step), (step, 0))


def to_partner(value):
    return lax.ppermute(value, "rows", [(r, r ^ 1) for r in range(16)])


def to_next_chip(value, step):
    pairs = []
    for q in range(8):
        if 0 <= q + step < 8:
            pairs += [(q * 2 + c, (q + step) * 2 + 1 - c) for c in range(2)]
    return lax.ppermute(value, "rows", pairs)


def along_z(value, step):
    return lax.ppermute(value, "hid", [(z, (z + step) % NZ) for z in range(NZ)])


def dot(a, b, dims):
    return lax.dot_general(a, b, (dims, ((), ())), preferred_element_type=F32)


def local(kernel, name, outs, args, scratch=(), flops=2**20, hbm=(), hbm_out=()):
    shapes = [
        pltpu.HBM(s, t) if i in hbm_out else jax.ShapeDtypeStruct(s, t) for i, (s, t) in enumerate(outs)
    ]
    size = sum(a.size * a.dtype.itemsize for a in args[1:])
    return pl.pallas_call(
        kernel,
        out_shape=shapes,
        in_specs=[SMEM] + [HBM if i in hbm else VMEM for i in range(1, len(args))],
        out_specs=[HBM if i in hbm_out else VMEM for i in range(len(outs))],
        scratch_shapes=list(scratch),
        compiler_params=pltpu.CompilerParams(vmem_limit_bytes=20 * 2**20),
        cost_estimate=pl.CostEstimate(flops=flops, transcendentals=0, bytes_accessed=size),
        name=name,
    )(*args)


def lanes(c):
    return pl.ds(pl.multiple_of(c * BS, BS), BS)


def split_kernel(meta, *refs):
    sources, (mine, theirs, *held, sems) = refs[:4], refs[4:]
    copies = [pltpu.make_async_copy(a, b, sems.at[i]) for i, (a, b) in enumerate(zip(sources, held))]
    for copy in copies:
        copy.start()
    for copy in copies:
        copy.wait()
    w_in, w_out, tok, cot = held
    is_in = meta[CORE] == 0

    def put(at, a, b):
        mine[at] = jnp.where(is_in, a, b).astype(BF16)
        theirs[at] = jnp.where(is_in, b, a).astype(BF16)

    for k in range(NNZ):
        a, b = (jnp.swapaxes(w[:, k].astype(F32), 0, 1) for w in (w_in, w_out))
        for c in range(COLS):
            put(c * NNZ + k, a[c], b[c])
    for p in range(2):
        for r in range(8):
            part = (slice(r * 16, r * 16 + 16), slice(p * BS, p * BS + BS))
            put(COLS * NNZ + p * 8 + r, tok[part].astype(F32), cot[part].astype(F32))


def join_kernel(meta, mine, got, own, rows):
    for s in range(2):
        here = meta[CORE] == s

        def take(at):
            return jnp.where(here, mine[at].astype(F32), got[at].astype(F32)).astype(BF16)

        for c in range(COLS):
            for k in range(NNZ):
                own[s, c, k] = take(c * NNZ + k)
        for p in range(2):
            for r in range(8):
                at = s * 128 + r * 16
                rows[at : at + 16, p * BS : p * BS + BS] = take(COLS * NNZ + p * 8 + r)


def start_tokens(meta, pieces, buf, sem):
    z = meta[ZPOS]
    own, r1, r2, r3, l1, l2, l3, r4, l4 = pieces
    plan = [(own, 0, 0), (r1, 7, 0), (r2, 6, 0), (r3, 5, 0), (l1, 1, 0), (l2, 2, 0), (l3, 3, 0)]
    for src, d, at in plan + [(r4, 4, 0), (l4, 4, 128)]:
        h = (z + d) % NZ
        for part in range(2):
            rows = pl.ds(at, src.shape[0])
            target = buf.at[2 * h + part, rows]
            pltpu.make_async_copy(src.at[:, pl.ds(part * BS, BS)], target, sem).start()


def weight_plan(meta, pieces):
    core, x, ylo = meta[CORE], meta[XPOS], meta[YLO]
    own, a, b, c, d, e, f, g, h, i = pieces
    here, there = ylo * NX, (1 - ylo) * NX
    side = jnp.where(core == 0, NX - 1, 1)
    at = lambda base, step: base + (x + step) % NX
    slots = [
        (own, at(here, 0)),
        (a, at(here, side)),
        (b, at(there, 0)),
        (c, at(here, NX - side)),
        (d, at(there, side)),
        (e, at(there, NX - side)),
    ]
    plan = [(src, s, 2 * j + s) for src, j in slots for s in range(2)]
    for j, low, high in ((at(here, 2), f, g), (at(there, 2), h, i)):
        plan += [(low, 0, 2 * j), (high, 0, 2 * j + 1)]
    return plan


def hold(meta, value, *others):
    def kernel(meta, src, *refs):
        refs[-1][...] = src[...]

    outs = [(value.shape, value.dtype)]
    return local(kernel, "hold", outs, (meta, value, *others))[0]


def cut_kernel(meta, a, c, *refs):
    low, high = refs[-2:]
    low[...] = a[:1]
    high[...] = c[1:]


def forward_kernel(meta, *refs):
    tokens, pieces, outs = refs[:9], refs[9:19], refs[19:]
    pre, out, top, bot, wts, tok, sem = outs
    start_tokens(meta, tokens, tok, sem)
    plan = weight_plan(meta, pieces)
    core = meta[CORE]

    @pl.loop(0, COLS)
    def _(c):
        for k in range(NNZ):
            for src, row, slot in plan:
                wts[c, k, slot] = src[row, c, k]

    pltpu.make_async_copy(tok, tok, sem).wait()

    def total(c, dims):
        acc = None
        for k in range(NNZ):
            part = dot(tok[meta[c * NNZ + k]], wts[c, k].reshape(BS, BS), dims)
            acc = part if acc is None else acc + part
        return acc

    @pl.when(core == 0)
    def _():
        @pl.loop(0, COLS)
        def _(c):
            p = total(c, ((1,), (0,)))
            pre[:, lanes(c)] = p
            t = jnp.tanh(root_two_pi * (p + cubic_coef * p * p * p))
            out[:, lanes(c)] = (0.5 * p * (1.0 + t)).astype(BF16)

    @pl.when(core != 0)
    def _():
        @pl.loop(0, COLS)
        def _(c):
            out[:, lanes(c)] = total(c, ((1,), (1,))).astype(BF16)

    top[...] = out[:PW]
    bot[...] = out[TOK - PW :]


def forward(meta, tokens, pieces):
    wide = COLS * BS
    outs = [((TOK, wide), F32), ((TOK, wide), BF16), ((PW, wide), BF16), ((PW, wide), BF16)]
    outs += [((COLS, NNZ, 16, 16, BS), BF16), ((16, TOK, BS), BF16)]
    return local(
        forward_kernel,
        "forward",
        outs,
        (meta, *tokens, *pieces),
        [pltpu.SemaphoreType.DMA],
        flops=2 * TOK * BS * BS * NNZ * COLS,
        hbm=range(1, 10),
    )


def shifted_rows(mid, up, down, cols):
    cells = lax.broadcasted_iota(jnp.int32, (PW, BS), 0)
    out = []
    for row in [up[:, cols]] + [mid[i * PW : (i + 1) * PW, cols] for i in range(4)] + [down[:, cols]]:
        row = row.astype(F32)
        left = jnp.where(cells == 0, 0.0, pltpu.roll(row, 1, 0))
        right = jnp.where(cells == PW - 1, 0.0, pltpu.roll(row, PW - 1, 0))
        out.append((left, row, right))
    return out


def backward_kernel(meta, tok, got, mine, up, down, pre, taps, *refs):
    *outs, pgrad, conv, lhs, res, slab, moved, stage, sems = refs
    core, x, y = meta[CORE], meta[XPOS], meta[YPOS]
    is_in = core == 0
    slab[...] = jnp.zeros_like(slab)
    here = jnp.where(is_in, y, x)
    far = jnp.where(is_in, NX, 1)
    near = jnp.where(is_in, 1, NY)

    @pl.loop(0, COLS)
    def _(c):
        cols = lanes(c)
        for i, rows in enumerate(shifted_rows(got, up, down, cols)):
            for b in range(3):
                moved[3 * i + b] = rows[b]
        tap = [jnp.where(is_in, taps[8 - j : 9 - j, cols], taps[j : j + 1, cols]) for j in range(9)]
        for i in range(4):
            acc = jnp.zeros((PW, BS), F32)
            for a in range(3):
                for b in range(3):
                    acc += tap[3 * a + b] * moved[3 * (i + a) + b]
            conv[i * PW : (i + 1) * PW] = acc

        @pl.when(is_in)
        def _():
            p = pre[:, cols]
            t = jnp.tanh(root_two_pi * (p + cubic_coef * p * p * p))
            slope = 0.5 * (1.0 + t) + 0.5 * p * (1.0 - t * t) * root_two_pi * (
                1.0 + 3.0 * cubic_coef * p * p
            )
            lhs[...] = (conv[...] * slope).astype(BF16)
            pgrad[:, cols] = lhs[...]
            for k in range(NNZ):
                part = dot(tok[meta[c * NNZ + k]], lhs[...], ((0,), (0,))) * loss_scale
                res[k] = part.astype(BF16).reshape(16, 16, BS)

        @pl.when(core != 0)
        def _():
            lhs[...] = conv[...].astype(BF16)
            for k in range(NNZ):
                part = dot(lhs[...], tok[meta[c * NNZ + k]], ((0,), (0,))) * loss_scale
                res[k] = part.astype(BF16).reshape(16, 16, BS)
            sums = []
            for a in range(3):
                for b in range(3):
                    acc = jnp.zeros((PW, BS), F32)
                    for i in range(4):
                        acc += moved[3 * (i + a) + b] * mine[i * PW : (i + 1) * PW, cols].astype(F32)
                    sums.append(jnp.sum(acc, axis=0, keepdims=True))
            rows = jnp.concatenate(sums + [jnp.zeros((7, BS), F32)], axis=0) * loss_scale
            slab[...] = rows.astype(BF16)

        for d, out in enumerate(outs):
            start = (here + d) % 4 * far
            for k in range(NNZ):
                for s in range(4):
                    stage[d, c, k * 4 + s] = res[k, start + s * near]
            stage[d, c, KERN] = slab[...]
            pltpu.make_async_copy(stage.at[d, c], out.at[c], sems.at[d]).start()

    for d, out in enumerate(outs):
        pltpu.make_async_copy(stage.at[d], out, sems.at[d]).wait()


def backward(meta, tok, got, mine, up, down, pre, taps):
    outs = [((COLS, KERN + 1, 16, BS), BF16)] * 4 + [((TOK, COLS * BS), BF16)]
    scratch = [
        pltpu.VMEM((TOK, BS), F32),
        pltpu.VMEM((TOK, BS), BF16),
        pltpu.VMEM((NNZ, 16, 16, BS), BF16),
        pltpu.VMEM((16, BS), BF16),
        pltpu.VMEM((18, PW, BS), F32),
        pltpu.VMEM((4, COLS, KERN + 1, 16, BS), BF16),
        pltpu.SemaphoreType.DMA((4,)),
    ]
    args = (meta, tok, got, mine, up, down, pre, taps)
    return local(
        backward_kernel,
        "backward",
        outs,
        args,
        scratch,
        flops=2 * TOK * BS * BS * NNZ * COLS,
        hbm_out=range(4),
    )


def token_grad_kernel(meta, pgrad, wts, keep, send, acc):
    @pl.when(meta[CORE] == 0)
    def _():
        acc[...] = jnp.zeros_like(acc)

        @pl.loop(0, COLS, unroll=2)
        def _(c):
            for k in range(NNZ):
                wt = wts[c, k].reshape(BS, BS)
                acc[meta[c * NNZ + k]] += dot(pgrad[:, lanes(c)], wt, ((1,), (1,)))

        @pl.loop(0, 16)
        def _(r):
            keep[r] = acc[r, :128].astype(BF16)
            send[r] = acc[r, 128:].astype(BF16)


def token_grad(meta, pgrad, wts):
    return local(
        token_grad_kernel,
        "tokengrad",
        [((16, 128, BS), BF16)] * 2,
        (meta, pgrad, wts),
        [pltpu.VMEM((16, TOK, BS), F32)],
        flops=2 * TOK * BS * BS * NNZ * COLS,
    )


def gather_sum_kernel(meta, parts, out, flag):
    flag[...] = jnp.zeros_like(flag)
    for b in range(2):
        total = parts[b].astype(F32)
        for z in range(1, NZ):
            total += parts[2 * z + b].astype(F32)
        out[:, b * BS : (b + 1) * BS] = total.astype(BF16)


def first_sum_kernel(meta, *refs):
    parts, outs, (held, sems) = refs[:4], refs[5:9], refs[9:]
    here = jnp.where(meta[CORE] == 0, meta[XPOS], meta[YPOS])
    for c in range(COLS):
        for i, part in enumerate(parts):
            pltpu.make_async_copy(part.at[c], held.at[c, i], sems.at[c]).start()

    @pl.loop(0, COLS)
    def _(c):
        pltpu.make_async_copy(held.at[c], held.at[c], sems.at[c]).wait()

        def total(at):
            a, b, e, f = (held[c, i, at].astype(F32) for i in range(4))
            return ((a + f) + (b + e)).astype(BF16)

        for d in range(4):
            for k in range(NNZ):
                outs[d][c, k] = total(k * 4 + (here + d) % 4)
        slab = total(KERN)
        for out in outs:
            out[c, NNZ] = slab


def second_sum_kernel(meta, own, prev, nxt, far, keep, send):
    first_core = meta[CORE] == 0

    @pl.loop(0, COLS)
    def _(c):
        for k in range(NNZ + 1):
            a, b, e, f = (r[c, k].astype(F32) for r in (own, prev, nxt, far))
            total = ((a + f) + (b + e)).astype(BF16)
            low, high = total[:8], total[8:]
            if k < NNZ:
                keep[c, k] = jnp.where(first_core, low, high)
                send[c, k] = jnp.where(first_core, high, low)
            else:
                for out in (keep, send):
                    out[c, NNZ] = low
                    out[c, NNZ + 1] = high


def place_kernel(meta, keep, got, _, win, wout, kern):
    is_in = meta[CORE] == 0

    @pl.loop(0, NNZ)
    def _(k):
        mine = jnp.stack([keep[c, k].astype(F32) for c in range(COLS)], axis=0)
        its = jnp.stack([got[c, k].astype(F32) for c in range(COLS)], axis=0)
        mine, its = jnp.swapaxes(mine, 0, 1), jnp.swapaxes(its, 0, 1)
        win[:, k] = jnp.where(is_in, mine, its)
        wout[:, k] = jnp.where(is_in, its, mine)

    for c in range(COLS):
        rows = [jnp.where(is_in, got[c, NNZ + i], keep[c, NNZ + i]).astype(F32) for i in range(2)]
        kern[:, c * BS : (c + 1) * BS] = jnp.concatenate(rows, axis=0)[:9]


def on_device(tokens, cotangent, weight_in, weight_out, mix_kernel, block_rows):
    row, crop, z = lax.axis_index("rows"), lax.axis_index("crop"), lax.axis_index("hid")
    core, x, ylo = row % 2, row // 2 % NX, row // 8
    place = jnp.stack([core, x, crop * 2 + ylo, ylo, z]).astype(jnp.int32)
    meta = jnp.concatenate([block_rows.reshape(-1), place])
    is_in = core == 0
    views = [w.transpose(0, 2, 1, 3) for w in (weight_in, weight_out)]
    rows = [t.reshape(128, 512) for t in (tokens, cotangent)]
    slabs = [((SLABS, 16, BS), BF16)] * 2
    held = [pltpu.VMEM(a.shape, BF16) for a in views + rows] + [pltpu.SemaphoreType.DMA((4,))]
    args = (meta, *(pltpu.with_memory_space_constraint(a, pltpu.HBM) for a in views + rows))
    mine, theirs = local(split_kernel, "split", slabs, args, held, hbm=range(1, 5))
    shapes = [((2, COLS, NNZ, 16, BS), BF16), ((TOK, 2 * BS), BF16)]
    own, t0 = local(join_kernel, "join", shapes, (meta, mine, to_partner(theirs)))

    wa = by_core(own, (0, 1), (0, -1))
    wb = by_core(own, (-1, 0), (1, 0))
    zr1, zl1 = along_z(t0, 1), along_z(t0, -1)
    wc = by_core(hold(meta, own, wa, wb, zr1, zl1), (0, -1), (0, 1))
    wd = by_core(wa, (1, 0), (-1, 0))
    zr2, zl2 = along_z(zr1, 1), along_z(zl1, -1)
    cuts = [((1, *own.shape[1:]), BF16)] * 2
    low, high = local(cut_kernel, "cut", cuts, (meta, wa, wc, wd, zr2, zl2))
    wf = by_core(low, (0, 1), (0, -1))
    wg = by_core(high, (0, -1), (0, 1))
    we = by_core(wc, (-1, 0), (1, 0))
    zr3, zl3 = along_z(zr2, 1), along_z(zl2, -1)
    wh = by_core(wf, (1, 0), (-1, 0))
    wi = by_core(wg, (-1, 0), (1, 0))
    zr4, zl4 = along_z(zr3[:128], 1), along_z(zl3[128:], -1)
    pieces = (own, wa, wb, wc, wd, we, wf, wg, wh, wi)
    token_pieces = (t0, zr1, zr2, zr3, zl1, zl2, zl3, zr4, zl4)

    pre, out, top, bot, wts, tok = forward(meta, token_pieces, pieces)
    got = to_partner(out)
    up, down = to_next_chip(bot, 1), to_next_chip(top, -1)
    *g, pgrad = backward(meta, tok, got, out, up, down, pre, mix_kernel)
    parts = (g[0], first(g[1], 1), first(g[3], -1), first(g[2], 2))

    keep, send = token_grad(meta, pgrad, wts)
    terms = jnp.where(is_in, keep, to_partner(send))
    shares = lax.all_to_all(terms, "hid", 0, 0, tiled=True)
    outs = [((128, 512), BF16), ((8, 128), F32)]
    grad_tokens, flag = local(gather_sum_kernel, "gathersum", outs, (meta, shares))

    h = local(
        first_sum_kernel,
        "firstsum",
        [((COLS, NNZ + 1, 16, BS), BF16)] * 4,
        (meta, *parts, terms),
        [pltpu.VMEM((COLS, 4, KERN + 1, 16, BS), BF16), pltpu.SemaphoreType.DMA((COLS,))],
        hbm=range(1, 6),
    )
    last = (h[0], second(h[1], 1), second(h[3], -1), second(h[2], 2))
    shape = ((COLS, NNZ + 2, 8, BS), BF16)
    kept, sent = local(second_sum_kernel, "secondsum", [shape] * 2, (meta, *last))
    out_shape = ((8, NNZ, 8, BS), F32)
    win, wout, kern = local(
        place_kernel,
        "place",
        [out_shape, out_shape, ((9, 8 * BS), F32)],
        (meta, kept, to_partner(sent), flag),
    )
    grad_tokens = grad_tokens.reshape(1, 2, PW, 512)
    return grad_tokens, win.transpose(0, 2, 1, 3), wout.transpose(0, 2, 1, 3), kern


def solution(mesh):
    placed = (
        P("crop", "rows", None, "hid"),
        P("crop", "rows", None, "hid"),
        P("rows", "hid", None, None),
        P("rows", "hid", None, None),
        P(None, "hid"),
        P("hid", None),
    )
    return jax.shard_map(
        on_device,
        mesh=mesh,
        in_specs=placed,
        out_specs=(
            P("crop", "rows", None, "hid"),
            P(("crop", "rows"), "hid", None, None),
            P(("crop", "rows"), "hid", None, None),
            P(None, "hid"),
        ),
        check_vma=False,
    )
```

```python
import jax
import jax.numpy as jnp
from jax import lax
from jax.experimental import pallas as pl
from jax.experimental.pallas import tpu as pltpu
from jax.sharding import PartitionSpec as P

root_two_pi = 0.7978845608
cubic_coef = 0.044715
loss_scale = 0.03125

F32, BF16 = jnp.float32, jnp.bfloat16
NX, NY, NZ = 4, 4, 8
COLS, NNZ, BS, PW = 8, 5, 256, 64
TOK, KERN, SPLIT = 256, 20, 4
CORE, XPOS, YPOS, YLO, ZPOS = 40, 41, 42, 43, 44
HBM = pl.BlockSpec(memory_space=pltpu.MemorySpace.HBM)
VMEM = pl.BlockSpec(memory_space=pltpu.VMEM)
SMEM = pl.BlockSpec(memory_space=pltpu.SMEM)


def by_core(value, step0, step1):
    pairs = []
    for y in range(NY):
        for x in range(NX):
            for c, (dy, dx) in enumerate((step0, step1)):
                target = (y + dy) % NY * 8 + (x + dx) % NX * 2 + c
                pairs.append((y * 8 + x * 2 + c, target))
    return lax.ppermute(value, ("crop", "rows"), pairs)


def first(value, step):
    return by_core(value, (step, 0), (0, step))


def second(value, step):
    return by_core(value, (0, step), (step, 0))


def to_partner(value):
    return lax.ppermute(value, "rows", [(r, r ^ 1) for r in range(16)])


def to_next_chip(value, step):
    pairs = []
    for q in range(8):
        if 0 <= q + step < 8:
            pairs += [(q * 2 + c, (q + step) * 2 + 1 - c) for c in range(2)]
    return lax.ppermute(value, "rows", pairs)


def along_z(value, step):
    return lax.ppermute(value, "hid", [(z, (z + step) % NZ) for z in range(NZ)])


def dot(a, b, dims):
    return lax.dot_general(a, b, (dims, ((), ())), preferred_element_type=F32)


def local(kernel, name, outs, args, scratch=(), flops=2**20, hbm=(), hbm_out=()):
    shapes = [
        pltpu.HBM(s, t) if i in hbm_out else jax.ShapeDtypeStruct(s, t) for i, (s, t) in enumerate(outs)
    ]
    size = sum(a.size * a.dtype.itemsize for a in args[1:])
    return pl.pallas_call(
        kernel,
        out_shape=shapes,
        in_specs=[SMEM] + [HBM if i in hbm else VMEM for i in range(1, len(args))],
        out_specs=[HBM if i in hbm_out else VMEM for i in range(len(outs))],
        scratch_shapes=list(scratch),
        compiler_params=pltpu.CompilerParams(vmem_limit_bytes=20 * 2**20),
        cost_estimate=pl.CostEstimate(flops=flops, transcendentals=0, bytes_accessed=size),
        name=name,
    )(*args)


def lanes(c):
    return pl.ds(pl.multiple_of(c * BS, BS), BS)


def start_tokens(meta, pieces, buf, sem):
    z = meta[ZPOS]
    own, r1, r2, r3, l1, l2, l3, r4, l4 = pieces
    plan = [(own, 0, 0), (r1, 7, 0), (r2, 6, 0), (r3, 5, 0), (l1, 1, 0), (l2, 2, 0), (l3, 3, 0)]
    for src, d, at in plan + [(r4, 4, 0), (l4, 4, 128)]:
        h = (z + d) % NZ
        for part in range(2):
            rows = pl.ds(at, src.shape[0])
            target = buf.at[2 * h + part, rows]
            pltpu.make_async_copy(src.at[:, pl.ds(part * BS, BS)], target, sem).start()


def weight_plan(meta, pieces):
    core, x, ylo = meta[CORE], meta[XPOS], meta[YLO]
    own, a, b, c, d, e, f, g, h, i = pieces
    here, there = ylo * NX, (1 - ylo) * NX
    side = jnp.where(core == 0, NX - 1, 1)
    at = lambda base, step: base + (x + step) % NX
    slots = [
        (own, at(here, 0)),
        (a, at(here, side)),
        (b, at(there, 0)),
        (c, at(here, NX - side)),
        (d, at(there, side)),
        (e, at(there, NX - side)),
    ]
    plan = [(src, s, 2 * j + s) for src, j in slots for s in range(2)]
    for j, low, high in ((at(here, 2), f, g), (at(there, 2), h, i)):
        plan += [(low, 0, 2 * j), (high, 0, 2 * j + 1)]
    return plan


def hold(meta, value, *others):
    def kernel(meta, src, *refs):
        refs[-1][...] = src[...]

    outs = [(value.shape, value.dtype)]
    return local(kernel, "hold", outs, (meta, value, *others))[0]


def cut_kernel(meta, a, c, *refs):
    low, high = refs[-2:]
    low[...] = a[:1]
    high[...] = c[1:]


def forward_kernel(meta, *refs):
    tokens, pieces, outs = refs[:9], refs[9:19], refs[19:]
    pre, out, top, bot, wts, tok, sem = outs
    start_tokens(meta, tokens, tok, sem)
    plan = weight_plan(meta, pieces)
    core = meta[CORE]

    @pl.loop(0, COLS)
    def _(c):
        for k in range(NNZ):
            for src, row, slot in plan:
                wts[c, k, slot] = src[row, c, k]

    pltpu.make_async_copy(tok, tok, sem).wait()

    def total(c, dims):
        acc = None
        for k in range(NNZ):
            part = dot(tok[meta[c * NNZ + k]], wts[c, k].reshape(BS, BS), dims)
            acc = part if acc is None else acc + part
        return acc

    @pl.when(core == 0)
    def _():
        @pl.loop(0, COLS)
        def _(c):
            p = total(c, ((1,), (0,)))
            pre[:, lanes(c)] = p
            t = jnp.tanh(root_two_pi * (p + cubic_coef * p * p * p))
            out[:, lanes(c)] = (0.5 * p * (1.0 + t)).astype(BF16)

    @pl.when(core != 0)
    def _():
        @pl.loop(0, COLS)
        def _(c):
            out[:, lanes(c)] = total(c, ((1,), (1,))).astype(BF16)

    top[...] = out[:PW]
    bot[...] = out[TOK - PW :]


def forward(meta, tokens, pieces):
    wide = COLS * BS
    outs = [((TOK, wide), F32), ((TOK, wide), BF16), ((PW, wide), BF16), ((PW, wide), BF16)]
    outs += [((COLS, NNZ, 16, 16, BS), BF16), ((16, TOK, BS), BF16)]
    return local(
        forward_kernel,
        "forward",
        outs,
        (meta, *tokens, *pieces),
        [pltpu.SemaphoreType.DMA],
        flops=2 * TOK * BS * BS * NNZ * COLS,
        hbm=range(1, 10),
    )


def shifted_rows(mid, up, down, cols):
    cells = lax.broadcasted_iota(jnp.int32, (PW, BS), 0)
    out = []
    for row in [up[:, cols]] + [mid[i * PW : (i + 1) * PW, cols] for i in range(4)] + [down[:, cols]]:
        row = row.astype(F32)
        left = jnp.where(cells == 0, 0.0, pltpu.roll(row, 1, 0))
        right = jnp.where(cells == PW - 1, 0.0, pltpu.roll(row, PW - 1, 0))
        out.append((left, row, right))
    return out


def backward_kernel(meta, tok, got, mine, up, down, pre, taps, *refs):
    g0, m1, m3, g1, g3, pgrad, conv, lhs, res, slab, moved, stage, sems = refs
    core, x, y = meta[CORE], meta[XPOS], meta[YPOS]
    is_in = core == 0
    slab[...] = jnp.zeros_like(slab)
    here = jnp.where(is_in, y, x)
    far = jnp.where(is_in, NX, 1)
    near = jnp.where(is_in, 1, NY)

    @pl.loop(0, COLS)
    def _(c):
        cols = lanes(c)
        for i, rows in enumerate(shifted_rows(got, up, down, cols)):
            for b in range(3):
                moved[3 * i + b] = rows[b]
        tap = [jnp.where(is_in, taps[8 - j : 9 - j, cols], taps[j : j + 1, cols]) for j in range(9)]
        for i in range(4):
            acc = jnp.zeros((PW, BS), F32)
            for a in range(3):
                for b in range(3):
                    acc += tap[3 * a + b] * moved[3 * (i + a) + b]
            conv[i * PW : (i + 1) * PW] = acc

        @pl.when(is_in)
        def _():
            p = pre[:, cols]
            t = jnp.tanh(root_two_pi * (p + cubic_coef * p * p * p))
            slope = 0.5 * (1.0 + t) + 0.5 * p * (1.0 - t * t) * root_two_pi * (
                1.0 + 3.0 * cubic_coef * p * p
            )
            lhs[...] = (conv[...] * slope).astype(BF16)
            pgrad[:, cols] = lhs[...]
            for k in range(NNZ):
                part = dot(tok[meta[c * NNZ + k]], lhs[...], ((0,), (0,))) * loss_scale
                res[k] = part.astype(BF16).reshape(16, 16, BS)

        @pl.when(core != 0)
        def _():
            lhs[...] = conv[...].astype(BF16)
            for k in range(NNZ):
                part = dot(lhs[...], tok[meta[c * NNZ + k]], ((0,), (0,))) * loss_scale
                res[k] = part.astype(BF16).reshape(16, 16, BS)
            sums = []
            for a in range(3):
                for b in range(3):
                    acc = jnp.zeros((PW, BS), F32)
                    for i in range(4):
                        acc += moved[3 * (i + a) + b] * mine[i * PW : (i + 1) * PW, cols].astype(F32)
                    sums.append(jnp.sum(acc, axis=0, keepdims=True))
            rows = jnp.concatenate(sums + [jnp.zeros((7, BS), F32)], axis=0) * loss_scale
            slab[...] = rows.astype(BF16)

        def emit(out, d, at):
            start = (here + d) % 4 * far
            for k in range(NNZ):
                for s in range(4):
                    stage[d, c, k * 4 + s] = res[k, start + s * near]
            stage[d, c, KERN] = slab[...]
            pltpu.make_async_copy(stage.at[d, c], out.at[at], sems.at[d]).start()

        emit(g0, 0, c)

        @pl.when(c < SPLIT)
        def _():
            emit(m1, 2, c)
            emit(g1, 1, c)
            emit(m3, 3, c + SPLIT)

        @pl.when(c >= SPLIT)
        def _():
            emit(m3, 2, c - SPLIT)
            emit(m1, 1, c)
            emit(g3, 3, c - SPLIT)

    for d in range(4):
        pltpu.make_async_copy(stage.at[d], g0, sems.at[d]).wait()


def backward(meta, tok, got, mine, up, down, pre, taps):
    full, part = (COLS, KERN + 1, 16, BS), (SPLIT, KERN + 1, 16, BS)
    outs = [(full, BF16)] * 3 + [(part, BF16)] * 2 + [((TOK, COLS * BS), BF16)]
    scratch = [
        pltpu.VMEM((TOK, BS), F32),
        pltpu.VMEM((TOK, BS), BF16),
        pltpu.VMEM((NNZ, 16, 16, BS), BF16),
        pltpu.VMEM((16, BS), BF16),
        pltpu.VMEM((18, PW, BS), F32),
        pltpu.VMEM((4, COLS, KERN + 1, 16, BS), BF16),
        pltpu.SemaphoreType.DMA((4,)),
    ]
    args = (meta, tok, got, mine, up, down, pre, taps)
    return local(
        backward_kernel,
        "backward",
        outs,
        args,
        scratch,
        flops=2 * TOK * BS * BS * NNZ * COLS,
        hbm_out=range(5),
    )


def token_grad_kernel(meta, pgrad, wts, keep, send, acc):
    @pl.when(meta[CORE] == 0)
    def _():
        acc[...] = jnp.zeros_like(acc)

        @pl.loop(0, COLS, unroll=2)
        def _(c):
            for k in range(NNZ):
                wt = wts[c, k].reshape(BS, BS)
                acc[meta[c * NNZ + k]] += dot(pgrad[:, lanes(c)], wt, ((1,), (1,)))

        @pl.loop(0, 16)
        def _(r):
            keep[r] = acc[r, :128].astype(BF16)
            send[r] = acc[r, 128:].astype(BF16)


def token_grad(meta, pgrad, wts):
    return local(
        token_grad_kernel,
        "tokengrad",
        [((16, 128, BS), BF16)] * 2,
        (meta, pgrad, wts),
        [pltpu.VMEM((16, TOK, BS), F32)],
        flops=2 * TOK * BS * BS * NNZ * COLS,
    )


def gather_sum_kernel(meta, parts, out, flag):
    flag[...] = jnp.zeros_like(flag)
    for b in range(2):
        total = parts[b].astype(F32)
        for z in range(1, NZ):
            total += parts[2 * z + b].astype(F32)
        out[:, b * BS : (b + 1) * BS] = total.astype(BF16)


def relay_kernel(meta, g1, g3, m1, m3, _, o1, o3):
    for out, own, got in ((o1, g1, m1), (o3, g3, m3)):

        @pl.loop(0, SPLIT)
        def _(c):
            for k in range(KERN):
                out[c, k] = (own[c, k].astype(F32) + got[c, k].astype(F32)).astype(BF16)
            out[c, KERN] = own[c, KERN]
            out[c, KERN + 1] = got[c, KERN]


def first_sum_kernel(meta, own, m1, m3, p1, p3, *outs):
    here = jnp.where(meta[CORE] == 0, meta[XPOS], meta[YPOS])

    for shift, relayed, direct in ((0, p1, m3), (SPLIT, p3, m1)):

        @pl.loop(0, SPLIT)
        def _(c):
            at, got = c + shift, c + SPLIT
            near = relayed[c, KERN].astype(F32) + direct[got, KERN].astype(F32)
            far = own[at, KERN].astype(F32) + relayed[c, KERN + 1].astype(F32)
            for d in range(4):
                s = (here + d) % 4
                for k in range(NNZ):
                    total = own[at, k * 4 + s].astype(F32) + relayed[c, k * 4 + s].astype(F32)
                    outs[d][at, k] = (total + direct[got, k * 4 + s].astype(F32)).astype(BF16)
                outs[d][at, NNZ] = (far + near).astype(BF16)


def second_sum_kernel(meta, own, prev, nxt, far, keep, send):
    first_core = meta[CORE] == 0

    @pl.loop(0, COLS)
    def _(c):
        for k in range(NNZ + 1):
            a, b, e, f = (r[c, k].astype(F32) for r in (own, prev, nxt, far))
            total = ((a + f) + (b + e)).astype(BF16)
            low, high = total[:8], total[8:]
            if k < NNZ:
                keep[c, k] = jnp.where(first_core, low, high)
                send[c, k] = jnp.where(first_core, high, low)
            else:
                for out in (keep, send):
                    out[c, NNZ] = low
                    out[c, NNZ + 1] = high


def place_kernel(meta, keep, got, _, win, wout, kern):
    is_in = meta[CORE] == 0

    @pl.loop(0, NNZ)
    def _(k):
        mine = jnp.stack([keep[c, k].astype(F32) for c in range(COLS)], axis=0)
        its = jnp.stack([got[c, k].astype(F32) for c in range(COLS)], axis=0)
        mine, its = jnp.swapaxes(mine, 0, 1), jnp.swapaxes(its, 0, 1)
        win[:, k] = jnp.where(is_in, mine, its)
        wout[:, k] = jnp.where(is_in, its, mine)

    for c in range(COLS):
        rows = [jnp.where(is_in, got[c, NNZ + i], keep[c, NNZ + i]).astype(F32) for i in range(2)]
        kern[:, c * BS : (c + 1) * BS] = jnp.concatenate(rows, axis=0)[:9]


def on_device(tokens, cotangent, weight_in, weight_out, mix_kernel, block_rows):
    row, crop, z = lax.axis_index("rows"), lax.axis_index("crop"), lax.axis_index("hid")
    core, x, ylo = row % 2, row // 2 % NX, row // 8
    place = jnp.stack([core, x, crop * 2 + ylo, ylo, z]).astype(jnp.int32)
    meta = jnp.concatenate([block_rows.reshape(-1), place])
    is_in = core == 0

    def side(a, b):
        mine, theirs = jnp.where(is_in, a, b), jnp.where(is_in, b, a)
        got = to_partner(theirs)
        return jnp.where(is_in, mine, got), jnp.where(is_in, got, mine)

    own = jnp.stack(side(*(w.transpose(1, 2, 0, 3) for w in (weight_in, weight_out))))
    t0 = jnp.concatenate(side(tokens.reshape(128, 512), cotangent.reshape(128, 512)))

    wa = by_core(own, (0, 1), (0, -1))
    wb = by_core(own, (-1, 0), (1, 0))
    zr1, zl1 = along_z(t0, 1), along_z(t0, -1)
    wc = by_core(hold(meta, own, wa, wb, zr1, zl1), (0, -1), (0, 1))
    wd = by_core(wa, (1, 0), (-1, 0))
    zr2, zl2 = along_z(zr1, 1), along_z(zl1, -1)
    cuts = [((1, *own.shape[1:]), BF16)] * 2
    low, high = local(cut_kernel, "cut", cuts, (meta, wa, wc, wd, zr2, zl2))
    wf = by_core(low, (0, 1), (0, -1))
    wg = by_core(high, (0, -1), (0, 1))
    we = by_core(wc, (-1, 0), (1, 0))
    zr3, zl3 = along_z(zr2, 1), along_z(zl2, -1)
    wh = by_core(wf, (1, 0), (-1, 0))
    wi = by_core(wg, (-1, 0), (1, 0))
    zr4, zl4 = along_z(zr3[:128], 1), along_z(zl3[128:], -1)
    pieces = (own, wa, wb, wc, wd, we, wf, wg, wh, wi)
    token_pieces = (t0, zr1, zr2, zr3, zl1, zl2, zl3, zr4, zl4)

    pre, out, top, bot, wts, tok = forward(meta, token_pieces, pieces)
    got = to_partner(out)
    up, down = to_next_chip(bot, 1), to_next_chip(top, -1)
    g0, m1, m3, g1, g3, pgrad = backward(meta, tok, got, out, up, down, pre, mix_kernel)
    m1, m3 = first(m1, 1), first(m3, -1)

    keep, send = token_grad(meta, pgrad, wts)
    terms = jnp.where(is_in, keep, to_partner(send))
    relayed = [((SPLIT, KERN + 2, 16, BS), BF16)] * 2
    r1, r3 = local(relay_kernel, "relay", relayed, (meta, g1, g3, m1, m3, terms), hbm=(5,))
    terms = lax.all_to_all(terms, "hid", 0, 0, tiled=True)
    outs = [((128, 512), BF16), ((8, 128), F32)]
    grad_tokens, flag = local(gather_sum_kernel, "gathersum", outs, (meta, terms))

    h = local(
        first_sum_kernel,
        "firstsum",
        [((COLS, NNZ + 1, 16, BS), BF16)] * 4,
        (meta, g0, m1, m3, first(r1, 1), first(r3, -1)),
    )
    last = (h[0], second(h[1], 1), second(h[3], -1), second(h[2], 2))
    shape = ((COLS, NNZ + 2, 8, BS), BF16)
    kept, sent = local(second_sum_kernel, "secondsum", [shape] * 2, (meta, *last))
    out_shape = ((8, NNZ, 8, BS), F32)
    win, wout, kern = local(
        place_kernel,
        "place",
        [out_shape, out_shape, ((9, 8 * BS), F32)],
        (meta, kept, to_partner(sent), flag),
    )
    grad_tokens = grad_tokens.reshape(1, 2, PW, 512)
    return grad_tokens, win.transpose(0, 2, 1, 3), wout.transpose(0, 2, 1, 3), kern


def solution(mesh):
    placed = (
        P("crop", "rows", None, "hid"),
        P("crop", "rows", None, "hid"),
        P("rows", "hid", None, None),
        P("rows", "hid", None, None),
        P(None, "hid"),
        P("hid", None),
    )
    return jax.shard_map(
        on_device,
        mesh=mesh,
        in_specs=placed,
        out_specs=(
            P("crop", "rows", None, "hid"),
            P(("crop", "rows"), "hid", None, None),
            P(("crop", "rows"), "hid", None, None),
            P(None, "hid"),
        ),
        check_vma=False,
    )
```

```python
import jax
import jax.numpy as jnp
from jax import lax
from jax.experimental import pallas as pl
from jax.experimental.pallas import tpu as pltpu
from jax.sharding import PartitionSpec as P

root_two_pi = 0.7978845608
cubic_coef = 0.044715
loss_scale = 0.03125

F32, BF16 = jnp.float32, jnp.bfloat16
NX, NY, NZ = 4, 4, 8
COLS, NNZ, BS, PW = 8, 5, 256, 64
TOK, KERN, SPLIT, PARTS = 256, 20, 4, 2
CORE, XPOS, YPOS, YLO, ZPOS = 40, 41, 42, 43, 44
HBM = pl.BlockSpec(memory_space=pltpu.MemorySpace.HBM)
VMEM = pl.BlockSpec(memory_space=pltpu.VMEM)
SMEM = pl.BlockSpec(memory_space=pltpu.SMEM)


def by_core(value, step0, step1):
    pairs = []
    for y in range(NY):
        for x in range(NX):
            for c, (dy, dx) in enumerate((step0, step1)):
                target = (y + dy) % NY * 8 + (x + dx) % NX * 2 + c
                pairs.append((y * 8 + x * 2 + c, target))
    return lax.ppermute(value, ("crop", "rows"), pairs)


def first(value, step):
    return by_core(value, (step, 0), (0, step))


def second(value, step):
    return by_core(value, (0, step), (step, 0))


def to_partner(value):
    return lax.ppermute(value, "rows", [(r, r ^ 1) for r in range(16)])


def to_next_chip(value, step):
    pairs = []
    for q in range(8):
        if 0 <= q + step < 8:
            pairs += [(q * 2 + c, (q + step) * 2 + 1 - c) for c in range(2)]
    return lax.ppermute(value, "rows", pairs)


def along_z(value, step):
    return lax.ppermute(value, "hid", [(z, (z + step) % NZ) for z in range(NZ)])


def dot(a, b, dims):
    return lax.dot_general(a, b, (dims, ((), ())), preferred_element_type=F32)


def local(kernel, name, outs, args, scratch=(), flops=2**20, hbm=(), hbm_out=()):
    shapes = [
        pltpu.HBM(s, t) if i in hbm_out else jax.ShapeDtypeStruct(s, t) for i, (s, t) in enumerate(outs)
    ]
    size = sum(a.size * a.dtype.itemsize for a in args[1:])
    return pl.pallas_call(
        kernel,
        out_shape=shapes,
        in_specs=[SMEM] + [HBM if i in hbm else VMEM for i in range(1, len(args))],
        out_specs=[HBM if i in hbm_out else VMEM for i in range(len(outs))],
        scratch_shapes=list(scratch),
        compiler_params=pltpu.CompilerParams(vmem_limit_bytes=20 * 2**20),
        cost_estimate=pl.CostEstimate(flops=flops, transcendentals=0, bytes_accessed=size),
        name=name,
    )(*args)


def lanes(c):
    return pl.ds(pl.multiple_of(c * BS, BS), BS)


def start_tokens(meta, pieces, buf, sem):
    z = meta[ZPOS]
    own, r1, r2, r3, l1, l2, l3, r4, l4 = pieces
    plan = [(own, 0, 0), (r1, 7, 0), (r2, 6, 0), (r3, 5, 0), (l1, 1, 0), (l2, 2, 0), (l3, 3, 0)]
    for src, d, at in plan + [(r4, 4, 0), (l4, 4, 128)]:
        h = (z + d) % NZ
        for part in range(2):
            rows = pl.ds(at, src.shape[0])
            target = buf.at[2 * h + part, rows]
            pltpu.make_async_copy(src.at[:, pl.ds(part * BS, BS)], target, sem).start()


def weight_plan(meta, pieces):
    core, x, ylo = meta[CORE], meta[XPOS], meta[YLO]
    own, a, b, c, d, e, f, g, h, i = pieces
    here, there = ylo * NX, (1 - ylo) * NX
    side = jnp.where(core == 0, NX - 1, 1)
    at = lambda base, step: base + (x + step) % NX
    slots = [
        (own, at(here, 0)),
        (a, at(here, side)),
        (b, at(there, 0)),
        (c, at(here, NX - side)),
        (d, at(there, side)),
        (e, at(there, NX - side)),
    ]
    plan = [(src, s, 2 * j + s) for src, j in slots for s in range(2)]
    for j, low, high in ((at(here, 2), f, g), (at(there, 2), h, i)):
        plan += [(low, 0, 2 * j), (high, 0, 2 * j + 1)]
    return plan


def hold(meta, value, *others):
    def kernel(meta, src, *refs):
        refs[-1][...] = src[...]

    outs = [(value.shape, value.dtype)]
    return local(kernel, "hold", outs, (meta, value, *others))[0]


def cut_kernel(meta, a, c, *refs):
    low, high = refs[-2:]
    low[...] = a[:1]
    high[...] = c[1:]


def forward_kernel(meta, *refs):
    tokens, pieces, outs = refs[:9], refs[9:19], refs[19:]
    pre, out, top, bot, wts, tok, sem = outs
    start_tokens(meta, tokens, tok, sem)
    plan = weight_plan(meta, pieces)
    core = meta[CORE]

    @pl.loop(0, COLS)
    def _(c):
        for k in range(NNZ):
            for src, row, slot in plan:
                wts[c, k, slot] = src[row, c, k]

    pltpu.make_async_copy(tok, tok, sem).wait()

    def total(c, dims):
        acc = None
        for k in range(NNZ):
            part = dot(tok[meta[c * NNZ + k]], wts[c, k].reshape(BS, BS), dims)
            acc = part if acc is None else acc + part
        return acc

    @pl.when(core == 0)
    def _():
        @pl.loop(0, COLS)
        def _(c):
            p = total(c, ((1,), (0,)))
            pre[:, lanes(c)] = p
            t = jnp.tanh(root_two_pi * (p + cubic_coef * p * p * p))
            out[:, lanes(c)] = (0.5 * p * (1.0 + t)).astype(BF16)

    @pl.when(core != 0)
    def _():
        @pl.loop(0, COLS)
        def _(c):
            out[:, lanes(c)] = total(c, ((1,), (1,))).astype(BF16)

    top[...] = out[:PW]
    bot[...] = out[TOK - PW :]


def forward(meta, tokens, pieces):
    wide = COLS * BS
    outs = [((TOK, wide), F32), ((TOK, wide), BF16), ((PW, wide), BF16), ((PW, wide), BF16)]
    outs += [((COLS, NNZ, 16, 16, BS), BF16), ((16, TOK, BS), BF16)]
    return local(
        forward_kernel,
        "forward",
        outs,
        (meta, *tokens, *pieces),
        [pltpu.SemaphoreType.DMA],
        flops=2 * TOK * BS * BS * NNZ * COLS,
        hbm=range(1, 10),
    )


def shifted_rows(mid, up, down, cols):
    cells = lax.broadcasted_iota(jnp.int32, (PW, BS), 0)
    out = []
    for row in [up[:, cols]] + [mid[i * PW : (i + 1) * PW, cols] for i in range(4)] + [down[:, cols]]:
        row = row.astype(F32)
        left = jnp.where(cells == 0, 0.0, pltpu.roll(row, 1, 0))
        right = jnp.where(cells == PW - 1, 0.0, pltpu.roll(row, PW - 1, 0))
        out.append((left, row, right))
    return out


def backward_kernel(meta, tok, got, mine, up, down, pre, taps, *refs):
    g0, m1, m3, g1, g3, pgrad, conv, lhs, res, slab, moved, stage, sems = refs
    core, x, y = meta[CORE], meta[XPOS], meta[YPOS]
    is_in = core == 0
    slab[...] = jnp.zeros_like(slab)
    here = jnp.where(is_in, y, x)
    far = jnp.where(is_in, NX, 1)
    near = jnp.where(is_in, 1, NY)

    @pl.loop(0, COLS)
    def _(c):
        cols = lanes(c)
        for i, rows in enumerate(shifted_rows(got, up, down, cols)):
            for b in range(3):
                moved[3 * i + b] = rows[b]
        tap = [jnp.where(is_in, taps[8 - j : 9 - j, cols], taps[j : j + 1, cols]) for j in range(9)]
        for i in range(4):
            acc = jnp.zeros((PW, BS), F32)
            for a in range(3):
                for b in range(3):
                    acc += tap[3 * a + b] * moved[3 * (i + a) + b]
            conv[i * PW : (i + 1) * PW] = acc

        @pl.when(is_in)
        def _():
            p = pre[:, cols]
            t = jnp.tanh(root_two_pi * (p + cubic_coef * p * p * p))
            slope = 0.5 * (1.0 + t) + 0.5 * p * (1.0 - t * t) * root_two_pi * (
                1.0 + 3.0 * cubic_coef * p * p
            )
            lhs[...] = (conv[...] * slope).astype(BF16)
            pgrad[:, cols] = lhs[...]
            for k in range(NNZ):
                part = dot(tok[meta[c * NNZ + k]], lhs[...], ((0,), (0,))) * loss_scale
                res[k] = part.astype(BF16).reshape(16, 16, BS)

        @pl.when(core != 0)
        def _():
            lhs[...] = conv[...].astype(BF16)
            for k in range(NNZ):
                part = dot(lhs[...], tok[meta[c * NNZ + k]], ((0,), (0,))) * loss_scale
                res[k] = part.astype(BF16).reshape(16, 16, BS)
            sums = []
            for a in range(3):
                for b in range(3):
                    acc = jnp.zeros((PW, BS), F32)
                    for i in range(4):
                        acc += moved[3 * (i + a) + b] * mine[i * PW : (i + 1) * PW, cols].astype(F32)
                    sums.append(jnp.sum(acc, axis=0, keepdims=True))
            rows = jnp.concatenate(sums + [jnp.zeros((7, BS), F32)], axis=0) * loss_scale
            slab[...] = rows.astype(BF16)

        def emit(out, d, at):
            start = (here + d) % 4 * far
            for k in range(NNZ):
                for s in range(4):
                    stage[d, c, k * 4 + s] = res[k, start + s * near]
            stage[d, c, KERN] = slab[...]
            pltpu.make_async_copy(stage.at[d, c], out.at[at], sems.at[d]).start()

        emit(g0, 0, c)

        @pl.when(c < SPLIT)
        def _():
            emit(m1, 2, c)
            emit(g1, 1, c)
            emit(m3, 3, c + SPLIT)

        @pl.when(c >= SPLIT)
        def _():
            emit(m3, 2, c - SPLIT)
            emit(m1, 1, c)
            emit(g3, 3, c - SPLIT)

    for d in range(4):
        pltpu.make_async_copy(stage.at[d], g0, sems.at[d]).wait()


def backward(meta, tok, got, mine, up, down, pre, taps):
    full, part = (COLS, KERN + 1, 16, BS), (SPLIT, KERN + 1, 16, BS)
    outs = [(full, BF16)] * 3 + [(part, BF16)] * 2 + [((TOK, COLS * BS), BF16)]
    scratch = [
        pltpu.VMEM((TOK, BS), F32),
        pltpu.VMEM((TOK, BS), BF16),
        pltpu.VMEM((NNZ, 16, 16, BS), BF16),
        pltpu.VMEM((16, BS), BF16),
        pltpu.VMEM((18, PW, BS), F32),
        pltpu.VMEM((4, COLS, KERN + 1, 16, BS), BF16),
        pltpu.SemaphoreType.DMA((4,)),
    ]
    args = (meta, tok, got, mine, up, down, pre, taps)
    return local(
        backward_kernel,
        "backward",
        outs,
        args,
        scratch,
        flops=2 * TOK * BS * BS * NNZ * COLS,
        hbm_out=range(5),
    )


def token_grad_kernel(meta, pgrad, wts, keep, *refs):
    *sends, acc = refs

    @pl.when(meta[CORE] == 0)
    def _():
        acc[...] = jnp.zeros_like(acc)

        @pl.loop(0, COLS, unroll=2)
        def _(c):
            for k in range(NNZ):
                wt = wts[c, k].reshape(BS, BS)
                acc[meta[c * NNZ + k]] += dot(pgrad[:, lanes(c)], wt, ((1,), (1,)))

        size = 16 // len(sends)
        for i, send in enumerate(sends):

            @pl.loop(0, size)
            def _(r):
                keep[r + i * size] = acc[r + i * size, :128].astype(BF16)
                send[r] = acc[r + i * size, 128:].astype(BF16)


def token_grad(meta, pgrad, wts):
    return local(
        token_grad_kernel,
        "tokengrad",
        [((16, 128, BS), BF16)] + [((16 // PARTS, 128, BS), BF16)] * PARTS,
        (meta, pgrad, wts),
        [pltpu.VMEM((16, TOK, BS), F32)],
        flops=2 * TOK * BS * BS * NNZ * COLS,
    )


def gather_sum_kernel(meta, parts, out, flag):
    flag[...] = jnp.zeros_like(flag)
    for b in range(2):
        total = parts[b].astype(F32)
        for z in range(1, NZ):
            total += parts[2 * z + b].astype(F32)
        out[:, b * BS : (b + 1) * BS] = total.astype(BF16)


def relay_kernel(meta, g1, g3, m1, m3, _, o1, o3):
    for out, own, got in ((o1, g1, m1), (o3, g3, m3)):

        @pl.loop(0, SPLIT)
        def _(c):
            for k in range(KERN):
                out[c, k] = (own[c, k].astype(F32) + got[c, k].astype(F32)).astype(BF16)
            out[c, KERN] = own[c, KERN]
            out[c, KERN + 1] = got[c, KERN]


def first_sum_kernel(meta, own, m1, m3, p1, p3, *outs):
    here = jnp.where(meta[CORE] == 0, meta[XPOS], meta[YPOS])

    for shift, relayed, direct in ((0, p1, m3), (SPLIT, p3, m1)):

        @pl.loop(0, SPLIT)
        def _(c):
            at, got = c + shift, c + SPLIT
            near = relayed[c, KERN].astype(F32) + direct[got, KERN].astype(F32)
            far = own[at, KERN].astype(F32) + relayed[c, KERN + 1].astype(F32)
            for d in range(4):
                s = (here + d) % 4
                for k in range(NNZ):
                    total = own[at, k * 4 + s].astype(F32) + relayed[c, k * 4 + s].astype(F32)
                    outs[d][at, k] = (total + direct[got, k * 4 + s].astype(F32)).astype(BF16)
                outs[d][at, NNZ] = (far + near).astype(BF16)


def second_sum_kernel(meta, own, prev, nxt, far, keep, send):
    first_core = meta[CORE] == 0

    @pl.loop(0, COLS)
    def _(c):
        for k in range(NNZ + 1):
            a, b, e, f = (r[c, k].astype(F32) for r in (own, prev, nxt, far))
            total = ((a + f) + (b + e)).astype(BF16)
            low, high = total[:8], total[8:]
            if k < NNZ:
                keep[c, k] = jnp.where(first_core, low, high)
                send[c, k] = jnp.where(first_core, high, low)
            else:
                for out in (keep, send):
                    out[c, NNZ] = low
                    out[c, NNZ + 1] = high


def place_kernel(meta, keep, got, _, win, wout, kern):
    is_in = meta[CORE] == 0

    @pl.loop(0, NNZ)
    def _(k):
        mine = jnp.stack([keep[c, k].astype(F32) for c in range(COLS)], axis=0)
        its = jnp.stack([got[c, k].astype(F32) for c in range(COLS)], axis=0)
        mine, its = jnp.swapaxes(mine, 0, 1), jnp.swapaxes(its, 0, 1)
        win[:, k] = jnp.where(is_in, mine, its)
        wout[:, k] = jnp.where(is_in, its, mine)

    for c in range(COLS):
        rows = [jnp.where(is_in, got[c, NNZ + i], keep[c, NNZ + i]).astype(F32) for i in range(2)]
        kern[:, c * BS : (c + 1) * BS] = jnp.concatenate(rows, axis=0)[:9]


def on_device(tokens, cotangent, weight_in, weight_out, mix_kernel, block_rows):
    row, crop, z = lax.axis_index("rows"), lax.axis_index("crop"), lax.axis_index("hid")
    core, x, ylo = row % 2, row // 2 % NX, row // 8
    place = jnp.stack([core, x, crop * 2 + ylo, ylo, z]).astype(jnp.int32)
    meta = jnp.concatenate([block_rows.reshape(-1), place])
    is_in = core == 0

    def side(a, b):
        mine, theirs = jnp.where(is_in, a, b), jnp.where(is_in, b, a)
        got = to_partner(theirs)
        return jnp.where(is_in, mine, got), jnp.where(is_in, got, mine)

    own = jnp.stack(side(*(w.transpose(1, 2, 0, 3) for w in (weight_in, weight_out))))
    t0 = jnp.concatenate(side(tokens.reshape(128, 512), cotangent.reshape(128, 512)))

    wa = by_core(own, (0, 1), (0, -1))
    wb = by_core(own, (-1, 0), (1, 0))
    zr1, zl1 = along_z(t0, 1), along_z(t0, -1)
    wc = by_core(hold(meta, own, wa, wb, zr1, zl1), (0, -1), (0, 1))
    wd = by_core(wa, (1, 0), (-1, 0))
    zr2, zl2 = along_z(zr1, 1), along_z(zl1, -1)
    cuts = [((1, *own.shape[1:]), BF16)] * 2
    low, high = local(cut_kernel, "cut", cuts, (meta, wa, wc, wd, zr2, zl2))
    wf = by_core(low, (0, 1), (0, -1))
    wg = by_core(high, (0, -1), (0, 1))
    we = by_core(wc, (-1, 0), (1, 0))
    zr3, zl3 = along_z(zr2, 1), along_z(zl2, -1)
    wh = by_core(wf, (1, 0), (-1, 0))
    wi = by_core(wg, (-1, 0), (1, 0))
    zr4, zl4 = along_z(zr3[:128], 1), along_z(zl3[128:], -1)
    pieces = (own, wa, wb, wc, wd, we, wf, wg, wh, wi)
    token_pieces = (t0, zr1, zr2, zr3, zl1, zl2, zl3, zr4, zl4)

    pre, out, top, bot, wts, tok = forward(meta, token_pieces, pieces)
    got = to_partner(out)
    up, down = to_next_chip(bot, 1), to_next_chip(top, -1)
    g0, m1, m3, g1, g3, pgrad = backward(meta, tok, got, out, up, down, pre, mix_kernel)
    m1, m3 = first(m1, 1), first(m3, -1)

    keep, *sends = token_grad(meta, pgrad, wts)
    terms = jnp.where(is_in, keep, jnp.concatenate([to_partner(send) for send in sends]))
    relayed = [((SPLIT, KERN + 2, 16, BS), BF16)] * 2
    r1, r3 = local(relay_kernel, "relay", relayed, (meta, g1, g3, m1, m3, terms), hbm=(5,))
    terms = lax.all_to_all(terms, "hid", 0, 0, tiled=True)
    outs = [((128, 512), BF16), ((8, 128), F32)]
    grad_tokens, flag = local(gather_sum_kernel, "gathersum", outs, (meta, terms))

    h = local(
        first_sum_kernel,
        "firstsum",
        [((COLS, NNZ + 1, 16, BS), BF16)] * 4,
        (meta, g0, m1, m3, first(r1, 1), first(r3, -1)),
    )
    last = (h[0], second(h[1], 1), second(h[3], -1), second(h[2], 2))
    shape = ((COLS, NNZ + 2, 8, BS), BF16)
    kept, sent = local(second_sum_kernel, "secondsum", [shape] * 2, (meta, *last))
    out_shape = ((8, NNZ, 8, BS), F32)
    win, wout, kern = local(
        place_kernel,
        "place",
        [out_shape, out_shape, ((9, 8 * BS), F32)],
        (meta, kept, to_partner(sent), flag),
    )
    grad_tokens = grad_tokens.reshape(1, 2, PW, 512)
    return grad_tokens, win.transpose(0, 2, 1, 3), wout.transpose(0, 2, 1, 3), kern


def solution(mesh):
    placed = (
        P("crop", "rows", None, "hid"),
        P("crop", "rows", None, "hid"),
        P("rows", "hid", None, None),
        P("rows", "hid", None, None),
        P(None, "hid"),
        P("hid", None),
    )
    return jax.shard_map(
        on_device,
        mesh=mesh,
        in_specs=placed,
        out_specs=(
            P("crop", "rows", None, "hid"),
            P(("crop", "rows"), "hid", None, None),
            P(("crop", "rows"), "hid", None, None),
            P(None, "hid"),
        ),
        check_vma=False,
    )
```

```python
import jax
import jax.numpy as jnp
from jax import lax
from jax.experimental import pallas as pl
from jax.experimental.pallas import tpu as pltpu
from jax.sharding import PartitionSpec as P

root_two_pi = 0.7978845608
cubic_coef = 0.044715
loss_scale = 0.03125

F32, BF16 = jnp.float32, jnp.bfloat16
NX, NY, NZ = 4, 4, 8
COLS, NNZ, BS, PW = 8, 5, 256, 64
TOK, KERN, SPLIT, PARTS = 256, 20, 4, 2
CORE, XPOS, YPOS, YLO, ZPOS = 40, 41, 42, 43, 44
HBM = pl.BlockSpec(memory_space=pltpu.MemorySpace.HBM)
VMEM = pl.BlockSpec(memory_space=pltpu.VMEM)
SMEM = pl.BlockSpec(memory_space=pltpu.SMEM)


def by_core(value, step0, step1):
    pairs = []
    for y in range(NY):
        for x in range(NX):
            for c, (dy, dx) in enumerate((step0, step1)):
                target = (y + dy) % NY * 8 + (x + dx) % NX * 2 + c
                pairs.append((y * 8 + x * 2 + c, target))
    return lax.ppermute(value, ("crop", "rows"), pairs)


def first(value, step):
    return by_core(value, (step, 0), (0, step))


def second(value, step):
    return by_core(value, (0, step), (step, 0))


def to_partner(value):
    return lax.ppermute(value, "rows", [(r, r ^ 1) for r in range(16)])


def to_next_chip(value, step):
    pairs = []
    for q in range(8):
        if 0 <= q + step < 8:
            pairs += [(q * 2 + c, (q + step) * 2 + 1 - c) for c in range(2)]
    return lax.ppermute(value, "rows", pairs)


def along_z(value, step):
    return lax.ppermute(value, "hid", [(z, (z + step) % NZ) for z in range(NZ)])


def dot(a, b, dims):
    return lax.dot_general(a, b, (dims, ((), ())), preferred_element_type=F32)


def local(kernel, name, outs, args, scratch=(), flops=2**20, hbm=(), hbm_out=()):
    shapes = [
        pltpu.HBM(s, t) if i in hbm_out else jax.ShapeDtypeStruct(s, t) for i, (s, t) in enumerate(outs)
    ]
    size = sum(a.size * a.dtype.itemsize for a in args[1:])
    return pl.pallas_call(
        kernel,
        out_shape=shapes,
        in_specs=[SMEM] + [HBM if i in hbm else VMEM for i in range(1, len(args))],
        out_specs=[HBM if i in hbm_out else VMEM for i in range(len(outs))],
        scratch_shapes=list(scratch),
        compiler_params=pltpu.CompilerParams(vmem_limit_bytes=20 * 2**20),
        cost_estimate=pl.CostEstimate(flops=flops, transcendentals=0, bytes_accessed=size),
        name=name,
    )(*args)


def lanes(c):
    return pl.ds(pl.multiple_of(c * BS, BS), BS)


def start_tokens(meta, pieces, buf, sem):
    z = meta[ZPOS]
    own, r1, r2, r3, l1, l2, l3, r4, l4 = pieces
    plan = [(own, 0, 0), (r1, 7, 0), (r2, 6, 0), (r3, 5, 0), (l1, 1, 0), (l2, 2, 0), (l3, 3, 0)]
    for src, d, at in plan + [(r4, 4, 0), (l4, 4, 128)]:
        h = (z + d) % NZ
        for part in range(2):
            rows = pl.ds(at, src.shape[0])
            target = buf.at[2 * h + part, rows]
            pltpu.make_async_copy(src.at[:, pl.ds(part * BS, BS)], target, sem).start()


def weight_plan(meta, pieces):
    core, x, ylo = meta[CORE], meta[XPOS], meta[YLO]
    own, a, b, c, d, e, f, g, h, i = pieces
    here, there = ylo * NX, (1 - ylo) * NX
    side = jnp.where(core == 0, NX - 1, 1)
    at = lambda base, step: base + (x + step) % NX
    slots = [
        (own, at(here, 0)),
        (a, at(here, side)),
        (b, at(there, 0)),
        (c, at(here, NX - side)),
        (d, at(there, side)),
        (e, at(there, NX - side)),
    ]
    plan = [(src, s, 2 * j + s) for src, j in slots for s in range(2)]
    for j, low, high in ((at(here, 2), f, g), (at(there, 2), h, i)):
        plan += [(low, 0, 2 * j), (high, 0, 2 * j + 1)]
    return plan


def hold(meta, value, *others):
    def kernel(meta, src, *refs):
        refs[-1][...] = src[...]

    outs = [(value.shape, value.dtype)]
    return local(kernel, "hold", outs, (meta, value, *others))[0]


def cut_kernel(meta, a, c, *refs):
    low, high = refs[-2:]
    low[...] = a[:1]
    high[...] = c[1:]


def forward_kernel(meta, *refs):
    tokens, pieces, outs = refs[:9], refs[9:19], refs[19:]
    pre, out, top, bot, wts, tok, sem = outs
    start_tokens(meta, tokens, tok, sem)
    plan = weight_plan(meta, pieces)
    core = meta[CORE]

    @pl.loop(0, COLS)
    def _(c):
        for k in range(NNZ):
            for src, row, slot in plan:
                wts[c, k, slot] = src[row, c, k]

    pltpu.make_async_copy(tok, tok, sem).wait()

    def total(c, dims):
        acc = None
        for k in range(NNZ):
            part = dot(tok[meta[c * NNZ + k]], wts[c, k].reshape(BS, BS), dims)
            acc = part if acc is None else acc + part
        return acc

    @pl.when(core == 0)
    def _():
        @pl.loop(0, COLS)
        def _(c):
            p = total(c, ((1,), (0,)))
            pre[:, lanes(c)] = p
            t = jnp.tanh(root_two_pi * (p + cubic_coef * p * p * p))
            out[:, lanes(c)] = (0.5 * p * (1.0 + t)).astype(BF16)

    @pl.when(core != 0)
    def _():
        @pl.loop(0, COLS)
        def _(c):
            out[:, lanes(c)] = total(c, ((1,), (1,))).astype(BF16)

    top[...] = out[:PW]
    bot[...] = out[TOK - PW :]


def forward(meta, tokens, pieces):
    wide = COLS * BS
    outs = [((TOK, wide), F32), ((TOK, wide), BF16), ((PW, wide), BF16), ((PW, wide), BF16)]
    outs += [((COLS, NNZ, 16, 16, BS), BF16), ((16, TOK, BS), BF16)]
    return local(
        forward_kernel,
        "forward",
        outs,
        (meta, *tokens, *pieces),
        [pltpu.SemaphoreType.DMA],
        flops=2 * TOK * BS * BS * NNZ * COLS,
        hbm=range(1, 10),
    )


def shifted_rows(mid, up, down, cols):
    cells = lax.broadcasted_iota(jnp.int32, (PW, BS), 0)
    out = []
    for row in [up[:, cols]] + [mid[i * PW : (i + 1) * PW, cols] for i in range(4)] + [down[:, cols]]:
        row = row.astype(F32)
        left = jnp.where(cells == 0, 0.0, pltpu.roll(row, 1, 0))
        right = jnp.where(cells == PW - 1, 0.0, pltpu.roll(row, PW - 1, 0))
        out.append((left, row, right))
    return out


def backward_kernel(meta, tok, got, mine, up, down, pre, taps, *refs):
    g0, m1, m3, g1, g3, pgrad, conv, lhs, res, slab, moved, stage, sems = refs
    core, x, y = meta[CORE], meta[XPOS], meta[YPOS]
    is_in = core == 0
    slab[...] = jnp.zeros_like(slab)
    here = jnp.where(is_in, y, x)
    far = jnp.where(is_in, NX, 1)
    near = jnp.where(is_in, 1, NY)

    @pl.loop(0, COLS)
    def _(c):
        cols = lanes(c)
        for i, rows in enumerate(shifted_rows(got, up, down, cols)):
            for b in range(3):
                moved[3 * i + b] = rows[b]
        tap = [jnp.where(is_in, taps[8 - j : 9 - j, cols], taps[j : j + 1, cols]) for j in range(9)]
        for i in range(4):
            acc = jnp.zeros((PW, BS), F32)
            for a in range(3):
                for b in range(3):
                    acc += tap[3 * a + b] * moved[3 * (i + a) + b]
            conv[i * PW : (i + 1) * PW] = acc

        @pl.when(is_in)
        def _():
            p = pre[:, cols]
            t = jnp.tanh(root_two_pi * (p + cubic_coef * p * p * p))
            slope = 0.5 * (1.0 + t) + 0.5 * p * (1.0 - t * t) * root_two_pi * (
                1.0 + 3.0 * cubic_coef * p * p
            )
            lhs[...] = (conv[...] * slope).astype(BF16)
            pgrad[:, cols] = lhs[...]
            for k in range(NNZ):
                part = dot(tok[meta[c * NNZ + k]], lhs[...], ((0,), (0,))) * loss_scale
                res[k] = part.astype(BF16).reshape(16, 16, BS)

        @pl.when(core != 0)
        def _():
            lhs[...] = conv[...].astype(BF16)
            for k in range(NNZ):
                part = dot(lhs[...], tok[meta[c * NNZ + k]], ((0,), (0,))) * loss_scale
                res[k] = part.astype(BF16).reshape(16, 16, BS)
            sums = []
            for a in range(3):
                for b in range(3):
                    acc = jnp.zeros((PW, BS), F32)
                    for i in range(4):
                        acc += moved[3 * (i + a) + b] * mine[i * PW : (i + 1) * PW, cols].astype(F32)
                    sums.append(jnp.sum(acc, axis=0, keepdims=True))
            rows = jnp.concatenate(sums + [jnp.zeros((7, BS), F32)], axis=0) * loss_scale
            slab[...] = rows.astype(BF16)

        def emit(out, d, at):
            start = (here + d) % 4 * far
            for k in range(NNZ):
                for s in range(4):
                    stage[d, c, k * 4 + s] = res[k, start + s * near]
            stage[d, c, KERN] = slab[...]
            pltpu.make_async_copy(stage.at[d, c], out.at[at], sems.at[d]).start()

        emit(g0, 0, c)

        @pl.when(c < SPLIT)
        def _():
            emit(m1, 2, c)
            emit(g1, 1, c)
            emit(m3, 3, c + SPLIT)

        @pl.when(c >= SPLIT)
        def _():
            emit(m3, 2, c - SPLIT)
            emit(m1, 1, c)
            emit(g3, 3, c - SPLIT)

    for d in range(4):
        pltpu.make_async_copy(stage.at[d], g0, sems.at[d]).wait()


def backward(meta, tok, got, mine, up, down, pre, taps):
    full, part = (COLS, KERN + 1, 16, BS), (SPLIT, KERN + 1, 16, BS)
    outs = [(full, BF16)] * 3 + [(part, BF16)] * 2 + [((TOK, COLS * BS), BF16)]
    scratch = [
        pltpu.VMEM((TOK, BS), F32),
        pltpu.VMEM((TOK, BS), BF16),
        pltpu.VMEM((NNZ, 16, 16, BS), BF16),
        pltpu.VMEM((16, BS), BF16),
        pltpu.VMEM((18, PW, BS), F32),
        pltpu.VMEM((4, COLS, KERN + 1, 16, BS), BF16),
        pltpu.SemaphoreType.DMA((4,)),
    ]
    args = (meta, tok, got, mine, up, down, pre, taps)
    return local(
        backward_kernel,
        "backward",
        outs,
        args,
        scratch,
        flops=2 * TOK * BS * BS * NNZ * COLS,
        hbm_out=range(5),
    )


def token_grad_kernel(meta, pgrad, wts, keep, *refs):
    *sends, acc = refs

    @pl.when(meta[CORE] == 0)
    def _():
        acc[...] = jnp.zeros_like(acc)

        @pl.loop(0, COLS, unroll=2)
        def _(c):
            for k in range(NNZ):
                wt = wts[c, k].reshape(BS, BS)
                acc[meta[c * NNZ + k]] += dot(pgrad[:, lanes(c)], wt, ((1,), (1,)))

        size = 16 // len(sends)
        for i, send in enumerate(sends):

            @pl.loop(0, size)
            def _(r):
                keep[r + i * size] = acc[r + i * size, :128].astype(BF16)
                send[r] = acc[r + i * size, 128:].astype(BF16)


def token_grad(meta, pgrad, wts):
    return local(
        token_grad_kernel,
        "tokengrad",
        [((16, 128, BS), BF16)] + [((16 // PARTS, 128, BS), BF16)] * PARTS,
        (meta, pgrad, wts),
        [pltpu.VMEM((16, TOK, BS), F32)],
        flops=2 * TOK * BS * BS * NNZ * COLS,
    )


def gather_sum_kernel(meta, parts, out, flag):
    flag[...] = jnp.zeros_like(flag)
    for b in range(2):
        total = parts[b].astype(F32)
        for z in range(1, NZ):
            total += parts[2 * z + b].astype(F32)
        out[:, b * BS : (b + 1) * BS] = total.astype(BF16)


def relay_kernel(meta, s1, s3, m1, m3, _, o1, o3, g1, g3, sems):
    copies = [pltpu.make_async_copy(a, b, sems.at[i]) for i, (a, b) in enumerate(((s1, g1), (s3, g3)))]
    for copy in copies:
        copy.start()
    for copy in copies:
        copy.wait()
    for out, own, got in ((o1, g1, m1), (o3, g3, m3)):

        @pl.loop(0, SPLIT)
        def _(c):
            for k in range(KERN):
                out[c, k] = (own[c, k].astype(F32) + got[c, k].astype(F32)).astype(BF16)
            out[c, KERN] = own[c, KERN]
            out[c, KERN + 1] = got[c, KERN]


def first_sum_kernel(meta, own, m1, m3, p1, p3, *outs):
    here = jnp.where(meta[CORE] == 0, meta[XPOS], meta[YPOS])

    for shift, relayed, direct in ((0, p1, m3), (SPLIT, p3, m1)):

        @pl.loop(0, SPLIT)
        def _(c):
            at, got = c + shift, c + SPLIT
            near = relayed[c, KERN].astype(F32) + direct[got, KERN].astype(F32)
            far = own[at, KERN].astype(F32) + relayed[c, KERN + 1].astype(F32)
            for d in range(4):
                s = (here + d) % 4
                for k in range(NNZ):
                    total = own[at, k * 4 + s].astype(F32) + relayed[c, k * 4 + s].astype(F32)
                    outs[d][at, k] = (total + direct[got, k * 4 + s].astype(F32)).astype(BF16)
                outs[d][at, NNZ] = (far + near).astype(BF16)


def second_sum_kernel(meta, own, prev, nxt, far, keep, send):
    first_core = meta[CORE] == 0

    @pl.loop(0, COLS)
    def _(c):
        for k in range(NNZ + 1):
            a, b, e, f = (r[c, k].astype(F32) for r in (own, prev, nxt, far))
            total = ((a + f) + (b + e)).astype(BF16)
            low, high = total[:8], total[8:]
            if k < NNZ:
                keep[c, k] = jnp.where(first_core, low, high)
                send[c, k] = jnp.where(first_core, high, low)
            else:
                for out in (keep, send):
                    out[c, NNZ] = low
                    out[c, NNZ + 1] = high


def place_kernel(meta, keep, got, _, win, wout, kern):
    is_in = meta[CORE] == 0

    @pl.loop(0, NNZ)
    def _(k):
        mine = jnp.stack([keep[c, k].astype(F32) for c in range(COLS)], axis=0)
        its = jnp.stack([got[c, k].astype(F32) for c in range(COLS)], axis=0)
        mine, its = jnp.swapaxes(mine, 0, 1), jnp.swapaxes(its, 0, 1)
        win[:, k] = jnp.where(is_in, mine, its)
        wout[:, k] = jnp.where(is_in, its, mine)

    for c in range(COLS):
        rows = [jnp.where(is_in, got[c, NNZ + i], keep[c, NNZ + i]).astype(F32) for i in range(2)]
        kern[:, c * BS : (c + 1) * BS] = jnp.concatenate(rows, axis=0)[:9]


def on_device(tokens, cotangent, weight_in, weight_out, mix_kernel, block_rows):
    row, crop, z = lax.axis_index("rows"), lax.axis_index("crop"), lax.axis_index("hid")
    core, x, ylo = row % 2, row // 2 % NX, row // 8
    place = jnp.stack([core, x, crop * 2 + ylo, ylo, z]).astype(jnp.int32)
    meta = jnp.concatenate([block_rows.reshape(-1), place])
    is_in = core == 0

    def side(a, b):
        mine, theirs = jnp.where(is_in, a, b), jnp.where(is_in, b, a)
        got = to_partner(theirs)
        return jnp.where(is_in, mine, got), jnp.where(is_in, got, mine)

    own = jnp.stack(side(*(w.transpose(1, 2, 0, 3) for w in (weight_in, weight_out))))
    t0 = jnp.concatenate(side(tokens.reshape(128, 512), cotangent.reshape(128, 512)))

    wa = by_core(own, (0, 1), (0, -1))
    wb = by_core(own, (-1, 0), (1, 0))
    zr1, zl1 = along_z(t0, 1), along_z(t0, -1)
    wc = by_core(hold(meta, own, wa, wb, zr1, zl1), (0, -1), (0, 1))
    wd = by_core(wa, (1, 0), (-1, 0))
    zr2, zl2 = along_z(zr1, 1), along_z(zl1, -1)
    cuts = [((1, *own.shape[1:]), BF16)] * 2
    low, high = local(cut_kernel, "cut", cuts, (meta, wa, wc, wd, zr2, zl2))
    wf = by_core(low, (0, 1), (0, -1))
    wg = by_core(high, (0, -1), (0, 1))
    we = by_core(wc, (-1, 0), (1, 0))
    zr3, zl3 = along_z(zr2, 1), along_z(zl2, -1)
    wh = by_core(wf, (1, 0), (-1, 0))
    wi = by_core(wg, (-1, 0), (1, 0))
    zr4, zl4 = along_z(zr3[:128], 1), along_z(zl3[128:], -1)
    pieces = (own, wa, wb, wc, wd, we, wf, wg, wh, wi)
    token_pieces = (t0, zr1, zr2, zr3, zl1, zl2, zl3, zr4, zl4)

    pre, out, top, bot, wts, tok = forward(meta, token_pieces, pieces)
    got = to_partner(out)
    up, down = to_next_chip(bot, 1), to_next_chip(top, -1)
    g0, m1, m3, g1, g3, pgrad = backward(meta, tok, got, out, up, down, pre, mix_kernel)
    m1, m3 = first(m1, 1), first(m3, -1)

    keep, *sends = token_grad(meta, pgrad, wts)
    terms = jnp.where(is_in, keep, jnp.concatenate([to_partner(send) for send in sends]))
    relayed = [((SPLIT, KERN + 2, 16, BS), BF16)] * 2
    held = [pltpu.VMEM(g1.shape, BF16)] * 2 + [pltpu.SemaphoreType.DMA((2,))]
    g1, g3 = (pltpu.with_memory_space_constraint(g, pltpu.HBM) for g in (g1, g3))
    r1, r3 = local(relay_kernel, "relay", relayed, (meta, g1, g3, m1, m3, terms), held, hbm=(1, 2, 5))
    terms = lax.all_to_all(terms, "hid", 0, 0, tiled=True)
    outs = [((128, 512), BF16), ((8, 128), F32)]
    grad_tokens, flag = local(gather_sum_kernel, "gathersum", outs, (meta, terms))

    h = local(
        first_sum_kernel,
        "firstsum",
        [((COLS, NNZ + 1, 16, BS), BF16)] * 4,
        (meta, g0, m1, m3, first(r1, 1), first(r3, -1)),
    )
    last = (h[0], second(h[1], 1), second(h[3], -1), second(h[2], 2))
    shape = ((COLS, NNZ + 2, 8, BS), BF16)
    kept, sent = local(second_sum_kernel, "secondsum", [shape] * 2, (meta, *last))
    out_shape = ((8, NNZ, 8, BS), F32)
    win, wout, kern = local(
        place_kernel,
        "place",
        [out_shape, out_shape, ((9, 8 * BS), F32)],
        (meta, kept, to_partner(sent), flag),
    )
    grad_tokens = grad_tokens.reshape(1, 2, PW, 512)
    return grad_tokens, win.transpose(0, 2, 1, 3), wout.transpose(0, 2, 1, 3), kern


def solution(mesh):
    placed = (
        P("crop", "rows", None, "hid"),
        P("crop", "rows", None, "hid"),
        P("rows", "hid", None, None),
        P("rows", "hid", None, None),
        P(None, "hid"),
        P("hid", None),
    )
    return jax.shard_map(
        on_device,
        mesh=mesh,
        in_specs=placed,
        out_specs=(
            P("crop", "rows", None, "hid"),
            P(("crop", "rows"), "hid", None, None),
            P(("crop", "rows"), "hid", None, None),
            P(None, "hid"),
        ),
        check_vma=False,
    )
```

```python
import jax
import jax.numpy as jnp
from jax import lax
from jax.experimental import pallas as pl
from jax.experimental.pallas import tpu as pltpu
from jax.sharding import PartitionSpec as P

root_two_pi = 0.7978845608
cubic_coef = 0.044715
loss_scale = 0.03125

F32, BF16 = jnp.float32, jnp.bfloat16
NX, NY, NZ = 4, 4, 8
COLS, NNZ, BS, PW = 8, 5, 256, 64
TOK, KERN, SPLIT, PARTS = 256, 20, 4, 2
CORE, XPOS, YPOS, YLO, ZPOS = 40, 41, 42, 43, 44
HBM = pl.BlockSpec(memory_space=pltpu.MemorySpace.HBM)
VMEM = pl.BlockSpec(memory_space=pltpu.VMEM)
SMEM = pl.BlockSpec(memory_space=pltpu.SMEM)


def by_core(value, step0, step1):
    pairs = []
    for y in range(NY):
        for x in range(NX):
            for c, (dy, dx) in enumerate((step0, step1)):
                target = (y + dy) % NY * 8 + (x + dx) % NX * 2 + c
                pairs.append((y * 8 + x * 2 + c, target))
    return lax.ppermute(value, ("crop", "rows"), pairs)


def first(value, step):
    return by_core(value, (step, 0), (0, step))


def second(value, step):
    return by_core(value, (0, step), (step, 0))


def to_partner(value):
    return lax.ppermute(value, "rows", [(r, r ^ 1) for r in range(16)])


def to_next_chip(value, step):
    pairs = []
    for q in range(8):
        if 0 <= q + step < 8:
            pairs += [(q * 2 + c, (q + step) * 2 + 1 - c) for c in range(2)]
    return lax.ppermute(value, "rows", pairs)


def along_z(value, step):
    return lax.ppermute(value, "hid", [(z, (z + step) % NZ) for z in range(NZ)])


def dot(a, b, dims):
    return lax.dot_general(a, b, (dims, ((), ())), preferred_element_type=F32)


def local(kernel, name, outs, args, scratch=(), flops=2**20, hbm=(), hbm_out=()):
    shapes = [
        pltpu.HBM(s, t) if i in hbm_out else jax.ShapeDtypeStruct(s, t) for i, (s, t) in enumerate(outs)
    ]
    size = sum(a.size * a.dtype.itemsize for a in args[1:])
    return pl.pallas_call(
        kernel,
        out_shape=shapes,
        in_specs=[SMEM] + [HBM if i in hbm else VMEM for i in range(1, len(args))],
        out_specs=[HBM if i in hbm_out else VMEM for i in range(len(outs))],
        scratch_shapes=list(scratch),
        compiler_params=pltpu.CompilerParams(vmem_limit_bytes=20 * 2**20),
        cost_estimate=pl.CostEstimate(flops=flops, transcendentals=0, bytes_accessed=size),
        name=name,
    )(*args)


def lanes(c):
    return pl.ds(pl.multiple_of(c * BS, BS), BS)


def start_tokens(meta, pieces, buf, sem):
    z = meta[ZPOS]
    own, r1, r2, r3, l1, l2, l3, r4, l4 = pieces
    plan = [(own, 0, 0), (r1, 7, 0), (r2, 6, 0), (r3, 5, 0), (l1, 1, 0), (l2, 2, 0), (l3, 3, 0)]
    for src, d, at in plan + [(r4, 4, 0), (l4, 4, 128)]:
        h = (z + d) % NZ
        for part in range(2):
            rows = pl.ds(at, src.shape[0])
            target = buf.at[2 * h + part, rows]
            pltpu.make_async_copy(src.at[:, pl.ds(part * BS, BS)], target, sem).start()


def weight_plan(meta, pieces):
    core, x, ylo = meta[CORE], meta[XPOS], meta[YLO]
    own, a, b, c, d, e, f, g, h, i = pieces
    here, there = ylo * NX, (1 - ylo) * NX
    side = jnp.where(core == 0, NX - 1, 1)
    at = lambda base, step: base + (x + step) % NX
    slots = [
        (own, at(here, 0)),
        (a, at(here, side)),
        (b, at(there, 0)),
        (c, at(here, NX - side)),
        (d, at(there, side)),
        (e, at(there, NX - side)),
    ]
    plan = [(src, s, 2 * j + s) for src, j in slots for s in range(2)]
    for j, low, high in ((at(here, 2), f, g), (at(there, 2), h, i)):
        plan += [(low, 0, 2 * j), (high, 0, 2 * j + 1)]
    return plan


def hold(meta, value, *others):
    def kernel(meta, src, *refs):
        refs[-1][...] = src[...]

    outs = [(value.shape, value.dtype)]
    return local(kernel, "hold", outs, (meta, value, *others))[0]


def cut_kernel(meta, a, c, *refs):
    low, high = refs[-2:]
    low[...] = a[:1]
    high[...] = c[1:]


def forward_kernel(meta, *refs):
    tokens, pieces, outs = refs[:9], refs[9:19], refs[19:]
    pre, out, top, bot, wts, tok, sem = outs
    start_tokens(meta, tokens, tok, sem)
    plan = weight_plan(meta, pieces)
    core = meta[CORE]

    @pl.loop(0, COLS, unroll=2)
    def _(c):
        for k in range(NNZ):
            for src, row, slot in plan:
                wts[c, k, slot] = src[row, c, k]

    pltpu.make_async_copy(tok, tok, sem).wait()

    def total(c, dims):
        acc = None
        for k in range(NNZ):
            part = dot(tok[meta[c * NNZ + k]], wts[c, k].reshape(BS, BS), dims)
            acc = part if acc is None else acc + part
        return acc

    @pl.when(core == 0)
    def _():
        @pl.loop(0, COLS, unroll=2)
        def _(c):
            p = total(c, ((1,), (0,)))
            pre[:, lanes(c)] = p
            t = jnp.tanh(root_two_pi * (p + cubic_coef * p * p * p))
            out[:, lanes(c)] = (0.5 * p * (1.0 + t)).astype(BF16)

    @pl.when(core != 0)
    def _():
        @pl.loop(0, COLS, unroll=2)
        def _(c):
            out[:, lanes(c)] = total(c, ((1,), (1,))).astype(BF16)

    top[...] = out[:PW]
    bot[...] = out[TOK - PW :]


def forward(meta, tokens, pieces):
    wide = COLS * BS
    outs = [((TOK, wide), F32), ((TOK, wide), BF16), ((PW, wide), BF16), ((PW, wide), BF16)]
    outs += [((COLS, NNZ, 16, 16, BS), BF16), ((16, TOK, BS), BF16)]
    return local(
        forward_kernel,
        "forward",
        outs,
        (meta, *tokens, *pieces),
        [pltpu.SemaphoreType.DMA],
        flops=2 * TOK * BS * BS * NNZ * COLS,
        hbm=range(1, 10),
    )


def shifted_rows(mid, up, down, cols):
    cells = lax.broadcasted_iota(jnp.int32, (PW, BS), 0)
    out = []
    for row in [up[:, cols]] + [mid[i * PW : (i + 1) * PW, cols] for i in range(4)] + [down[:, cols]]:
        row = row.astype(F32)
        left = jnp.where(cells == 0, 0.0, pltpu.roll(row, 1, 0))
        right = jnp.where(cells == PW - 1, 0.0, pltpu.roll(row, PW - 1, 0))
        out.append((left, row, right))
    return out


def backward_kernel(meta, tok, got, mine, up, down, pre, taps, *refs):
    g0, m1, m3, g1, g3, pgrad, conv, lhs, res, slab, moved, stage, sems = refs
    core, x, y = meta[CORE], meta[XPOS], meta[YPOS]
    is_in = core == 0
    slab[...] = jnp.zeros_like(slab)
    here = jnp.where(is_in, y, x)
    far = jnp.where(is_in, NX, 1)
    near = jnp.where(is_in, 1, NY)

    @pl.loop(0, COLS)
    def _(c):
        cols = lanes(c)
        for i, rows in enumerate(shifted_rows(got, up, down, cols)):
            for b in range(3):
                moved[3 * i + b] = rows[b]
        tap = [jnp.where(is_in, taps[8 - j : 9 - j, cols], taps[j : j + 1, cols]) for j in range(9)]
        for i in range(4):
            acc = jnp.zeros((PW, BS), F32)
            for a in range(3):
                for b in range(3):
                    acc += tap[3 * a + b] * moved[3 * (i + a) + b]
            conv[i * PW : (i + 1) * PW] = acc

        @pl.when(is_in)
        def _():
            p = pre[:, cols]
            t = jnp.tanh(root_two_pi * (p + cubic_coef * p * p * p))
            slope = 0.5 * (1.0 + t) + 0.5 * p * (1.0 - t * t) * root_two_pi * (
                1.0 + 3.0 * cubic_coef * p * p
            )
            lhs[...] = (conv[...] * slope).astype(BF16)
            pgrad[:, cols] = lhs[...]
            for k in range(NNZ):
                part = dot(tok[meta[c * NNZ + k]], lhs[...], ((0,), (0,))) * loss_scale
                res[k] = part.astype(BF16).reshape(16, 16, BS)

        @pl.when(core != 0)
        def _():
            lhs[...] = conv[...].astype(BF16)
            for k in range(NNZ):
                part = dot(lhs[...], tok[meta[c * NNZ + k]], ((0,), (0,))) * loss_scale
                res[k] = part.astype(BF16).reshape(16, 16, BS)
            sums = []
            for a in range(3):
                for b in range(3):
                    acc = jnp.zeros((PW, BS), F32)
                    for i in range(4):
                        acc += moved[3 * (i + a) + b] * mine[i * PW : (i + 1) * PW, cols].astype(F32)
                    sums.append(jnp.sum(acc, axis=0, keepdims=True))
            rows = jnp.concatenate(sums + [jnp.zeros((7, BS), F32)], axis=0) * loss_scale
            slab[...] = rows.astype(BF16)

        def emit(out, d, at):
            start = (here + d) % 4 * far
            for k in range(NNZ):
                for s in range(4):
                    stage[d, c, k * 4 + s] = res[k, start + s * near]
            stage[d, c, KERN] = slab[...]
            pltpu.make_async_copy(stage.at[d, c], out.at[at], sems.at[d]).start()

        emit(g0, 0, c)

        @pl.when(c < SPLIT)
        def _():
            emit(m1, 2, c)
            emit(g1, 1, c)
            emit(m3, 3, c + SPLIT)

        @pl.when(c >= SPLIT)
        def _():
            emit(m3, 2, c - SPLIT)
            emit(m1, 1, c)
            emit(g3, 3, c - SPLIT)

    for d in range(4):
        pltpu.make_async_copy(stage.at[d], g0, sems.at[d]).wait()


def backward(meta, tok, got, mine, up, down, pre, taps):
    full, part = (COLS, KERN + 1, 16, BS), (SPLIT, KERN + 1, 16, BS)
    outs = [(full, BF16)] * 3 + [(part, BF16)] * 2 + [((TOK, COLS * BS), BF16)]
    scratch = [
        pltpu.VMEM((TOK, BS), F32),
        pltpu.VMEM((TOK, BS), BF16),
        pltpu.VMEM((NNZ, 16, 16, BS), BF16),
        pltpu.VMEM((16, BS), BF16),
        pltpu.VMEM((18, PW, BS), F32),
        pltpu.VMEM((4, COLS, KERN + 1, 16, BS), BF16),
        pltpu.SemaphoreType.DMA((4,)),
    ]
    args = (meta, tok, got, mine, up, down, pre, taps)
    return local(
        backward_kernel,
        "backward",
        outs,
        args,
        scratch,
        flops=2 * TOK * BS * BS * NNZ * COLS,
        hbm_out=range(5),
    )


def token_grad_kernel(meta, pgrad, wts, keep, *refs):
    *sends, acc = refs

    @pl.when(meta[CORE] == 0)
    def _():
        acc[...] = jnp.zeros_like(acc)

        @pl.loop(0, COLS, unroll=2)
        def _(c):
            for k in range(NNZ):
                wt = wts[c, k].reshape(BS, BS)
                acc[meta[c * NNZ + k]] += dot(pgrad[:, lanes(c)], wt, ((1,), (1,)))

        size = 16 // len(sends)
        for i, send in enumerate(sends):

            @pl.loop(0, size)
            def _(r):
                keep[r + i * size] = acc[r + i * size, :128].astype(BF16)
                send[r] = acc[r + i * size, 128:].astype(BF16)


def token_grad(meta, pgrad, wts):
    return local(
        token_grad_kernel,
        "tokengrad",
        [((16, 128, BS), BF16)] + [((16 // PARTS, 128, BS), BF16)] * PARTS,
        (meta, pgrad, wts),
        [pltpu.VMEM((16, TOK, BS), F32)],
        flops=2 * TOK * BS * BS * NNZ * COLS,
    )


def gather_sum_kernel(meta, parts, out, flag):
    flag[...] = jnp.zeros_like(flag)
    for b in range(2):
        total = parts[b].astype(F32)
        for z in range(1, NZ):
            total += parts[2 * z + b].astype(F32)
        out[:, b * BS : (b + 1) * BS] = total.astype(BF16)


def relay_kernel(meta, s1, s3, m1, m3, _, o1, o3, g1, g3, sems):
    copies = [pltpu.make_async_copy(a, b, sems.at[i]) for i, (a, b) in enumerate(((s1, g1), (s3, g3)))]
    for copy in copies:
        copy.start()
    for copy in copies:
        copy.wait()
    for out, own, got in ((o1, g1, m1), (o3, g3, m3)):

        @pl.loop(0, SPLIT)
        def _(c):
            for k in range(KERN):
                out[c, k] = (own[c, k].astype(F32) + got[c, k].astype(F32)).astype(BF16)
            out[c, KERN] = own[c, KERN]
            out[c, KERN + 1] = got[c, KERN]


def first_sum_kernel(meta, own, m1, m3, p1, p3, *outs):
    here = jnp.where(meta[CORE] == 0, meta[XPOS], meta[YPOS])

    for shift, relayed, direct in ((0, p1, m3), (SPLIT, p3, m1)):

        @pl.loop(0, SPLIT)
        def _(c):
            at, got = c + shift, c + SPLIT
            near = relayed[c, KERN].astype(F32) + direct[got, KERN].astype(F32)
            far = own[at, KERN].astype(F32) + relayed[c, KERN + 1].astype(F32)
            for d in range(4):
                s = (here + d) % 4
                for k in range(NNZ):
                    total = own[at, k * 4 + s].astype(F32) + relayed[c, k * 4 + s].astype(F32)
                    outs[d][at, k] = (total + direct[got, k * 4 + s].astype(F32)).astype(BF16)
                outs[d][at, NNZ] = (far + near).astype(BF16)


def second_sum_kernel(meta, own, prev, nxt, far, keep, send):
    first_core = meta[CORE] == 0

    @pl.loop(0, COLS)
    def _(c):
        for k in range(NNZ + 1):
            a, b, e, f = (r[c, k].astype(F32) for r in (own, prev, nxt, far))
            total = ((a + f) + (b + e)).astype(BF16)
            low, high = total[:8], total[8:]
            if k < NNZ:
                keep[c, k] = jnp.where(first_core, low, high)
                send[c, k] = jnp.where(first_core, high, low)
            else:
                for out in (keep, send):
                    out[c, NNZ] = low
                    out[c, NNZ + 1] = high


def place_kernel(meta, keep, got, _, win, wout, kern):
    is_in = meta[CORE] == 0

    @pl.loop(0, NNZ)
    def _(k):
        mine = jnp.stack([keep[c, k].astype(F32) for c in range(COLS)], axis=0)
        its = jnp.stack([got[c, k].astype(F32) for c in range(COLS)], axis=0)
        mine, its = jnp.swapaxes(mine, 0, 1), jnp.swapaxes(its, 0, 1)
        win[:, k] = jnp.where(is_in, mine, its)
        wout[:, k] = jnp.where(is_in, its, mine)

    for c in range(COLS):
        rows = [jnp.where(is_in, got[c, NNZ + i], keep[c, NNZ + i]).astype(F32) for i in range(2)]
        kern[:, c * BS : (c + 1) * BS] = jnp.concatenate(rows, axis=0)[:9]


def on_device(tokens, cotangent, weight_in, weight_out, mix_kernel, block_rows):
    row, crop, z = lax.axis_index("rows"), lax.axis_index("crop"), lax.axis_index("hid")
    core, x, ylo = row % 2, row // 2 % NX, row // 8
    place = jnp.stack([core, x, crop * 2 + ylo, ylo, z]).astype(jnp.int32)
    meta = jnp.concatenate([block_rows.reshape(-1), place])
    is_in = core == 0

    def side(a, b):
        mine, theirs = jnp.where(is_in, a, b), jnp.where(is_in, b, a)
        got = to_partner(theirs)
        return jnp.where(is_in, mine, got), jnp.where(is_in, got, mine)

    own = jnp.stack(side(*(w.transpose(1, 2, 0, 3) for w in (weight_in, weight_out))))
    t0 = jnp.concatenate(side(tokens.reshape(128, 512), cotangent.reshape(128, 512)))

    wa = by_core(own, (0, 1), (0, -1))
    wb = by_core(own, (-1, 0), (1, 0))
    zr1, zl1 = along_z(t0, 1), along_z(t0, -1)
    wc = by_core(hold(meta, own, wa, wb, zr1, zl1), (0, -1), (0, 1))
    wd = by_core(wa, (1, 0), (-1, 0))
    zr2, zl2 = along_z(zr1, 1), along_z(zl1, -1)
    cuts = [((1, *own.shape[1:]), BF16)] * 2
    low, high = local(cut_kernel, "cut", cuts, (meta, wa, wc, wd, zr2, zl2))
    wf = by_core(low, (0, 1), (0, -1))
    wg = by_core(high, (0, -1), (0, 1))
    we = by_core(wc, (-1, 0), (1, 0))
    zr3, zl3 = along_z(zr2, 1), along_z(zl2, -1)
    wh = by_core(wf, (1, 0), (-1, 0))
    wi = by_core(wg, (-1, 0), (1, 0))
    zr4, zl4 = along_z(zr3[:128], 1), along_z(zl3[128:], -1)
    pieces = (own, wa, wb, wc, wd, we, wf, wg, wh, wi)
    token_pieces = (t0, zr1, zr2, zr3, zl1, zl2, zl3, zr4, zl4)

    pre, out, top, bot, wts, tok = forward(meta, token_pieces, pieces)
    got = to_partner(out)
    up, down = to_next_chip(bot, 1), to_next_chip(top, -1)
    g0, m1, m3, g1, g3, pgrad = backward(meta, tok, got, out, up, down, pre, mix_kernel)
    m1, m3 = first(m1, 1), first(m3, -1)

    keep, *sends = token_grad(meta, pgrad, wts)
    terms = jnp.where(is_in, keep, jnp.concatenate([to_partner(send) for send in sends]))
    relayed = [((SPLIT, KERN + 2, 16, BS), BF16)] * 2
    held = [pltpu.VMEM(g1.shape, BF16)] * 2 + [pltpu.SemaphoreType.DMA((2,))]
    g1, g3 = (pltpu.with_memory_space_constraint(g, pltpu.HBM) for g in (g1, g3))
    r1, r3 = local(relay_kernel, "relay", relayed, (meta, g1, g3, m1, m3, terms), held, hbm=(1, 2, 5))
    terms = lax.all_to_all(terms, "hid", 0, 0, tiled=True)
    outs = [((128, 512), BF16), ((8, 128), F32)]
    grad_tokens, flag = local(gather_sum_kernel, "gathersum", outs, (meta, terms))

    h = local(
        first_sum_kernel,
        "firstsum",
        [((COLS, NNZ + 1, 16, BS), BF16)] * 4,
        (meta, g0, m1, m3, first(r1, 1), first(r3, -1)),
    )
    last = (h[0], second(h[1], 1), second(h[3], -1), second(h[2], 2))
    shape = ((COLS, NNZ + 2, 8, BS), BF16)
    kept, sent = local(second_sum_kernel, "secondsum", [shape] * 2, (meta, *last))
    out_shape = ((8, NNZ, 8, BS), F32)
    win, wout, kern = local(
        place_kernel,
        "place",
        [out_shape, out_shape, ((9, 8 * BS), F32)],
        (meta, kept, to_partner(sent), flag),
    )
    grad_tokens = grad_tokens.reshape(1, 2, PW, 512)
    return grad_tokens, win.transpose(0, 2, 1, 3), wout.transpose(0, 2, 1, 3), kern


def solution(mesh):
    placed = (
        P("crop", "rows", None, "hid"),
        P("crop", "rows", None, "hid"),
        P("rows", "hid", None, None),
        P("rows", "hid", None, None),
        P(None, "hid"),
        P("hid", None),
    )
    return jax.shard_map(
        on_device,
        mesh=mesh,
        in_specs=placed,
        out_specs=(
            P("crop", "rows", None, "hid"),
            P(("crop", "rows"), "hid", None, None),
            P(("crop", "rows"), "hid", None, None),
            P(None, "hid"),
        ),
        check_vma=False,
    )
```
